32 devices in a mesh: dp: 4 (over z), fsdp: 8 (over y, x, core).
Axes of the slice: x: 2, y: 2, z: 4, core: 2. Of those that a mesh axis runs over, the one named last changes fastest.
Arguments:
- block_input: bfloat16 [2, 32, 576, 768], P(None, ('dp', 'fsdp')), may hold values from -6 to 6
- valid_counts: int32 [2, 32], P(None, ('dp', 'fsdp')), may hold values from 288 to 576
- output_cotangent: bfloat16 [2, 32, 576, 768], P(None, ('dp', 'fsdp')), may hold values from -6 to 6
- triple_weight: float32 [768, 2304], P(('dp', 'fsdp')), may hold values from -0.21875 to 0.21875
- merge_weight: float32 [768, 768], P(('dp', 'fsdp')), may hold values from -0.875 to 0.875
- expand_weight: float32 [768, 3072], P(('dp', 'fsdp')), may hold values from -0.21875 to 0.21875
- reduce_weight: float32 [3072, 768], P(('dp', 'fsdp')), may hold values from -0.109375 to 0.109375
- first_gain: float32 [768], P(('dp', 'fsdp')), may hold values from 0.25 to 1.75
- first_shift: float32 [768], P(('dp', 'fsdp')), may hold values from -3 to 3
- query_bias: float32 [768], P(('dp', 'fsdp')), may hold values from -3 to 3
- value_bias: float32 [768], P(('dp', 'fsdp')), may hold values from -3 to 3
- merge_bias: float32 [768], P(('dp', 'fsdp')), may hold values from -3 to 3
- second_gain: float32 [768], P(('dp', 'fsdp')), may hold values from 0.25 to 1.75
- second_shift: float32 [768], P(('dp', 'fsdp')), may hold values from -3 to 3
- expand_bias: float32 [3072], P(('dp', 'fsdp')), may hold values from -3 to 3
- reduce_bias: float32 [768], P(('dp', 'fsdp')), may hold values from -3 to 3
- position_table: float32 [529, 24], replicated, may hold values from -4 to 4
Outputs:
- block_output: bfloat16 [2, 32, 576, 768], P(None, ('dp', 'fsdp'))
- input_grad: bfloat16 [2, 32, 576, 768], P(None, ('dp', 'fsdp'))
- triple_grad: float32 [768, 2304], P(('dp', 'fsdp'))
- merge_grad: float32 [768, 768], P(('dp', 'fsdp'))
- expand_grad: float32 [768, 3072], P(('dp', 'fsdp'))
- reduce_grad: float32 [3072, 768], P(('dp', 'fsdp'))
- first_gain_grad: float32 [768], P(('dp', 'fsdp'))
- first_shift_grad: float32 [768], P(('dp', 'fsdp'))
- query_bias_grad: float32 [768], P(('dp', 'fsdp'))
- value_bias_grad: float32 [768], P(('dp', 'fsdp'))
- merge_bias_grad: float32 [768], P(('dp', 'fsdp'))
- second_gain_grad: float32 [768], P(('dp', 'fsdp'))
- second_shift_grad: float32 [768], P(('dp', 'fsdp'))
- expand_bias_grad: float32 [3072], P(('dp', 'fsdp'))
- reduce_bias_grad: float32 [768], P(('dp', 'fsdp'))
- position_table_grad: float32 [529, 24], replicated
The draws below stay inside these ranges and needn't reach their ends.
Inputs may be any that keep to these rules, and one draw needn't show every extreme that they name: `valid_counts`: tokens at raster positions from the count on are padding: they are no keys, and their attention output is zero.
All inputs are finite; a program needn't handle non-finite values.
Results may differ from the reference program's by a relative error of at most 0.012.
The reference program's roundings to bfloat16 on the way count: a program that leaves them out, or rounds other values in their place, can miss the bound.
Values may be sent and summed in bfloat16 or wider, within the bound.
A program may use at most 192 MiB of HBM per device.

```python
import jax
import jax.numpy as jnp
from jax import lax

D = 768
FF = 3072
HEADS = 24
HEAD_DIM = 32
WIN = 12
SIDE = 24
MB = 2
L = 576
SHIFT = 6
TABLE = 529
BATCH = 32


def set_ends(result, rng, low, high):
    dims = result.shape
    place = [jax.random.randint(jax.random.fold_in(rng, axis), (), 0, dims[axis]) for axis in range(len(dims))]
    result = result.at[tuple(place)].set(low)
    longest = dims.index(max(dims))
    place[longest] = (place[longest] + 1) % dims[longest]
    return result.at[tuple(place)].set(high)


def with_spikes(array, own_key, source, target, parts, factor):
    owner, partner = [(jnp.arange(array.shape[position]) // (array.shape[position] // parts)).reshape([-1 if axis == position else 1 for axis in range(array.ndim)]) for position in (source, target)]
    chosen = jax.random.permutation(own_key, parts)[partner]
    strong = (owner == chosen) | (owner == (partner + parts // 2) % parts)
    return jnp.where(strong, factor * array, array)


def levels(own_key, shape, cuts, low, largest):
    gain = 1.0
    for position, parts in cuts:
        draws = jax.random.uniform(jax.random.fold_in(jax.random.fold_in(own_key, 6), position), (parts,), jnp.float32, low / len(cuts), largest / len(cuts))
        gain = gain * jnp.repeat(jnp.exp(draws), shape[position] // parts).reshape((-1,) + (1,) * (len(shape) - 1 - position))
    return gain


def scatter_about(key, shape, scale, reach, pieces=(), kind=jnp.bfloat16):
    drawn = jax.random.normal(key, shape, jnp.float32) * scale
    if len(pieces) > 0:
        drawn = levels(key, shape, pieces, -0.22, 0.18) * drawn
    return jnp.clip(drawn, min=-reach, max=reach).astype(kind)


def gaussian_with(own_key, shape, deviation, limit, cuts, heavy, dtype=jnp.bfloat16):
    values = deviation * jax.random.normal(own_key, shape, jnp.float32)
    if cuts:
        values = values * levels(own_key, shape, cuts, -0.22, 0.18)
    return jnp.clip(with_spikes(values, jax.random.fold_in(own_key, 3), *heavy), -limit, limit).astype(dtype)


def setup_inputs(seed: int = 0) -> dict:
    keys = jax.random.split(jax.random.key(seed), 18)
    block_input = gaussian_with(keys[0], (MB, BATCH, L, D), 1.0, 6.0, ((1, 32),), (1, 3, 32, 2.75))
    valid_counts = set_ends(jax.random.randint(keys[1], (MB, BATCH), L // 2, L + 1), jax.random.fold_in(keys[1], 1), L // 2, L).astype(jnp.int32)
    output_cotangent = scatter_about(keys[2], (MB, BATCH, L, D), 1.0, 6.0, ((1, 32),))
    triple_weight = scatter_about(keys[3], (D, 3 * D), D ** -0.5, 0.21875, ((0, 32),), jnp.float32)
    merge_weight = scatter_about(keys[4], (D, D), (D // 16) ** -0.5, 0.875, ((0, 32),), jnp.float32)
    expand_weight = scatter_about(keys[5], (D, FF), D ** -0.5, 0.21875, ((0, 32),), jnp.float32)
    reduce_weight = scatter_about(keys[6], (FF, D), FF ** -0.5, 0.109375, ((0, 32),), jnp.float32)
    first_gain = jnp.clip(1.0 + 0.15 * jax.random.normal(keys[7], (D,), jnp.float32), 0.25, 1.75)
    first_shift = scatter_about(keys[8], (D,), 0.3, 3.0, ((0, 32),), jnp.float32)
    query_bias = scatter_about(keys[9], (D,), 0.3, 3.0, ((0, 32),), jnp.float32)
    value_bias = scatter_about(keys[10], (D,), 0.3, 3.0, ((0, 32),), jnp.float32)
    merge_bias = scatter_about(keys[11], (D,), 0.3, 3.0, ((0, 32),), jnp.float32)
    second_gain = jnp.clip(1.0 + 0.15 * jax.random.normal(keys[12], (D,), jnp.float32), 0.25, 1.75)
    second_shift = scatter_about(keys[13], (D,), 0.3, 3.0, ((0, 32),), jnp.float32)
    expand_bias = scatter_about(keys[14], (FF,), 0.3, 3.0, ((0, 32),), jnp.float32)
    reduce_bias = scatter_about(keys[15], (D,), 0.3, 3.0, ((0, 32),), jnp.float32)
    position_table = scatter_about(keys[16], (TABLE, HEADS), 1.0, 4.0, (), jnp.float32)
    return dict(block_input=block_input, valid_counts=valid_counts, output_cotangent=output_cotangent, triple_weight=triple_weight, merge_weight=merge_weight, expand_weight=expand_weight, reduce_weight=reduce_weight, first_gain=first_gain, first_shift=first_shift, query_bias=query_bias, value_bias=value_bias, merge_bias=merge_bias, second_gain=second_gain, second_shift=second_shift, expand_bias=expand_bias, reduce_bias=reduce_bias, position_table=position_table)


PRECISE = lax.Precision.HIGHEST
MASKED_SCORE = -1000000000.0
NORM_EPSILON = 1e-05

@jax.custom_vjp
def low(v):
    return lax.optimization_barrier(v.astype(jnp.bfloat16)).astype(jnp.float32)

@jax.custom_vjp
def low_back(v):
    return v

def low_keep(v):
    return (low(v), None)

def low_pass(kept, grad):
    return (grad,)

def back_keep(v):
    return (v, None)

def back_low(kept, grad):
    return (low(grad),)
low.defvjp(low_keep, low_pass)
low_back.defvjp(back_keep, back_low)

def partition(token_grid):
    across = SIDE // WIN
    channels = token_grid.shape[-1]
    shaped = token_grid.reshape(across, WIN, across, WIN, channels).transpose(0, 2, 1, 3, 4)
    return shaped.reshape(across * across, WIN * WIN, channels)

def window_order(tokens):
    token_grid = tokens.reshape(SIDE, SIDE, tokens.shape[-1])
    return partition(jnp.roll(token_grid, (-SHIFT, -SHIFT), (0, 1)))

def grid_order(windows):
    across = SIDE // WIN
    channels = windows.shape[-1]
    token_grid = windows.reshape(across, across, WIN, WIN, channels).transpose(0, 2, 1, 3, 4)
    token_grid = token_grid.reshape(SIDE, SIDE, channels)
    return jnp.roll(token_grid, (SHIFT, SHIFT), (0, 1)).reshape(SIDE * SIDE, channels)

def offset_onehot():
    query_pos = jnp.arange(WIN)[:, None, None]
    key_pos = jnp.arange(WIN)[None, :, None]
    target_pos = jnp.arange(2 * WIN - 1)[None, None, :]
    return (query_pos - key_pos + WIN - 1 == target_pos).astype(jnp.float32)

def relative_bias(position_table):
    onehot = offset_onehot()
    extent = 2 * WIN - 1
    table_cube = position_table.reshape(extent, extent, HEADS)
    partial_sum = jnp.einsum('cds,rsh->cdrh', onehot, table_cube, precision=PRECISE)
    bias_full = jnp.einsum('abr,cdrh->hacbd', onehot, partial_sum, precision=PRECISE)
    return bias_full.reshape(HEADS, WIN * WIN, WIN * WIN)

def region_labels():
    coords = jnp.arange(SIDE)
    region = (coords >= SIDE - WIN).astype(jnp.int32) + (coords >= SIDE - SHIFT).astype(jnp.int32)
    labels = region[:, None] * 3 + region[None, :]
    return partition(labels[:, :, None])[:, :, 0]

def layer_norm(values, gain_row, shift_row):
    center = values - lax.optimization_barrier(jnp.mean(values, axis=-1, keepdims=True))
    spread = lax.optimization_barrier(jnp.mean(center * center, axis=-1, keepdims=True))
    return center * lax.rsqrt(spread + NORM_EPSILON) * gain_row + shift_row

def image_block(weights, pos_bias, labels, image_rows, valid_count):
    triple_w, merge_w, expand_w, reduce_w, gains, expand_b = weights
    normed = low(layer_norm(image_rows, gains[0], gains[1]))
    triple_bias = jnp.concatenate([gains[2], jnp.zeros_like(gains[2]), gains[3]])
    triple = low_back(low(jnp.dot(normed, triple_w, precision=PRECISE) + triple_bias))
    windows = window_order(triple)
    across = windows.shape[0]
    queries = windows[:, :, :D].reshape(across, WIN * WIN, HEADS, HEAD_DIM)
    keys_win = windows[:, :, D:2 * D].reshape(across, WIN * WIN, HEADS, HEAD_DIM)
    values_win = windows[:, :, 2 * D:].reshape(across, WIN * WIN, HEADS, HEAD_DIM)
    valid_mask = (jnp.arange(SIDE * SIDE) < valid_count).astype(jnp.float32)
    valid_win = window_order(valid_mask[:, None])[:, :, 0]
    allowed = (labels[:, :, None] == labels[:, None, :]) & (valid_win[:, None, :] > 0.5)
    raw_scores = jnp.einsum('wqhd,wkhd->whqk', queries, keys_win, precision=PRECISE)
    scores = low_back(raw_scores) * float(HEAD_DIM) ** (-0.5) + pos_bias[None]
    scores = jnp.where(allowed[:, None], scores, MASKED_SCORE)
    attention = low(jax.nn.softmax(scores, axis=-1))
    attended = jnp.einsum('whqk,wkhd->wqhd', attention, values_win, precision=PRECISE)
    attended = attended.reshape(across, WIN * WIN, D) * valid_win[:, :, None]
    attended = low_back(low(grid_order(attended)))
    mixed_rows = image_rows + low_back(jnp.dot(attended, merge_w, precision=PRECISE)) + gains[4]
    normed_two = low(layer_norm(mixed_rows, gains[5], gains[6]))
    hidden = low_back(jnp.dot(normed_two, expand_w, precision=PRECISE)) + expand_b
    active = low(jax.nn.gelu(hidden, approximate=False))
    return mixed_rows + low_back(jnp.dot(active, reduce_w, precision=PRECISE)) + gains[7]

def reference(block_input, valid_counts, output_cotangent, triple_weight, merge_weight, expand_weight, reduce_weight, first_gain, first_shift, query_bias, value_bias, merge_bias, second_gain, second_shift, expand_bias, reduce_bias, position_table):
    inputs = block_input.astype(jnp.float32).reshape(MB * BATCH, SIDE * SIDE, D)
    counts_flat = valid_counts.reshape(MB * BATCH).astype(jnp.int32)
    small_master = jnp.stack([first_gain, first_shift, query_bias, value_bias, merge_bias, second_gain, second_shift, reduce_bias])
    masters = (triple_weight, merge_weight, expand_weight, reduce_weight, small_master, expand_bias, position_table)
    labels = region_labels()

    def forward(master_set, input_rows):
        weights = tuple((low(master) for master in master_set[:6]))
        pos_bias = relative_bias(master_set[6])

        def per_image(image_entry):
            return image_block(weights, pos_bias, labels, image_entry[0], image_entry[1])
        return lax.map(jax.checkpoint(per_image), (input_rows, counts_flat))
    outputs, pullback = jax.vjp(forward, masters, inputs)
    cotangent = output_cotangent.astype(jnp.float32).reshape(MB * BATCH, SIDE * SIDE, D)
    gradients, input_gradient = pullback(cotangent)
    triple_g, merge_g, expand_g, reduce_g, small_g, expand_bias_g, table_g = gradients
    return (outputs.reshape(MB, BATCH, SIDE * SIDE, D).astype(jnp.bfloat16), input_gradient.reshape(MB, BATCH, SIDE * SIDE, D).astype(jnp.bfloat16), triple_g, merge_g, expand_g, reduce_g, small_g[0], small_g[1], small_g[2], small_g[3], small_g[4], small_g[5], small_g[6], expand_bias_g, small_g[7], table_g)
```

```python
import math
import functools

import numpy as np
import jax
import jax.numpy as jnp
from jax import lax
from jax.experimental import pallas as pl
from jax.experimental.pallas import tpu as pltpu
from jax.sharding import PartitionSpec as P

D = 768
FF = 3072
HEADS = 24
HEAD_DIM = 32
WIN = 12
SIDE = 24
SHIFT = 6
TOK = SIDE * SIDE
WT = WIN * WIN
GROUPS = 3
GH = HEADS // GROUPS
GW = GH * HEAD_DIM
QL = GH * WT
SCALE = HEAD_DIM ** -0.5
MASKED = -1e30
EPS = 1e-5
F32 = jnp.float32
BF16 = jnp.bfloat16
VMEM_LIMIT = 62 << 20

NN = (((1,), (0,)), ((), ()))
NT = (((1,), (1,)), ((), ()))
TN = (((0,), (0,)), ((), ()))


def dot(a, b, dims=NN):
    return lax.dot_general(a, b, dims, preferred_element_type=F32)


def layout_constants():
    j = np.arange(WT)
    raster = np.zeros((4, WT), np.int32)
    label = np.zeros((4, WT), np.int32)
    for w in range(4):
        rr = (w // 2) * WIN + j // WIN
        rc = (w % 2) * WIN + j % WIN
        raster[w] = ((rr + SHIFT) % SIDE) * SIDE + (rc + SHIFT) % SIDE
        reg = lambda c: (c >= SIDE - WIN).astype(np.int32) + (c >= SIDE - SHIFT).astype(np.int32)
        label[w] = reg(rr) * 3 + reg(rc)
    perm = np.zeros((TOK, TOK), np.float32)
    perm[np.arange(TOK), raster.reshape(-1)] = 1.0
    raster_l = np.broadcast_to(raster[:, :, None], (4, WT, 128)).astype(np.int32)
    label_l = np.broadcast_to(label[:, :, None], (4, WT, 128)).astype(np.int32)
    label_q = np.broadcast_to(np.tile(label, (1, GH))[:, None, :], (4, 8, QL)).astype(np.int32)
    ext = 2 * WIN - 1
    target = np.full((4, WT), -1, np.int32)
    for p in range(4):
        r = j // WIN + (WIN - 1 if p // 2 == 0 else -1)
        s = j % WIN + (WIN - 1 if p % 2 == 0 else -1)
        ok = (r >= 0) & (s >= 0)
        target[p] = np.where(ok, r * ext + s, -1)
    target = np.broadcast_to(target.reshape(1, 4 * WT), (8, 4 * WT)).astype(np.int32)
    return perm, raster_l, label_l, label_q, target


PERM, RASTER_L, LABEL_L, LABEL_Q, TARGET = layout_constants()


def lane_iota(shape):
    return lax.broadcasted_iota(jnp.int32, shape, len(shape) - 1)


def stats(x):
    mean = jnp.mean(x, axis=-1, keepdims=True)
    center = x - mean
    var = jnp.mean(center * center, axis=-1, keepdims=True)
    inv = lax.rsqrt(var + EPS)
    return center * inv, inv


def head_stack(dst, x):
    lane = lane_iota(x.shape) // HEAD_DIM
    zero = jnp.zeros_like(x)
    for h in range(GH):
        dst[h * WT:(h + 1) * WT, :] = jnp.where(lane == h, x, zero)


def head_pick(o):
    lane = lane_iota((WT, GW)) // HEAD_DIM
    out = jnp.where(lane == 0, o[0:WT], 0.0)
    for h in range(1, GH):
        out = jnp.where(lane == h, o[h * WT:(h + 1) * WT], out)
    return out


def onehot(target_ref):
    ext = (2 * WIN - 1) ** 2
    t = lax.broadcasted_iota(jnp.int32, (ext, 4 * WT), 0)
    return (t == target_ref[0:1, :]).astype(F32)


def spread_bias(table_ref, target_ref, t4, bias, rowbuf):
    t4[...] = lax.dot_general(table_ref[...], onehot(target_ref), TN,
                              precision=lax.Precision.HIGHEST, preferred_element_type=F32) * (1.0 / SCALE)
    lane = lane_iota((1, QL))
    a_of = (lane % WT) // WIN
    lane16 = lane_iota((16, QL))
    c_of = lane16 % WIN
    for g in range(GROUPS):
        rows = []
        for p in range(4):
            acc = jnp.zeros((1, QL), F32)
            for h in range(GH):
                piece = t4[g * GH + h:g * GH + h + 1, p * WT:(p + 1) * WT]
                piece = jnp.concatenate([piece, jnp.zeros((1, QL - WT), F32)], axis=1)
                acc = acc + (pltpu.roll(piece, h * WT, axis=1) if h else piece)
            rows.append(acc)
        for s in range(2):
            for b in range(WIN):
                pos = pltpu.roll(rows[s], WIN * b, axis=1) if b else rows[s]
                neg = pltpu.roll(rows[2 + s], (WIN * b - WT) % QL, axis=1)
                rowbuf[s, b:b + 1, :] = jnp.where(a_of >= b, pos, neg)
        for d in range(WIN):
            pos = pltpu.roll(rowbuf[0], d, axis=1) if d else rowbuf[0]
            neg = pltpu.roll(rowbuf[1], (d - WIN) % QL, axis=1)
            both = jnp.where(c_of >= d, pos, neg)
            for n in range(9):
                bias[g * 9 + n, pl.ds(d, WIN, stride=WIN), :] = both[0:WIN, n * 128:(n + 1) * 128]


def fwd_kernel(counts, x, perm, raster, labk, labq, target, table, tm, sv,
               xp, normed, triple, pt, attended, mixed, n2,
               t4, bias, rowbuf, qs, st, lk):
    spread_bias(table, target, t4, bias, rowbuf)

    def ln1(i, _):
        b, w = i // 4, i % 4
        rows = pl.ds(pl.multiple_of(i * WT, WT), WT)
        pr = perm[pl.ds(pl.multiple_of(w * WT, WT), WT), :]
        xx = dot(pr, x[b])
        xp[rows, :] = xx.astype(BF16)
        hat, _i = stats(xx)
        normed[rows, :] = (hat * sv[0:1, :] + sv[1:2, :]).astype(BF16)
        return 0

    lax.fori_loop(0, 8, ln1, 0)

    for n in range(9):
        cols = pl.ds(n * 256, 256)
        r = dot(normed[...], tm[:, cols])
        if n < 3:
            r = r + sv[2:3, cols]
        if n >= 6:
            r = r + sv[3:4, pl.ds((n - 6) * 256, 256)]
        triple[:, cols] = r.astype(BF16)

    def attn(t, _):
        i, g = t // GROUPS, t % GROUPS
        b, w = i // 4, i % 4
        rows = pl.ds(pl.multiple_of(i * WT, WT), WT)
        col = lambda k: pl.ds(pl.multiple_of(k * D + g * GW, GW), GW)
        valid = raster[w] < counts[b]
        lk[...] = jnp.where(valid, labk[w], -1)
        head_stack(qs, triple[rows, col(0)])
        st[...] = dot(triple[rows, col(1)], qs[...], NT)
        for n in range(9):
            c = pl.ds(n * 128, 128)
            s = st[:, c] + bias[g * 9 + n]
            s = jnp.where(lk[...] == labq[w, 0:1, c], s, MASKED)
            m = jnp.max(s, axis=0, keepdims=True)
            e = jnp.exp((s - m) * SCALE)
            tot = jnp.sum(e, axis=0, keepdims=True)
            pt[t, :, c] = (e * (1.0 / tot)).astype(BF16)
        o = dot(pt[t], triple[rows, col(2)], TN)
        out = head_pick(o)
        vq = jnp.concatenate([valid, valid], axis=1)
        attended[rows, pl.ds(pl.multiple_of(g * GW, GW), GW)] = jnp.where(vq, out, 0.0).astype(BF16)
        return 0

    lax.fori_loop(0, 8 * GROUPS, attn, 0)

    for n in range(3):
        cols = pl.ds(n * 256, 256)
        r = dot(attended[...], tm[:, pl.ds(2304 + n * 256, 256)])
        mixed[:, cols] = xp[:, cols].astype(F32) + r + sv[4:5, cols]

    def ln2(i, _):
        rows = pl.ds(pl.multiple_of(i * WT, WT), WT)
        hat, _i = stats(mixed[rows, :])
        n2[rows, :] = (hat * sv[5:6, :] + sv[6:7, :]).astype(BF16)
        return 0

    lax.fori_loop(0, 8, ln2, 0)


def call(kernel, outs, scratch, ins, smem=0, name=None):
    specs = [pl.BlockSpec(memory_space=pltpu.SMEM)] * smem + [pl.BlockSpec(memory_space=pltpu.VMEM)] * (len(ins) - smem)
    return pl.pallas_call(
        kernel,
        out_shape=[jax.ShapeDtypeStruct(s, d) for s, d in outs],
        in_specs=specs,
        out_specs=[pl.BlockSpec(memory_space=pltpu.VMEM)] * len(outs),
        scratch_shapes=scratch,
        name=name,
        compiler_params=pltpu.CompilerParams(vmem_limit_bytes=VMEM_LIMIT),
    )(*ins)


def forward(counts, x, table, tm, sv):
    rows = 2 * TOK
    return call(
        fwd_kernel,
        [((rows, D), BF16), ((rows, D), BF16), ((rows, 3 * D), BF16), ((8 * GROUPS, WT, QL), BF16),
         ((rows, D), BF16), ((rows, D), F32), ((rows, D), BF16)],
        [pltpu.VMEM((HEADS, 4 * WT), F32), pltpu.VMEM((GROUPS * 9, WT, 128), F32), pltpu.VMEM((2, 16, QL), F32),
         pltpu.VMEM((QL, GW), BF16), pltpu.VMEM((WT, QL), F32), pltpu.VMEM((WT, 128), jnp.int32)],
        [counts, x, jnp.asarray(PERM, BF16), jnp.asarray(RASTER_L), jnp.asarray(LABEL_L), jnp.asarray(LABEL_Q),
         jnp.asarray(TARGET), table, tm, sv], smem=1, name="fwd")


ERF_SLOPE = 0.35
ERF_FIT = (0.19434814435164116, 0.235843067071591, -0.008625688056468914, 0.6849613674275746, -0.6811631064960405, 0.7727015621272543, -0.19806535099226122)


def gelu_pair(v):
    e = jnp.exp(v * v * -0.5)
    t = 1.0 / (1.0 + jnp.abs(v) * (ERF_SLOPE * math.sqrt(0.5)))
    poly = jnp.full_like(t, 0.5 * ERF_FIT[-1])
    for c in ERF_FIT[-2::-1]:
        poly = poly * t + 0.5 * c
    tail = poly * t * e
    cdf = jnp.where(v >= 0, 1.0 - tail, tail)
    return v * cdf, cdf + v * e * (1.0 / math.sqrt(2.0 * math.pi))


def ffn_kernel(do, perm, unperm, n2, mixed, ew, rw, eb, sv,
               out, dop, dre, dex, dn2, deb, drb,
               act, hlow, hs, ds, n2t, part):
    def permute(i, _):
        b, w = i // 4, i % 4
        rows = pl.ds(pl.multiple_of(i * WT, WT), WT)
        dop[rows, :] = dot(perm[pl.ds(pl.multiple_of(w * WT, WT), WT), :], do[b]).astype(BF16)
        return 0

    lax.fori_loop(0, 8, permute, 0)
    n2t[...] = n2[...].T
    drb[...] = jnp.sum(dop[...].astype(F32), axis=0, keepdims=True)

    def chunk(j, _):
        c = pl.ds(pl.multiple_of(j * 256, 256), 256)
        hs[...] = dot(n2[...], ew[:, c])
        ds[...] = dot(dop[...], rw[c, :], NT)
        bias = eb[0:1, c]
        total = jnp.zeros((8, 256), F32)
        for r in range(18):
            rr = pl.ds(r * 64, 64)
            a, s = gelu_pair(hs[rr, :] + bias)
            act[rr, c] = a.astype(BF16)
            hg = ds[rr, :] * s
            for q in range(8):
                total = total + hg[q * 8:(q + 1) * 8]
            hlow[rr, c] = hg.astype(BF16)
        deb[0:1, c] = jnp.sum(total, axis=0, keepdims=True)
        dre[c, :] = dot(act[:, c], dop[...], TN).astype(BF16)
        dex[:, c] = dot(n2t[...], hlow[:, c]).astype(BF16)
        return 0

    lax.fori_loop(0, FF // 256, chunk, 0)

    for n in range(3):
        c = pl.ds(n * 256, 256)
        part[:, c] = (mixed[:, c] + dot(act[...], rw[:, c]) + sv[7:8, c]).astype(BF16)
        dn2[:, c] = dot(hlow[...], ew[c, :], NT)
    for b in range(2):
        for m in range(4):
            rows = pl.ds(m * WT, WT)
            out[b, rows, :] = dot(unperm[rows, :], part[b * TOK:(b + 1) * TOK, :]).astype(BF16)


def ffn(do, n2, mixed, ew, rw, eb, sv):
    rows = 2 * TOK
    return call(
        ffn_kernel,
        [((2, TOK, D), BF16), ((rows, D), BF16), ((FF, D), BF16), ((D, FF), BF16), ((rows, D), F32), ((1, FF), F32),
         ((1, D), F32)],
        [pltpu.VMEM((rows, FF), BF16), pltpu.VMEM((rows, FF), BF16), pltpu.VMEM((rows, 256), F32),
         pltpu.VMEM((rows, 256), F32), pltpu.VMEM((D, rows), BF16), pltpu.VMEM((rows, D), BF16)],
        [do, jnp.asarray(PERM, BF16), jnp.asarray(PERM.T, BF16), n2, mixed, ew, rw, eb, sv], name="ffn")


def bwd_kernel(counts, unperm, raster, target, mixed, dn2, dop, attended, triple, pt, normed, xp, tm, sv,
               dx, dtm, sg, dtab,
               mg, ml, datt, dtri, bgrad, qs, dos, st, raw, stage, attt, accbuf, t4):
    sgrow = lambda k, v: sg.__setitem__((pl.ds(k, 1), slice(None)), v)

    def norm_back(hat, inv, gain, grad):
        scaled = grad * gain
        return inv * (scaled - jnp.mean(scaled, axis=-1, keepdims=True)
                      - hat * jnp.mean(scaled * hat, axis=-1, keepdims=True))

    sg[...] = jnp.zeros_like(sg)

    def ln2b(i, _):
        rows = pl.ds(pl.multiple_of(i * WT, WT), WT)
        hat, inv = stats(mixed[rows, :])
        g = dn2[rows, :]
        sg[5:6, :] += jnp.sum(g * hat, axis=0, keepdims=True)
        sg[6:7, :] += jnp.sum(g, axis=0, keepdims=True)
        m = dop[rows, :].astype(F32) + norm_back(hat, inv, sv[5:6, :], g)
        sg[4:5, :] += jnp.sum(m, axis=0, keepdims=True)
        mg[rows, :] = m
        ml[rows, :] = m.astype(BF16)
        return 0

    lax.fori_loop(0, 8, ln2b, 0)
    attt[...] = attended[...].T
    for n in range(3):
        c = pl.ds(n * 256, 256)
        dtm[:, pl.ds(2304 + n * 256, 256)] = dot(attt[...], ml[:, c]).astype(BF16)
        datt[:, c] = dot(ml[...], tm[c, 2304:3072], NT).astype(BF16)

    bgrad[...] = jnp.zeros_like(bgrad)

    def attn(t, _):
        i, g = t // GROUPS, t % GROUPS
        b, w = i // 4, i % 4
        rows = pl.ds(pl.multiple_of(i * WT, WT), WT)
        col = lambda k: pl.ds(pl.multiple_of(k * D + g * GW, GW), GW)
        valid = raster[w] < counts[b]
        vq = jnp.concatenate([valid, valid], axis=1)
        da = datt[rows, pl.ds(pl.multiple_of(g * GW, GW), GW)]
        da = jnp.where(vq, da.astype(F32), 0.0).astype(BF16)
        head_stack(qs, triple[rows, col(0)])
        head_stack(dos, da)
        st[...] = dot(triple[rows, col(2)], dos[...], NT)
        for n in range(9):
            c = pl.ds(n * 128, 128)
            p = pt[t, :, c].astype(F32)
            d = st[:, c]
            inner = jnp.sum(p * d, axis=0, keepdims=True)
            s = p * (d - inner)
            bgrad[g * 9 + n] += s
            raw[:, c] = (s * SCALE).astype(BF16)
        dtri[rows, col(2)] = dot(pt[t], dos[...]).astype(BF16)
        dtri[rows, col(1)] = dot(raw[...], qs[...]).astype(BF16)
        dtri[rows, col(0)] = head_pick(dot(raw[...], triple[rows, col(0 + 1)], TN)).astype(BF16)
        return 0

    lax.fori_loop(0, 8 * GROUPS, attn, 0)
    gather_bias(bgrad, accbuf, t4, target, dtab)

    attt[...] = normed[...].T
    for n in range(9):
        c = pl.ds(n * 256, 256)
        if n < 3 or n >= 6:
            k, o = (2, n * 256) if n < 3 else (3, (n - 6) * 256)
            sg[k:k + 1, o:o + 256] = jnp.sum(dtri[:, c].astype(F32), axis=0, keepdims=True)
        dtm[:, c] = dot(attt[...], dtri[:, c]).astype(BF16)
    for n in range(3):
        c = pl.ds(n * 256, 256)
        stage[:, c] = dot(dtri[...], tm[c, 0:2304], NT)

    def ln1b(i, _):
        rows = pl.ds(pl.multiple_of(i * WT, WT), WT)
        hat, inv = stats(xp[rows, :].astype(F32))
        g = stage[rows, :]
        sg[0:1, :] += jnp.sum(g * hat, axis=0, keepdims=True)
        sg[1:2, :] += jnp.sum(g, axis=0, keepdims=True)
        m = mg[rows, :] + norm_back(hat, inv, sv[0:1, :], g)
        ml[rows, :] = m.astype(BF16)
        return 0

    lax.fori_loop(0, 8, ln1b, 0)
    for b in range(2):
        for m in range(4):
            rows = pl.ds(m * WT, WT)
            dx[b, rows, :] = dot(unperm[rows, :], ml[b * TOK:(b + 1) * TOK, :]).astype(BF16)


def gather_bias(bgrad, accbuf, t4, target, dtab):
    lane = lane_iota((1, QL))
    a_of = (lane % WT) // WIN
    c_of = lane_iota((WIN, QL)) % WIN
    for g in range(GROUPS):
        pos = jnp.zeros((WIN, QL), F32)
        neg = jnp.zeros((WIN, QL), F32)
        for d in range(WIN):
            r = jnp.concatenate([bgrad[g * 9 + n, pl.ds(d, WIN, stride=WIN), :] for n in range(9)], axis=1)
            p = jnp.where(c_of >= d, r, 0.0)
            pos = pos + (pltpu.roll(p, QL - d, axis=1) if d else p)
            if d:
                neg = neg + pltpu.roll(jnp.where(c_of < d, r, 0.0), WIN - d, axis=1)
        accbuf[0, 0:WIN, :] = pos
        accbuf[1, 0:WIN, :] = neg
        for s in range(2):
            pp = jnp.zeros((1, QL), F32)
            nn = jnp.zeros((1, QL), F32)
            for b in range(WIN):
                r = accbuf[s, b:b + 1, :]
                p = jnp.where(a_of >= b, r, 0.0)
                pp = pp + (pltpu.roll(p, QL - WIN * b, axis=1) if b else p)
                if b:
                    nn = nn + pltpu.roll(jnp.where(a_of < b, r, 0.0), WT - WIN * b, axis=1)
            for part, row in ((s, pp), (2 + s, nn)):
                for h in range(GH):
                    moved = pltpu.roll(row, QL - h * WT, axis=1) if h else row
                    t4[g * GH + h:g * GH + h + 1, part * WT:(part + 1) * WT] = moved[:, 0:WT]
    dtab[...] = t4[...]


def backward(counts, mixed, dn2, dop, attended, triple, pt, normed, xp, tm, sv):
    rows = 2 * TOK
    return call(
        bwd_kernel,
        [((2, TOK, D), BF16), ((D, 4 * D), BF16), ((8, D), F32), ((HEADS, 4 * WT), F32)],
        [pltpu.VMEM((rows, D), F32), pltpu.VMEM((rows, D), BF16), pltpu.VMEM((rows, D), BF16),
         pltpu.VMEM((rows, 3 * D), BF16), pltpu.VMEM((GROUPS * 9, WT, 128), F32), pltpu.VMEM((QL, GW), BF16),
         pltpu.VMEM((QL, GW), BF16), pltpu.VMEM((WT, QL), F32), pltpu.VMEM((WT, QL), BF16),
         pltpu.VMEM((rows, D), F32), pltpu.VMEM((D, rows), BF16),
         pltpu.VMEM((2, 16, QL), F32), pltpu.VMEM((HEADS, 4 * WT), F32)],
        [counts, jnp.asarray(PERM.T, BF16), jnp.asarray(RASTER_L), jnp.asarray(TARGET), mixed, dn2, dop, attended,
         triple, pt, normed, xp, tm, sv], smem=1, name="bwd")


def table_kernel(target, t4, table):
    table[...] = lax.dot_general(onehot(target), t4[...], NT, precision=lax.Precision.HIGHEST,
                                 preferred_element_type=F32)


AXES = ("dp", "fsdp")
MESH = pl.DeviceIdType.MESH


class Place:
    def __init__(self, dims):
        self.nz, self.ny, self.nx = dims
        f = lax.axis_index("fsdp")
        self.z = lax.axis_index("dp")
        self.c = lax.rem(f, 2)
        self.x = lax.rem(f // 2, self.nx)
        self.y = f // (2 * self.nx)

    def size(self, axis):
        return {"z": self.nz, "y": self.ny, "x": self.nx, "c": 2}[axis]

    def at(self, axis):
        return {"z": self.z, "y": self.y, "x": self.x, "c": self.c}[axis]

    def step(self, axis, k):
        n = self.size(axis)
        return lax.rem(self.at(axis) + k, n)

    def device(self, axis, k):
        p = {a: (self.step(a, k) if a == axis else self.at(a)) for a in "zyxc"}
        return (p["z"], (p["y"] * self.nx + p["x"]) * 2 + p["c"])

    def greet(self):
        barrier = pltpu.get_barrier_semaphore()
        total = 0
        for axis in "czyx":
            for k in range(1, self.size(axis)):
                pl.semaphore_signal(barrier, inc=1, device_id=self.device(axis, k), device_id_type=MESH)
                total += 1
        pl.semaphore_wait(barrier, total)


def mesh_dims(mesh):
    chips = mesh.shape["fsdp"] // 2
    ny = max(n for n in range(1, chips + 1) if n * n <= chips and chips % n == 0)
    return mesh.shape["dp"], ny, chips // ny


class Sems:
    def __init__(self, send, recv):
        self.send, self.recv, self.used = send, recv, 0

    def take(self):
        self.used += 1
        return self.send.at[self.used - 1], self.recv.at[self.used - 1]


class Swap:
    def __init__(self, place, sems, axis, src, dst, from_slot):
        self.copies = []
        for k in range(1, place.size(axis)):
            s, r = sems.take()
            out = pltpu.make_async_remote_copy(src_ref=src(k), dst_ref=dst(k), send_sem=s, recv_sem=r,
                                               device_id=place.device(axis, k), device_id_type=MESH)
            back = pltpu.make_async_remote_copy(src_ref=from_slot(k), dst_ref=from_slot(k), send_sem=s, recv_sem=r,
                                                device_id=place.device(axis, k), device_id_type=MESH)
            self.copies.append((out, back))

    def start(self):
        for out, _ in self.copies:
            out.start()

    def arrive(self):
        for _, back in self.copies:
            back.wait_recv()

    def done(self):
        for out, _ in self.copies:
            out.wait_send()


def cols_at(c, half, lo, width):
    return pl.ds(pl.multiple_of(c * half + lo, 128), width)


def gather_chain(place, sems, ref, order, block):
    z, y, x = place.z, place.y, place.x
    first, second = order
    own = lambda zz, yy, xx: ref.at[(zz, yy, xx) + block(place.c)]
    every = slice(None)
    chain = [Swap(place, sems, "z", lambda k: own(z, y, x), lambda k: own(z, y, x),
                  lambda k: own(place.step("z", place.nz - k), y, x))]
    back = lambda a, k: place.step(a, place.size(a) - k)
    if first == "x":
        chain.append(Swap(place, sems, "x", lambda k: own(every, y, x), lambda k: own(every, y, x),
                          lambda k: own(every, y, back("x", k))))
        chain.append(Swap(place, sems, "y", lambda k: own(every, y, every), lambda k: own(every, y, every),
                          lambda k: own(every, back("y", k), every)))
    else:
        chain.append(Swap(place, sems, "y", lambda k: own(every, y, x), lambda k: own(every, y, x),
                          lambda k: own(every, back("y", k), x)))
        chain.append(Swap(place, sems, "x", lambda k: own(every, every, x), lambda k: own(every, every, x),
                          lambda k: own(every, every, back("x", k))))
    mine = lambda k: ref.at[(every, every, every) + block(place.c)]
    other = lambda k: ref.at[(every, every, every) + block(1 - place.c)]
    chain.append(Swap(place, sems, "c", mine, mine, other))
    return chain


def wide_block(lo, width, r=None):
    def block(c):
        return (slice(None) if r is None else r, cols_at(c, 1536, lo, width))
    return block


def tall_block(lo, rows):
    def block(c):
        return (pl.ds(lo, rows), cols_at(c, 384, 0, 384))
    return block


def gather_pieces(place, sems, tm, ew, rw, sb):
    both = lambda ref, make, parts: [gather_chain(place, sems, ref, o, make(*p)) for o, p in zip(("xy", "yx"), parts)]
    small = gather_chain(place, sems, sb, "xy", lambda c: (c,))
    pieces = []
    for ref in (tm, ew):
        for p in range(2):
            lo = p * 768
            pieces.append(both(ref, wide_block, ((lo, 384), (lo + 384, 384))))
    rows = rw.shape[3]
    for p in range(2):
        lo = p * rows // 2
        pieces.append(both(rw, tall_block, ((lo, rows // 4), (lo + rows // 4, rows // 4))))
    pieces[0].append(small)
    return pieces


def run_chains(pieces):
    depth = 4
    for t in range(len(pieces) + depth):
        for p in range(max(0, t - depth), min(t, len(pieces) - 1) + 1):
            s = t - p
            for chain in pieces[p]:
                if s > 0:
                    chain[s - 1].arrive()
                if s < depth:
                    chain[s].start()
    for piece in pieces:
        for chain in piece:
            for swap in chain:
                swap.done()


def place_small(sb, sv, eb, lanes, wide):
    nz, ny, nx = sb.shape[:3]
    for out, row0, width, total in ((sv, 0, lanes, D), (eb, 8, wide, FF)):
        tiles = [jnp.zeros((8, 128), F32) for _ in range(total // 128)]
        lane = lane_iota((8, 128))
        n = 0
        for q in range(nz * ny * nx):
            for c in range(2):
                blk = sb[q // (ny * nx), (q // nx) % ny, q % nx, c, row0:row0 + 8, :]
                tile, off = divmod(n * width, 128)
                moved = pltpu.roll(blk, off, axis=1) if off else blk
                end = off + width
                tiles[tile] = jnp.where((lane >= off) & (lane < min(end, 128)), moved, tiles[tile])
                if end > 128:
                    tiles[tile + 1] = jnp.where(lane < end - 128, moved, tiles[tile + 1])
                n += 1
        out[...] = jnp.concatenate(tiles, axis=1)


def own_blocks(place, sems, stage_tm, stage_ew, stage_rw, mt, me, mr):
    swaps = []
    for ref, stage, half in ((mt, stage_tm, 1536), (me, stage_ew, 1536), (mr, stage_rw, 384)):
        r = ref.shape[0]
        mine = pl.ds(pl.multiple_of(place.c * r, 8), r)
        theirs = pl.ds(pl.multiple_of((1 - place.c) * r, 8), r)
        swaps.append(Swap(place, sems, "c", lambda k, ref=ref, half=half: ref.at[:, cols_at(1 - place.c, half, 0, half)],
                          lambda k, stage=stage, mine=mine: stage.at[mine, :],
                          lambda k, stage=stage, theirs=theirs: stage.at[theirs, :]))
    return swaps


def gather_kernel(dims, mt, me, mr, small, tm, ew, rw, sv, eb, sb, st_t, st_e, st_r, send, recv):
    place = Place(dims)
    sems = Sems(send, recv)
    place.greet()
    first = own_blocks(place, sems, st_t, st_e, st_r, mt, me, mr)
    for s in first:
        s.start()
    z, y, x, c = place.z, place.y, place.x, place.c
    sb[z, y, x, c] = small[...].astype(BF16).astype(F32)
    for s, ref, stage, full, half in zip(first, (mt, me, mr), (st_t, st_e, st_r), (tm, ew, rw), (1536, 1536, 384)):
        r = ref.shape[0]
        stage[pl.ds(pl.multiple_of(c * r, 8), r), :] = ref[:, cols_at(c, half, 0, half)]
        s.arrive()
        full[z, y, x, :, cols_at(c, half, 0, half)] = stage[...].astype(BF16)
    run_chains(gather_pieces(place, sems, tm, ew, rw, sb))
    for s in first:
        s.done()
    place_small(sb, sv, eb, D // (2 * dims[0] * dims[1] * dims[2]), FF // (2 * dims[0] * dims[1] * dims[2]))


def gather_weights(dims, mt, me, mr, small):
    nz, ny, nx = dims
    r, rr = mt.shape[0], mr.shape[0]
    n = 3 + 13 * (nz + ny + nx - 2)
    return pl.pallas_call(
        functools.partial(gather_kernel, dims),
        out_shape=[jax.ShapeDtypeStruct((nz, ny, nx, 2 * r, 4 * D), BF16), jax.ShapeDtypeStruct((nz, ny, nx, 2 * r, FF), BF16),
                   jax.ShapeDtypeStruct((nz, ny, nx, 2 * rr, D), BF16), jax.ShapeDtypeStruct((8, D), F32),
                   jax.ShapeDtypeStruct((8, FF), F32)],
        in_specs=[pl.BlockSpec(memory_space=pltpu.VMEM)] * 4,
        out_specs=[pl.BlockSpec(memory_space=pltpu.VMEM)] * 5,
        scratch_shapes=[pltpu.VMEM((nz, ny, nx, 2, 16, 128), F32), pltpu.VMEM((2 * r, 1536), F32),
                        pltpu.VMEM((2 * r, 1536), F32), pltpu.VMEM((2 * rr, 384), F32),
                        pltpu.SemaphoreType.DMA((n,)), pltpu.SemaphoreType.DMA((n,))],
        name="gather",
        compiler_params=pltpu.CompilerParams(vmem_limit_bytes=VMEM_LIMIT, collective_id=0, has_side_effects=True),
    )(mt, me, mr, small)


def scatter_chain(place, sems, g, recv0, recv1, recv2, recv3, out, order, part):
    z, y, x, c = place.z, place.y, place.x, place.c
    every = slice(None)
    lo_row, n_row, half, lo, width = part
    rows = pl.ds(lo_row, n_row)
    mine, other = cols_at(c, half, lo, width), cols_at(1 - c, half, lo, width)
    first, second = order
    place_of = {"z": z, "y": y, "x": x}

    def pick(a, v, b=None, w=None):
        sel = {"z": every, "y": every, "x": every}
        sel[a] = v
        if b:
            sel[b] = w
        return (sel["z"], sel["y"], sel["x"])

    steps = []
    swap = Swap(place, sems, "c", lambda k: g.at[every, every, every, rows, other], lambda k: recv0, lambda k: recv0)

    def add0():
        recv0[...] = (recv0[...].astype(F32) + g[:, :, :, rows, mine].astype(F32)).astype(BF16)

    steps.append((swap, add0))
    n1 = place.size(first)
    slot = lambda a, k: place.size(a) - 1 - k
    swap = Swap(place, sems, first, lambda k: recv0.at[pick(first, place.step(first, k))], lambda k: recv1.at[k - 1],
                lambda k: recv1.at[k - 1])

    def add1():
        s = recv0[pick(first, place_of[first])].astype(F32)
        for k in range(n1 - 1):
            s = s + recv1[k].astype(F32)
        recv1[0] = s.astype(BF16)

    steps.append((swap, add1))
    n2 = place.size(second)
    swap = Swap(place, sems, second, lambda k: recv1.at[(0, every, place.step(second, k))], lambda k: recv2.at[k - 1],
                lambda k: recv2.at[k - 1])

    def add2():
        s = recv1[(0, every, place_of[second])].astype(F32)
        for k in range(n2 - 1):
            s = s + recv2[k].astype(F32)
        recv2[0] = s.astype(BF16)

    steps.append((swap, add2))
    swap = Swap(place, sems, "z", lambda k: recv2.at[0, place.step("z", k)], lambda k: recv3.at[k - 1],
                lambda k: recv3.at[k - 1])
    final = recv3.shape[0]

    return steps, swap


def scatter_kernel(dims, dtm, dex, dre, sg, deb, t4, otm, oex, ore, osg, oeb, ot4, *scratch):
    place = Place(dims)
    nz, ny, nx = dims
    send, recv = scratch[-2:]
    sems = Sems(send, recv)
    place.greet()
    bufs = list(scratch[:-2])
    z, y, x, c = place.z, place.y, place.x, place.c
    every = slice(None)
    pieces, finals = [], []

    def piece(g, out, order, part):
        recv0, recv1, recv2, recv3, fin = bufs.pop(0), bufs.pop(0), bufs.pop(0), bufs.pop(0), bufs.pop(0)
        steps, zswap = scatter_chain(place, sems, g, recv0, recv1, recv2, recv3, out, order, part)
        lo_row, n_row, half, lo, width = part
        r = out.shape[0]

        def add3():
            s = recv2[0, z].astype(F32)
            for k in range(nz - 1):
                s = s + recv3[k].astype(F32)
            fin[...] = s

        steps.append((zswap, add3))
        return steps, fin

    def small_chain(buf, slots):
        steps = []
        for i, a in enumerate("cyxz"):
            n = place.size(a)
            base = sum(place.size(b) for b in "cyxz"[:i])
            me = base + place.at(a)
            swap = Swap(place, sems, a, lambda k, me=me: slots.at[me], lambda k, me=me: slots.at[me],
                        lambda k, base=base, n=n, a=a: slots.at[base + place.step(a, n - k)])

            def add(base=base, n=n, i=i):
                s = slots[base]
                for k in range(1, n):
                    s = s + slots[base + k]
                if i < 3:
                    b = "cyxz"[i + 1]
                    slots[base + n + place.at(b)] = s
                else:
                    buf[...] = s

            steps.append((swap, add))
        return steps

    buf, slots = bufs.pop(0), bufs.pop(0)
    slots[c] = jnp.zeros_like(buf)
    slots[c, 0:8, :] = sg[...]
    for k in range(4):
        slots[c, 8 + k:9 + k, :] = deb[0:1, k * D:(k + 1) * D]
    slots[c, 16:40, 0:4 * WT] = t4[...]

    last = []
    chains = []
    for g, out in ((dtm, otm), (dex, oex)):
        for p in range(2):
            pair = []
            for order, lo in (("yx", p * 768), ("xy", p * 768 + 384)):
                part = (0, g.shape[3], 1536, lo, 384)
                steps, fin = piece(g, out, order, part)
                pair.append(steps)
                last.append((out, fin, part))
            chains.append(pair)
    rr = dre.shape[3]
    for p in range(2):
        pair = []
        for order, lo in (("yx", p * rr // 2), ("xy", p * rr // 2 + rr // 4)):
            part = (lo, rr // 4, 384, 0, 384)
            steps, fin = piece(dre, ore, order, part)
            pair.append(steps)
            last.append((ore, fin, part))
        chains.append(pair)
    chains.append([small_chain(buf, slots)])
    depth = 4
    for t in range(len(chains) + depth):
        for p in range(max(0, t - depth), min(t, len(chains) - 1) + 1):
            s = t - p
            for steps in chains[p]:
                if s > 0:
                    steps[s - 1][0].arrive()
                    steps[s - 1][1]()
                if s < depth:
                    steps[s][0].start()
    for pair in chains:
        for steps in pair:
            for swap, _ in steps:
                swap.done()
    ends = []
    for out, fin, (lo_row, n_row, half, lo, width) in last:
        r = out.shape[0]
        if n_row == 2 * r:
            src = fin.at[pl.ds(pl.multiple_of((1 - c) * r, 8), r), :]
            dst = out.at[:, cols_at(c, half, lo, width)]
            back = out.at[:, cols_at(1 - c, half, lo, width)]
            out[:, cols_at(c, half, lo, width)] = fin[pl.ds(pl.multiple_of(c * r, 8), r), :]
            ends.append(Swap(place, sems, "c", lambda k, src=src: src, lambda k, dst=dst: dst, lambda k, back=back: back))
    tall = [(fin, part) for out, fin, part in last if out is ore]
    full = bufs.pop(0)
    for fin, (lo_row, n_row, half, lo, width) in tall:
        full[lo_row:lo_row + n_row, :] = fin[...]
    r = ore.shape[0]
    ore[:, cols_at(c, 384, 0, 384)] = full[pl.ds(pl.multiple_of(c * r, 8), r), :]
    ends.append(Swap(place, sems, "c", lambda k: full.at[pl.ds(pl.multiple_of((1 - c) * r, 8), r), :],
                     lambda k: ore.at[:, cols_at(c, 384, 0, 384)], lambda k: ore.at[:, cols_at(1 - c, 384, 0, 384)]))
    for e in ends:
        e.start()
    dev = z * (2 * ny * nx) + (y * nx + x) * 2 + c
    lanes = osg.shape[1]
    shift = lax.rem(D - dev * lanes, D)
    osg[...] = pltpu.roll(buf[0:8, :], shift, axis=1)[:, 0:lanes]
    wide = oeb.shape[1]
    per = D // wide
    row = buf[pl.ds(8 + dev // per, 1), :]
    oeb[...] = pltpu.roll(row, lax.rem(D - lax.rem(dev, per) * wide, D), axis=1)[:, 0:wide]
    ot4[...] = buf[16:40, 0:4 * WT]
    for e in ends:
        e.arrive()
        e.done()


def scatter_grads(dims, dtm, dex, dre, sg, deb, t4):
    nz, ny, nx = dims
    ndev = 2 * nz * ny * nx
    r, rr = D // ndev, FF // ndev
    scratch = [pltpu.VMEM((40, D), F32), pltpu.VMEM((2 + nz + ny + nx, 40, D), F32)]
    for i, (n_row, width) in enumerate([(2 * r, 384)] * 8 + [(2 * rr // 4, 384)] * 4):
        order = "xy" if i % 2 else "yx"
        n1, n2 = (ny, nx) if order == "yx" else (nx, ny)
        scratch += [pltpu.VMEM((nz, ny, nx, n_row, width), BF16), pltpu.VMEM((n1 - 1, nz, n2, n_row, width), BF16),
                    pltpu.VMEM((n2 - 1, nz, n_row, width), BF16), pltpu.VMEM((nz - 1, n_row, width), BF16),
                    pltpu.VMEM((n_row, width), F32)]
    n = 13 * (1 + nz + ny + nx - 3) + 9
    scratch += [pltpu.VMEM((2 * rr, 384), F32),
                pltpu.SemaphoreType.DMA((n,)), pltpu.SemaphoreType.DMA((n,))]
    return pl.pallas_call(
        functools.partial(scatter_kernel, dims),
        out_shape=[jax.ShapeDtypeStruct((r, 4 * D), F32), jax.ShapeDtypeStruct((r, FF), F32),
                   jax.ShapeDtypeStruct((rr, D), F32), jax.ShapeDtypeStruct((8, r), F32),
                   jax.ShapeDtypeStruct((1, rr), F32), jax.ShapeDtypeStruct((HEADS, 4 * WT), F32)],
        in_specs=[pl.BlockSpec(memory_space=pltpu.VMEM)] * 6,
        out_specs=[pl.BlockSpec(memory_space=pltpu.VMEM)] * 6,
        scratch_shapes=scratch,
        name="scatter",
        compiler_params=pltpu.CompilerParams(vmem_limit_bytes=VMEM_LIMIT, collective_id=1, has_side_effects=True),
    )(dtm.reshape(nz, ny, nx, 2 * r, 4 * D), dex.reshape(nz, ny, nx, 2 * r, FF), dre.reshape(nz, ny, nx, 2 * rr, D),
      sg, deb, t4)


def shards(dims, block_input, valid_counts, output_cotangent, triple_weight, merge_weight, expand_weight, reduce_weight,
           first_gain, first_shift, query_bias, value_bias, merge_bias, second_gain, second_shift, expand_bias,
           reduce_bias, position_table):
    x = block_input[:, 0]
    do = output_cotangent[:, 0]
    counts = valid_counts[:, 0]
    small = jnp.stack([first_gain, first_shift, query_bias, value_bias, merge_bias, second_gain, second_shift,
                       reduce_bias])
    tm_own = jnp.concatenate([triple_weight, merge_weight], axis=1)
    near = triple_weight.shape[0] % 8 == 0
    if near:
        block = jnp.zeros((16, 128), F32).at[:8, :small.shape[1]].set(small)
        block = block.at[8, :expand_bias.shape[0]].set(expand_bias)
        tm, ew, rw, sv, eb = gather_weights(dims, tm_own, expand_weight, reduce_weight, block)
        tm, ew, rw = tm.reshape(D, 4 * D), ew.reshape(D, FF), rw.reshape(FF, D)
    else:
        gather = lambda v, axis: lax.all_gather(v.astype(BF16), AXES, axis=axis, tiled=True)
        tm, ew, rw = gather(tm_own, 0), gather(expand_weight, 0), gather(reduce_weight, 0)
        sv, eb = gather(small, 1).astype(F32), gather(expand_bias, 0).astype(F32)[None]
    xp, normed, triple, pt, attended, mixed, n2 = forward(counts, x, position_table, tm, sv)
    out, dop, dre, dex, dn2, deb, drb = ffn(do, n2, mixed, ew, rw, eb, sv)
    dx, dtm, sg, t4 = backward(counts, mixed, dn2, dop, attended, triple, pt, normed, xp, tm, sv)
    sg = jnp.concatenate([sg[:7], drb])
    if near:
        otm, oex, ore, osg, oeb, ot4 = scatter_grads(dims, dtm, dex, dre, sg, deb, t4)
        oeb = oeb[0]
    else:
        scatter = lambda v, axis: lax.psum_scatter(v.astype(F32), AXES, scatter_dimension=axis, tiled=True)
        otm, oex, ore, osg, oeb = scatter(dtm, 0), scatter(dex, 0), scatter(dre, 0), scatter(sg, 1), scatter(deb[0], 0)
        ot4 = lax.psum(t4, AXES)
    table = call(table_kernel, [(((2 * WIN - 1) ** 2, HEADS), F32)], [], [jnp.asarray(TARGET), ot4], name="table")[0]
    return (out[:, None], dx[:, None], otm[:, :2304], otm[:, 2304:], oex, ore,
            osg[0], osg[1], osg[2], osg[3], osg[4], osg[5], osg[6], oeb, osg[7], table)


def solution(mesh):
    image = P(None, AXES, None, None)
    rows = P(AXES, None)
    vec = P(AXES)
    return jax.shard_map(
        functools.partial(shards, mesh_dims(mesh)), mesh=mesh,
        in_specs=(image, P(None, AXES), image) + (rows,) * 4 + (vec,) * 9 + (P(),),
        out_specs=(image, image) + (rows,) * 4 + (vec,) * 9 + (P(),),
        check_vma=False)
```

```python
import math
import functools

import numpy as np
import jax
import jax.numpy as jnp
from jax import lax
from jax.experimental import pallas as pl
from jax.experimental.pallas import tpu as pltpu
from jax.sharding import PartitionSpec as P

D = 768
FF = 3072
HEADS = 24
HEAD_DIM = 32
WIN = 12
SIDE = 24
SHIFT = 6
TOK = SIDE * SIDE
ROWS = 2 * TOK
WT = WIN * WIN
EXT = 2 * WIN - 1
GROUPS = 3
GH = HEADS // GROUPS
GW = GH * HEAD_DIM
QL = GH * WT
SCALE = HEAD_DIM ** -0.5
MASKED = -1e30
EPS = 1e-5
F32 = jnp.float32
BF16 = jnp.bfloat16
VMEM_LIMIT = 63 << 20
AXES = ("dp", "fsdp")
MESH = pl.DeviceIdType.MESH
ANY = pl.BlockSpec(memory_space=pl.ANY)
VM = pl.BlockSpec(memory_space=pltpu.VMEM)
SM = pl.BlockSpec(memory_space=pltpu.SMEM)
every = slice(None)

NN = (((1,), (0,)), ((), ()))
NT = (((1,), (1,)), ((), ()))
TN = (((0,), (0,)), ((), ()))


def dot(a, b, dims=NN):
    return lax.dot_general(a, b, dims, preferred_element_type=F32)


def layout_constants():
    j = np.arange(WT)
    raster = np.zeros((4, WT), np.int32)
    label = np.zeros((4, WT), np.int32)
    reg = lambda c: (c >= SIDE - WIN).astype(np.int32) + (c >= SIDE - SHIFT).astype(np.int32)
    for w in range(4):
        rr = (w // 2) * WIN + j // WIN
        rc = (w % 2) * WIN + j % WIN
        raster[w] = ((rr + SHIFT) % SIDE) * SIDE + (rc + SHIFT) % SIDE
        label[w] = reg(rr) * 3 + reg(rc)
    target = np.full((4, WT), -1, np.int32)
    for p in range(4):
        r = j // WIN + (WIN - 1 if p // 2 == 0 else -1)
        s = j % WIN + (WIN - 1 if p % 2 == 0 else -1)
        target[p] = np.where((r >= 0) & (s >= 0), r * EXT + s, -1)
    spread = lambda v, shape: np.broadcast_to(v, shape).astype(np.int32)
    return (spread(raster[:, :, None], (4, WT, 128)), spread(label[:, :, None], (4, WT, 128)),
            spread(np.tile(label, (1, GH))[:, None, :], (4, 8, QL)), spread(target.reshape(1, 4 * WT), (8, 4 * WT)),
            spread(raster.reshape(1, TOK), (8, TOK)))


RASTER_L, LABEL_L, LABEL_Q, TARGET, RASTER_Q = layout_constants()


def lane_iota(shape):
    return lax.broadcasted_iota(jnp.int32, shape, len(shape) - 1)


def aligned(v, n):
    return v if isinstance(v, int) else pl.multiple_of(v, n)


def lanes(start, width):
    return pl.ds(aligned(start, 128), width)


def window(i):
    return pl.ds(aligned(i * WT, WT), WT)


def to_window(raster, w):
    return (raster[w][:, 0:1] == lane_iota((WT, TOK))).astype(BF16)


def to_raster(raster_q, m):
    t = lax.broadcasted_iota(jnp.int32, (WT, TOK), 0) + m * WT
    return (raster_q[0:1, :] == t).astype(BF16)


def stats(x):
    mean = jnp.mean(x, axis=-1, keepdims=True)
    center = x - mean
    var = jnp.mean(center * center, axis=-1, keepdims=True)
    inv = lax.rsqrt(var + EPS)
    return center * inv, inv


def head_stack(dst, x):
    lane = lane_iota(x.shape) // HEAD_DIM
    zero = jnp.zeros_like(x)
    for h in range(GH):
        dst[h * WT:(h + 1) * WT, :] = jnp.where(lane == h, x, zero)


def head_pick(o):
    lane = lane_iota((WT, GW)) // HEAD_DIM
    out = jnp.where(lane == 0, o[0:WT], 0.0)
    for h in range(1, GH):
        out = jnp.where(lane == h, o[h * WT:(h + 1) * WT], out)
    return out


def onehot(target_ref):
    t = lax.broadcasted_iota(jnp.int32, (EXT * EXT, 4 * WT), 0)
    return (t == target_ref[0:1, :]).astype(F32)


def table_rows(table_ref, target_ref, t4):
    t4[...] = lax.dot_general(table_ref[...], onehot(target_ref), TN,
                              precision=lax.Precision.HIGHEST, preferred_element_type=F32) * (1.0 / SCALE)


def spread_bias(g, t4, bias, rowbuf):
    a_of = (lane_iota((1, QL)) % WT) // WIN
    c_of = lane_iota((16, QL)) % WIN
    rows = []
    for p in range(4):
        acc = jnp.zeros((1, QL), F32)
        for h in range(GH):
            piece = t4[pl.ds(g * GH + h, 1), p * WT:(p + 1) * WT]
            piece = jnp.concatenate([piece, jnp.zeros((1, QL - WT), F32)], axis=1)
            acc = acc + (pltpu.roll(piece, h * WT, axis=1) if h else piece)
        rows.append(acc)
    for s in range(2):
        for b in range(WIN):
            pos = pltpu.roll(rows[s], WIN * b, axis=1) if b else rows[s]
            neg = pltpu.roll(rows[2 + s], (WIN * b - WT) % QL, axis=1)
            rowbuf[s, b:b + 1, :] = jnp.where(a_of >= b, pos, neg)
    for d in range(WIN):
        pos = pltpu.roll(rowbuf[0], d, axis=1) if d else rowbuf[0]
        neg = pltpu.roll(rowbuf[1], (d - WIN) % QL, axis=1)
        both = jnp.where(c_of >= d, pos, neg)
        for n in range(9):
            bias[g * 9 + n, pl.ds(d, WIN, stride=WIN), :] = both[0:WIN, n * 128:(n + 1) * 128]


def gather_bias(g, bgrad, accbuf, t4):
    a_of = (lane_iota((1, QL)) % WT) // WIN
    c_of = lane_iota((WIN, QL)) % WIN
    pos = jnp.zeros((WIN, QL), F32)
    neg = jnp.zeros((WIN, QL), F32)
    for d in range(WIN):
        r = jnp.concatenate([bgrad[n, pl.ds(d, WIN, stride=WIN), :] for n in range(9)], axis=1)
        p = jnp.where(c_of >= d, r, 0.0)
        pos = pos + (pltpu.roll(p, QL - d, axis=1) if d else p)
        if d:
            neg = neg + pltpu.roll(jnp.where(c_of < d, r, 0.0), WIN - d, axis=1)
    accbuf[0, 0:WIN, :] = pos
    accbuf[1, 0:WIN, :] = neg
    for s in range(2):
        pp = jnp.zeros((1, QL), F32)
        nn = jnp.zeros((1, QL), F32)
        for b in range(WIN):
            r = accbuf[s, b:b + 1, :]
            p = jnp.where(a_of >= b, r, 0.0)
            pp = pp + (pltpu.roll(p, QL - WIN * b, axis=1) if b else p)
            if b:
                nn = nn + pltpu.roll(jnp.where(a_of < b, r, 0.0), WT - WIN * b, axis=1)
        for part, row in ((s, pp), (2 + s, nn)):
            for h in range(GH):
                moved = pltpu.roll(row, QL - h * WT, axis=1) if h else row
                t4[pl.ds(g * GH + h, 1), part * WT:(part + 1) * WT] = moved[:, 0:WT]


ERF_SLOPE = 0.35
ERF_FIT = (0.19434814435164116, 0.235843067071591, -0.008625688056468914, 0.6849613674275746, -0.6811631064960405, 0.7727015621272543, -0.19806535099226122)


def gelu_pair(v):
    e = jnp.exp(v * v * -0.5)
    t = 1.0 / (1.0 + jnp.abs(v) * (ERF_SLOPE * math.sqrt(0.5)))
    poly = jnp.full_like(t, 0.5 * ERF_FIT[-1])
    for c in ERF_FIT[-2::-1]:
        poly = poly * t + 0.5 * c
    tail = poly * t * e
    cdf = jnp.where(v >= 0, 1.0 - tail, tail)
    return v * cdf, cdf + v * e * (1.0 / math.sqrt(2.0 * math.pi))


def norm_back(hat, inv, gain, grad):
    scaled = grad * gain
    return inv * (scaled - jnp.mean(scaled, axis=-1, keepdims=True)
                  - hat * jnp.mean(scaled * hat, axis=-1, keepdims=True))


class Place:
    def __init__(self, dims):
        self.nz, self.ny, self.nx = dims
        f = lax.axis_index("fsdp")
        self.z = lax.axis_index("dp")
        self.c = lax.rem(f, 2)
        self.x = lax.rem(f // 2, self.nx)
        self.y = f // (2 * self.nx)

    def size(self, axis):
        return {"z": self.nz, "y": self.ny, "x": self.nx, "c": 2}[axis]

    def at(self, axis):
        return {"z": self.z, "y": self.y, "x": self.x, "c": self.c}[axis]

    def step(self, axis, k):
        return lax.rem(self.at(axis) + k, self.size(axis))

    def back(self, axis, k):
        return self.step(axis, self.size(axis) - k)

    def device(self, axis, k):
        p = {a: (self.step(a, k) if a == axis else self.at(a)) for a in "zyxc"}
        return (p["z"], (p["y"] * self.nx + p["x"]) * 2 + p["c"])

    def greet(self):
        barrier = pltpu.get_barrier_semaphore()
        total = 0
        for axis in "czyx":
            for k in range(1, self.size(axis)):
                pl.semaphore_signal(barrier, inc=1, device_id=self.device(axis, k), device_id_type=MESH)
                total += 1
        pl.semaphore_wait(barrier, total)


def mesh_dims(mesh):
    chips = mesh.shape["fsdp"] // 2
    ny = max(n for n in range(1, chips + 1) if n * n <= chips and chips % n == 0)
    return mesh.shape["dp"], ny, chips // ny


class Swap:
    def __init__(self, place, axis, sems, src, dst, came, has=None):
        self.has = has
        self.place, self.axis, self.sems = place, axis, sems
        self.src, self.dst, self.came = src, dst, came

    def make(self, k, src, dst):
        return pltpu.make_async_remote_copy(
            src_ref=src(k), dst_ref=dst(k), send_sem=self.sems[0](k), recv_sem=self.sems[1](k),
            device_id=self.place.device(self.axis, k), device_id_type=MESH)

    def peers(self):
        return range(1, self.place.size(self.axis))

    def each(self, sender, act):
        for k in self.peers():
            if self.has is None:
                act(k)
            else:
                pl.when(self.has(sender(k)))(lambda k=k: act(k))

    def start(self):
        self.each(lambda k: self.place.at(self.axis), lambda k: self.make(k, self.src, self.dst).start())

    def arrive(self):
        self.each(lambda k: self.place.back(self.axis, k), lambda k: self.make(k, self.came, self.came).wait_recv())

    def done(self):
        self.each(lambda k: self.place.at(self.axis), lambda k: self.make(k, self.src, self.dst).wait_send())


def when(cond, body):
    if isinstance(cond, (bool, np.bool_)):
        if cond:
            body()
    else:
        pl.when(cond)(body)


def both(*conds):
    out = True
    for c in conds:
        if isinstance(c, (bool, np.bool_)):
            if not c:
                return False
        else:
            out = c if out is True else jnp.logical_and(out, c)
    return out


def call(kernel, outs, scratch, ins, name):
    return pl.pallas_call(
        kernel, out_shape=[jax.ShapeDtypeStruct(s, d) for s, d in outs], in_specs=[VM] * len(ins),
        out_specs=[VM] * len(outs), scratch_shapes=scratch, name=name,
        compiler_params=pltpu.CompilerParams(vmem_limit_bytes=VMEM_LIMIT))(*ins)


HALF = 4 * D
TM_HALF = 2 * D
FF_HALF = FF // 2
FF_PART = FF // 4


class Gather:
    def __init__(self, place, w, half, base, n_w, r, part, send, recv):
        self.place = place
        self.w, self.half, self.base, self.n_w, self.r, self.part = w, half, base, n_w, r, part
        self.send, self.recv = send, recv
        self.n = n_w + 3

    def block(self, wide, p, c):
        if wide:
            return (every, lanes(c * self.half + self.base + p * 256, 256))
        return (every, lanes(c * (D // 2) + p * 128, 128))

    def swap(self, wide, p, odd, s):
        pc = self.place
        ref = self.w if wide else self.r
        q = p if wide else self.n_w + p
        sems = (lambda k: self.send.at[q, s, k - 1], lambda k: self.recv.at[q, s, k - 1])
        blk = self.block(wide, p, pc.c)
        zs = every if wide else pl.ds(self.part * (pc.nz // 2), pc.nz // 2)
        at = lambda zz, yy, xx, b=blk: ref.at[(zz, yy, xx) + b]
        z, y, x = pc.z, pc.y, pc.x
        if s == 0:
            has = None if wide else (lambda zz: (zz >= pc.nz // 2) == (self.part == 1))
            own = lambda k: at(z, y, x)
            return Swap(pc, "z", sems, own, own, lambda k: at(pc.back("z", k), y, x), has)
        if s == 3:
            mine = lambda k: at(zs, every, every)
            return Swap(pc, "c", sems, mine, mine, lambda k: at(zs, every, every, self.block(wide, p, 1 - pc.c)))
        first = "y" if odd else "x"
        if s == 1:
            own = lambda k: at(zs, y, x)
            if first == "x":
                return Swap(pc, "x", sems, own, own, lambda k: at(zs, y, pc.back("x", k)))
            return Swap(pc, "y", sems, own, own, lambda k: at(zs, pc.back("y", k), x))
        if first == "x":
            own = lambda k: at(zs, y, every)
            return Swap(pc, "y", sems, own, own, lambda k: at(zs, pc.back("y", k), every))
        own = lambda k: at(zs, every, x)
        return Swap(pc, "x", sems, own, own, lambda k: at(zs, every, pc.back("x", k)))

    def on_piece(self, p, body):
        when(both(p >= 0, p < self.n_w), lambda: body(True, p))
        when(both(p >= self.n_w, p < self.n), lambda: body(False, p - self.n_w))

    def tick(self, u, odd, landed=None):
        def last(wide, p):
            self.swap(wide, p, odd, 3).arrive()
            if landed is not None:
                landed(wide, p)

        def step(s):
            def body(wide, p):
                if s:
                    self.swap(wide, p, odd, s - 1).arrive()
                self.swap(wide, p, odd, s).start()
            return body

        self.on_piece(u - 8, last)
        for s in (3, 2, 1, 0):
            self.on_piece(u - 2 * s, step(s))

    def finish(self):
        for q in range(self.n):
            for s in range(4):
                self.swap(q < self.n_w, q if q < self.n_w else q - self.n_w, q % 2 == 1, s).done()


def small_swap(pc, sb, send, recv, s):
    sems = (lambda k: send.at[s, k - 1], lambda k: recv.at[s, k - 1])
    at = lambda zz, yy, xx, c=pc.c: sb.at[zz, yy, xx, c]
    z, y, x = pc.z, pc.y, pc.x
    own = [lambda k: at(z, y, x), lambda k: at(every, y, x), lambda k: at(every, y, every),
           lambda k: at(every, every, every)][s]
    came = [lambda k: at(pc.back("z", k), y, x), lambda k: at(every, y, pc.back("x", k)),
            lambda k: at(every, pc.back("y", k), every), lambda k: at(every, every, every, 1 - pc.c)][s]
    return Swap(pc, "zxyc"[s], sems, own, own, came)


def place_small(sb, sv, eb, n_small, n_wide):
    nz, ny, nx = sb.shape[:3]
    for out, row0, width, total in ((sv, 0, n_small, D), (eb, 8, n_wide, FF)):
        tiles = [jnp.zeros((8, 128), F32) for _ in range(total // 128)]
        lane = lane_iota((8, 128))
        n = 0
        for q in range(nz * ny * nx):
            for c in range(2):
                blk = sb[q // (ny * nx), (q // nx) % ny, q % nx, c, row0:row0 + 8, :]
                tile, off = divmod(n * width, 128)
                moved = pltpu.roll(blk, off, axis=1) if off else blk
                end = off + width
                tiles[tile] = jnp.where((lane >= off) & (lane < min(end, 128)), moved, tiles[tile])
                if end > 128:
                    tiles[tile + 1] = jnp.where(lane < end - 128, moved, tiles[tile + 1])
                n += 1
        out[...] = jnp.concatenate(tiles, axis=1)


def group_cols(g):
    return (((0, g * 384, 256),), ((0, g * 384 + 256, 128), (1, g * 384, 128)), ((1, g * 384 + 128, 256),))


MERGE_COLS = (((0, 1152, 256),), ((0, 1408, 128), (1, 1152, 128)), ((1, 1280, 256),))


def columns(ref, parts, half):
    take = [ref[:, lanes(h * half + lo, n)] for h, lo, n in parts]
    return take[0] if len(take) == 1 else jnp.concatenate(take, axis=1)


class Flat:
    def __init__(self, ref):
        self.ref = ref

    def __getitem__(self, idx):
        v = self.ref[:, :, :, :, idx[1]]
        return v.reshape(-1, v.shape[-1])


def own_halves(h):
    for g in range(GROUPS):
        yield 0, g * GW + h * 2 * D, g * 384 + h * 128, 256
        yield 0, D + g * GW + h * 128, g * 384 + 256 * (1 - h), 128
    yield 1, h * (D // 2), 1152, D // 2
    for s in range(2):
        yield 2, s * FF_HALF + h * FF_PART, TM_HALF + s * FF_PART, FF_PART
    yield 3, h * (D // 2), 0, D // 2


def forward_kernel(near, dims, counts, x, raster, labk, labq, target, table, *rest):
    n_in = 13 if near else 4
    given = rest[:n_in]
    (o_w, o_r, o_triple, o_pt, o_att, o_mixed, o_n2, o_normed, o_xp, sv, eb, o_ew, o_er,
     w, r, sb, stage_w, stage_r, xp, normed, triple, attended, mixed, n2, pt, t4, bias, rowbuf, qs, st, lk,
     send, recv, ssend, srecv, lsem, psem) = rest[n_in:]

    def keep(n, src, dst):
        return pltpu.make_async_copy(src, dst, lsem.at[n])

    if near:
        pc = Place(dims)
        gather = Gather(pc, w, HALF, 0, 9, r, 0, send, recv)

    def part_of(wide, p):
        zs = every if wide else pl.ds(0, dims[0] // 2)
        for c in range(2):
            n = 2 * (p if wide else 9 + p) + c
            blk = (zs, every, every) + gather.block(wide, p, c)
            yield (keep(n, w.at[blk], o_w.at[blk]) if wide else keep(n, r.at[blk], o_r.at[blk]))

    def landed(wide, p):
        for copy in part_of(wide, p):
            copy.start()

    def tick(u):
        if near:
            gather.tick(u, u % 2 == 1, landed)
            if u in (0, 2, 4, 6, 8):
                if u:
                    small_swap(pc, sb, ssend, srecv, u // 2 - 1).arrive()
                if u < 8:
                    small_swap(pc, sb, ssend, srecv, u // 2).start()

    if near:
        pc.greet()
        own, vectors = given[:4], given[4:]
        first = []
        for i, ((n, src, dst, width), (_, _, back, _)) in enumerate(zip(own_halves(1 - pc.c), own_halves(pc.c))):
            ref, stage = own[n], (stage_r if n == 3 else stage_w)
            rows = lambda c, m=ref.shape[0]: pl.ds(aligned(c * m, 8), m)
            sems = (lambda k, i=i: ssend.at[4 + i, 0], lambda k, i=i: srecv.at[4 + i, 0])
            first.append(Swap(pc, "c", sems, lambda k, v=ref.at[:, lanes(src, width)]: v,
                              lambda k, v=stage.at[rows(pc.c), lanes(dst, width)]: v,
                              lambda k, v=stage.at[rows(1 - pc.c), lanes(back, width)]: v))
        for s in first:
            s.start()
        sb[pc.z, pc.y, pc.x, pc.c] = jnp.zeros((16, 128), F32)
        for k, v in enumerate(vectors):
            sb[pc.z, pc.y, pc.x, pc.c, k, 0:v.shape[0]] = v[...].astype(BF16).astype(F32)
        for n, src, dst, width in own_halves(pc.c):
            ref, stage = own[n], (stage_r if n == 3 else stage_w)
            stage[pl.ds(aligned(pc.c * ref.shape[0], 8), ref.shape[0]), lanes(dst, width)] = ref[:, lanes(src, width)]
        for s in first[:-1]:
            s.arrive()
        w[pc.z, pc.y, pc.x, :, lanes(pc.c * HALF, HALF)] = stage_w[...].astype(BF16)
        tick(0)
        tick(1)
        first[-1].arrive()
        r[pc.z, pc.y, pc.x, :, lanes(pc.c * (D // 2), D // 2)] = stage_r[...].astype(BF16)
        o_ew[...] = stage_w[:, TM_HALF + FF_PART:HALF].astype(BF16)
        o_er[...] = stage_r[...].astype(BF16)
    else:
        wown, rown, sv_in, eb_in = given
        loads = [keep(0, wown, w), keep(1, rown, r)]
        for c in loads:
            c.start()
        for c in loads:
            c.wait()
        sv[...] = sv_in[...]
        eb[...] = eb_in[...]

    def permute(i, _):
        xp[window(i), :] = dot(to_window(raster, i % 4), x[i // 4]).astype(BF16)
        return 0

    def spread(g, _):
        spread_bias(g, t4, bias, rowbuf)
        return 0

    table_rows(table, target, t4)
    for u in range(2, 10):
        tick(u)
        if u < 5:
            lax.fori_loop(u - 2, u - 1, spread, 0)
        elif u < 9:
            lax.fori_loop(2 * (u - 5), 2 * (u - 4), permute, 0)
    if near:
        place_small(sb, sv, eb, given[0].shape[0], given[3].shape[0])

    def ln1(i, _):
        hat, _i = stats(xp[window(i), :].astype(F32))
        normed[window(i), :] = (hat * sv[0:1, :] + sv[1:2, :]).astype(BF16)
        return 0

    lax.fori_loop(0, 8, ln1, 0)
    keep(24, xp, o_xp).start()
    keep(25, normed, o_normed).start()
    wf = Flat(w)

    def attn(t, i, g):
        b, v = i // 4, i % 4
        rows = window(i)
        col = lambda k: lanes(g * D + k * GW, GW)
        valid = raster[v] < counts[b]
        lk[...] = jnp.where(valid, labk[v], -1)
        head_stack(qs, triple[rows, col(0)])
        st[...] = dot(triple[rows, col(1)], qs[...], NT)
        slot = t % 2
        for n in range(9):
            c = lanes(n * 128, 128)
            s = st[:, c] + bias[g * 9 + n]
            s = jnp.where(lk[...] == labq[v, 0:1, c], s, MASKED)
            m = jnp.max(s, axis=0, keepdims=True)
            e = jnp.exp((s - m) * SCALE)
            tot = jnp.sum(e, axis=0, keepdims=True)
            pt[slot, :, c] = (e * (1.0 / tot)).astype(BF16)
        pltpu.make_async_copy(pt.at[slot], o_pt.at[g * 8 + i], psem.at[slot]).start()
        out = head_pick(dot(pt[slot], triple[rows, col(2)], TN))
        vq = jnp.concatenate([valid, valid], axis=1)
        attended[rows, lanes(g * GW, GW)] = jnp.where(vq, out, 0.0).astype(BF16)

    def quarter(q, _):
        g = q // 4

        @pl.when(q % 4 == 0)
        def _():
            for k, parts in enumerate(group_cols(g)):
                v = dot(normed[...], columns(wf, parts, HALF))
                if k != 1:
                    v = v + sv[2 + k // 2:3 + k // 2, lanes(g * GW, GW)]
                triple[:, lanes(g * D + k * GW, GW)] = v.astype(BF16)

        def one(j, _):
            step = q * 2 + j

            @pl.when(step >= 2)
            def _():
                pltpu.make_async_copy(pt.at[step % 2], o_pt.at[0], psem.at[step % 2]).wait()

            attn(step, step % 8, g)
            return 0

        lax.fori_loop(0, 2, one, 0)
        if near:
            for odd in range(2):
                pl.when(q % 2 == odd)(lambda odd=odd: gather.tick(10 + q, odd == 1, landed))
        return 0

    lax.fori_loop(0, 4 * GROUPS, quarter, 0)
    keep(26, triple, o_triple).start()
    keep(27, attended, o_att).start()
    for n in range(3):
        cols = lanes(n * 256, 256)
        v = dot(attended[...], columns(wf, MERGE_COLS[n], HALF))
        mixed[:, cols] = xp[:, cols].astype(F32) + v + sv[4:5, cols]
    keep(28, mixed, o_mixed).start()

    def ln2(i, _):
        hat, _i = stats(mixed[window(i), :])
        n2[window(i), :] = (hat * sv[5:6, :] + sv[6:7, :]).astype(BF16)
        return 0

    lax.fori_loop(0, 8, ln2, 0)
    keep(29, n2, o_n2).start()
    if near:
        gather.finish()
        for s in first:
            s.done()
        for s in range(4):
            small_swap(pc, sb, ssend, srecv, s).done()
        for q in range(12):
            for copy in part_of(q < 9, q if q < 9 else q - 9):
                copy.wait()
    for n, src, dst in ((24, xp, o_xp), (25, normed, o_normed), (26, triple, o_triple), (27, attended, o_att),
                        (28, mixed, o_mixed), (29, n2, o_n2)):
        keep(n, src, dst).wait()
    for slot in range(2):
        pltpu.make_async_copy(pt.at[slot], o_pt.at[0], psem.at[slot]).wait()


def forward(near, dims, counts, x, table, *given):
    nz, ny, nx = dims if near else (1, 1, 1)
    rw, rr = (given[0].shape[0] * 2, given[3].shape[0] * 2) if near else (D, FF)
    peers = max(nz, ny, nx, 2) - 1
    full_w, full_r = (nz, ny, nx, rw, 2 * HALF), (nz, ny, nx, rr, D)
    tiny = (8, 128)
    outs = [(full_w if near else tiny, BF16), (full_r if near else tiny, BF16), ((ROWS, 3 * D), BF16),
            ((8 * GROUPS, WT, QL), BF16), ((ROWS, D), BF16), ((ROWS, D), F32), ((ROWS, D), BF16), ((ROWS, D), BF16),
            ((ROWS, D), BF16), ((8, D), F32), ((8, FF), F32), ((rw, FF_PART) if near else tiny, BF16),
            ((rr, D // 2) if near else tiny, BF16)]
    if not near:
        given = (given[0].reshape(full_w), given[1].reshape(full_r)) + given[2:]
    vm = pltpu.VMEM
    dma = pltpu.SemaphoreType.DMA
    scratch = [vm(full_w, BF16), vm(full_r, BF16), vm((nz, ny, nx, 2, 16, 128), F32), vm((rw if near else 8, HALF), F32),
               vm((rr if near else 8, D // 2), F32), vm((ROWS, D), BF16), vm((ROWS, D), BF16), vm((ROWS, 3 * D), BF16),
               vm((ROWS, D), BF16), vm((ROWS, D), F32), vm((ROWS, D), BF16), vm((2, WT, QL), BF16),
               vm((HEADS, 4 * WT), F32), vm((GROUPS * 9, WT, 128), F32), vm((2, 16, QL), F32), vm((QL, GW), BF16),
               vm((WT, QL), F32), vm((WT, 128), jnp.int32),
               dma((12, 4, peers)), dma((12, 4, peers)), dma((14, peers)), dma((14, peers)), dma((30,)), dma((2,))]
    params = dict(collective_id=0, has_side_effects=True) if near else {}
    return pl.pallas_call(
        functools.partial(forward_kernel, near, dims),
        out_shape=[jax.ShapeDtypeStruct(s, d) for s, d in outs],
        in_specs=[SM] + [VM] * 6 + ([VM] * 13 if near else [ANY, ANY, VM, VM]),
        out_specs=[ANY] * 9 + [VM] * 4,
        scratch_shapes=scratch, name="forward",
        compiler_params=pltpu.CompilerParams(vmem_limit_bytes=VMEM_LIMIT, **params),
    )(counts, x, jnp.asarray(RASTER_L), jnp.asarray(LABEL_L), jnp.asarray(LABEL_Q), jnp.asarray(TARGET), table,
      *given)


class Scatter:
    def __init__(self, place, bufs, send, recv):
        self.place = place
        self.bufs, self.send, self.recv = bufs, send, recv

    def src(self, kind, g, i, ab, c):
        if kind == "r":
            n = g.shape[3] // 2
            return g.at[every, every, every, pl.ds(ab * n, n), lanes(c * (D // 2) + i * 128, 128)]
        return g.at[every, every, every, every, lanes(c * FF_HALF + i * 256 + ab * 128, 128)]

    def swap(self, kind, g, out, i, ab, s):
        pc = self.place
        r0, r1, r2, r3, fin = self.bufs[kind]
        q = {"e": 0, "t": 6, "r": 12}[kind] + i
        sems = (lambda k: self.send.at[q, ab, s, k - 1], lambda k: self.recv.at[q, ab, s, k - 1])
        first, second = ("y", "x") if ab == 0 else ("x", "y")
        if s == 0:
            to = lambda k: r0.at[i, ab]
            return Swap(pc, "c", sems, lambda k: self.src(kind, g, i, ab, 1 - pc.c), to, to)
        if s == 1:
            to = lambda k: r1.at[i, ab, k - 1]
            at = lambda k: (every, pc.step("y", k), every) if first == "y" else (every, every, pc.step("x", k))
            return Swap(pc, first, sems, lambda k: r0.at[(i, ab) + at(k)], to, to)
        if s == 2:
            to = lambda k: r2.at[i, ab, k - 1]
            return Swap(pc, second, sems, lambda k: r1.at[i, ab, 0, every, pc.step(second, k)], to, to)
        if s == 3:
            to = lambda k: r3.at[i, ab, k - 1]
            return Swap(pc, "z", sems, lambda k: r2.at[i, ab, 0, pc.step("z", k)], to, to)
        n = out.shape[0]
        if kind == "r":
            cols = lambda c: lanes(c * (D // 2) + i * 128, 128)
            return Swap(pc, "c", sems, lambda k: fin.at[i, 1 - pc.c], lambda k: out.at[:, cols(pc.c)],
                        lambda k: out.at[:, cols(1 - pc.c)])
        cols = lambda c: lanes(c * FF_HALF + i * 256 + ab * 128, 128)
        return Swap(pc, "c", sems, lambda k: fin.at[i, ab, pl.ds(aligned((1 - pc.c) * n, 8), n), :],
                    lambda k: out.at[:, cols(pc.c)], lambda k: out.at[:, cols(1 - pc.c)])

    def advance(self, kind, g, out, i, s):
        pc = self.place
        r0, r1, r2, r3, fin = self.bufs[kind]
        if s == 5:
            for ab in range(1 if kind == "r" else 2):
                self.swap(kind, g, out, i, ab, 4).arrive()
            return
        for ab in range(2):
            first, second = ("y", "x") if ab == 0 else ("x", "y")
            if s:
                self.swap(kind, g, out, i, ab, s - 1).arrive()
            if s == 1:
                n = r0.shape[-2]

                def add(z, _):
                    if kind == "r":
                        own = g[z, :, :, ab * n:(ab + 1) * n, lanes(pc.c * (D // 2) + i * 128, 128)]
                    else:
                        own = g[z, :, :, :, lanes(pc.c * FF_HALF + i * 256 + ab * 128, 128)]
                    r0[i, ab, z] = (r0[i, ab, z].astype(F32) + own.astype(F32)).astype(BF16)
                    return 0

                lax.fori_loop(0, pc.nz, add, 0)
            if s == 2:
                at = (every, pc.y, every) if first == "y" else (every, every, pc.x)
                v = r0[(i, ab) + at].astype(F32)
                for k in range(pc.size(first) - 1):
                    v = v + r1[i, ab, k].astype(F32)
                r1[i, ab, 0] = v.astype(BF16)
            if s == 3:
                v = r1[i, ab, 0, :, pc.at(second)].astype(F32)
                for k in range(pc.size(second) - 1):
                    v = v + r2[i, ab, k].astype(F32)
                r2[i, ab, 0] = v.astype(BF16)
            if s == 4:
                v = r2[i, ab, 0, pc.z].astype(F32)
                for k in range(pc.nz - 1):
                    v = v + r3[i, ab, k].astype(F32)
                fin[i, ab] = v
                if kind != "r":
                    n = out.shape[0]
                    out[:, lanes(pc.c * FF_HALF + i * 256 + ab * 128, 128)] = fin[i, ab, pl.ds(aligned(pc.c * n, 8), n), :]
            if s < 4 or kind != "r":
                self.swap(kind, g, out, i, ab, s).start()
        if s == 4 and kind == "r":
            out[:, lanes(pc.c * (D // 2) + i * 128, 128)] = fin[i, pc.c]
            self.swap(kind, g, out, i, 0, 4).start()

    def done(self, kind, g, out, pieces, steps):
        for i in range(pieces):
            for s in steps:
                for ab in range(1 if (kind == "r" and s == 4) else 2):
                    self.swap(kind, g, out, i, ab, s).done()


class SmallSum:
    def __init__(self, place, slots, send, recv):
        self.place, self.slots, self.send, self.recv = place, slots, send, recv

    def base(self, i):
        return sum(self.place.size(a) for a in "cyxz"[:i])

    def swap(self, i):
        pc, a = self.place, "cyxz"[i]
        sems = (lambda k: self.send.at[i, k - 1], lambda k: self.recv.at[i, k - 1])
        me = lambda k: self.slots.at[self.base(i) + pc.at(a)]
        return Swap(pc, a, sems, me, me, lambda k: self.slots.at[self.base(i) + pc.back(a, k)])

    def start(self):
        self.swap(0).start()

    def advance(self, i):
        self.swap(i).arrive()
        s = self.slots[self.base(i)]
        for k in range(1, self.place.size("cyxz"[i])):
            s = s + self.slots[self.base(i) + k]
        if i == 3:
            return s
        self.slots[self.base(i + 1) + self.place.at("cyxz"[i + 1])] = s
        self.swap(i + 1).start()

    def done(self):
        for i in range(4):
            self.swap(i).done()


def events(t, loop=None):
    out = []
    for i in range(6):
        for s in range(6):
            if 2 * i + 1 + 2 * s == t and t >= 12:
                out.append(("e", i, s))
    for i, at in enumerate(((12, 15, 18, 20, 22, 24), (13, 16, 20, 22, 24, 26), (14, 18, 21, 23, 25, 27))):
        out += [("r", i, s) for s in range(6) if at[s] == t]
    out += [("t", 5, s) for s, at in enumerate((20, 22, 24, 26, 28, 29)) if at == t]
    return out


def backward_kernel(near, dims, counts, raster, rasq, do, w, r, own_ew, own_er, triple_h, pt_h, att_h, mixed_h, n2_h, normed_h,
                    xp_h, sv, eb, o_out, o_dx, o_t, o_e, o_r, o_small, o_deb, o_t4,
                    ew, rw, dop, dn2, mixed, part, e0, e1, e2, e3, ef, t0, t1, t2, t3, tf, b0, b1, b2, b3, bf, slots_a, slots_g, late, slots_l, sums_g, smalls,
                    gsend, grecv, send, recv, ssend, srecv, lsem):
    def load(n, src, dst):
        return pltpu.make_async_copy(src, dst, lsem.at[n])

    if near:
        pc = Place(dims)
        rs = Scatter(pc, {"e": (e0, e1, e2, e3, ef), "t": (t0, t1, t2, t3, tf), "r": (b0, b1, b2, b3, bf)}, send, recv)
        sum_a = SmallSum(pc, slots_a, ssend.at[0], srecv.at[0])
        sum_l = SmallSum(pc, slots_l, ssend.at[1], srecv.at[1])
        sum_g = lambda g: SmallSum(pc, slots_g.at[g], ssend.at[2 + g], srecv.at[2 + g])
        pc.greet()
    else:
        pc = None
    small = smalls
    small[...] = jnp.zeros(small.shape, F32)

    def feed_forward(n2, n2t, act, hs, ds, hl, de, dr):
        half_z = dims[0] // 2
        loads = [load(0, n2_h, n2), load(3, mixed_h, mixed)]
        if near:
            for c in range(2):
                a, b = lanes(c * HALF + TM_HALF, FF_PART), lanes(c * FF_HALF, FF_PART)
                loads.append(load(4 + c, w.at[:, :, :, :, a], ew.at[:, :, :, :, b]))
            loads.append(load(2, r.at[0:half_z], rw.at[0:half_z]))
        else:
            for c in range(2):
                a, b = lanes(c * HALF + TM_HALF, FF_HALF), lanes(c * FF_HALF, FF_HALF)
                loads.append(load(4 + c, w.at[:, :, :, :, a], ew.at[:, :, :, :, b]))
            loads.append(load(2, r, rw))
        for c in loads:
            c.start()
        if near:
            gather = Gather(pc, ew, FF_HALF, FF_PART, 3, rw, 1, gsend, grecv)
            ew[pc.z, pc.y, pc.x, :, lanes(pc.c * FF_HALF + FF_PART, FF_PART)] = own_ew[...]

            @pl.when(pc.z >= half_z)
            def _():
                rw[pc.z, pc.y, pc.x, :, lanes(pc.c * (D // 2), D // 2)] = own_er[...]

            gather.tick(0, False)
            gather.tick(1, True)

        def permute(i, _):
            dop[window(i), :] = dot(to_window(raster, i % 4), do[i // 4]).astype(BF16)
            return 0

        lax.fori_loop(0, 8, permute, 0)
        for c in loads:
            c.wait()
        n2t[...] = n2[...].T
        dn2[...] = jnp.zeros(dn2.shape, F32)
        small[7:8, :] = jnp.sum(dop[...].astype(F32), axis=0, keepdims=True)
        nz, ny, nx, rr = rw.shape[:4]
        per = FF // 256

        def rows_of(n0):
            return flat_r[pl.ds(aligned(n0, 256), 256), :]

        flat_r = rw.reshape(FF, D)
        fe, fde = Flat(ew), de

        def chunk(j, _):
            s, k = j // 6, j % 6
            c, off = k % 2, k // 2
            col = lanes(c * FF_HALF + s * FF_PART + off * 256, 256)
            n0 = s * FF_HALF + c * FF_PART + off * 256
            nat = lanes(n0, 256)
            weights = fe[:, col]
            rows = rows_of(n0)
            hs[...] = dot(n2[...], weights)
            ds[...] = dot(dop[...], rows, NT)
            bias = eb[0:1, nat]
            total = jnp.zeros((8, 256), F32)
            for m in range(18):
                rr_ = pl.ds(m * 64, 64)
                a, slope = gelu_pair(hs[rr_, :] + bias)
                act[rr_, nat] = a.astype(BF16)
                hg = ds[rr_, :] * slope
                for q in range(8):
                    total = total + hg[q * 8:(q + 1) * 8]
                hl[rr_, :] = hg.astype(BF16)
            small[pl.ds(8 + s * 2 + c, 1), lanes(off * 256, 256)] = jnp.sum(total, axis=0, keepdims=True)
            de[:, :, :, :, col] = dot(n2t[...], hl[...]).astype(BF16).reshape(de.shape[:4] + (256,))
            for n in range(3):
                cc = lanes(n * 256, 256)
                dn2[:, cc] += dot(hl[...], weights[n * 256:(n + 1) * 256], NT)
            if near:
                gather.tick(2 + 2 * j, False)
                gather.tick(3 + 2 * j, True)
                for step in range(5, -1, -1):
                    i = j // 2 - step
                    pl.when(jnp.logical_and(lax.rem(j, 2) == 1, i >= 0))(
                        lambda i=i, step=step: rs.advance("e", de, o_e, i, step))
            return 0

        lax.fori_loop(0, per, chunk, 0)

        def er_tick(t):
            for kind, i, s in events(t):
                rs.advance(kind, de if kind == "e" else dr, o_e if kind == "e" else o_r, i, s)

        for n in range(3):
            two = jnp.concatenate([dop[:, n * 128:(n + 1) * 128], dop[:, D // 2 + n * 128:D // 2 + (n + 1) * 128]], axis=1)
            for m in range(4):
                v = dot(act[:, m * D:(m + 1) * D], two, TN).astype(BF16)
                zz = pl.ds(m * nz // 4, nz // 4) if nz >= 4 else every
                rows = pl.ds(0, rr) if nz >= 4 else pl.ds(m * D, D)
                v = v.reshape((max(nz // 4, 1), ny, nx, rr if nz >= 4 else D, 256))
                dr[zz, :, :, rows, n * 128:(n + 1) * 128] = v[..., :128]
                dr[zz, :, :, rows, D // 2 + n * 128:D // 2 + (n + 1) * 128] = v[..., 128:]
            if near:
                er_tick(12 + n)
        for n in range(3):
            c = lanes(n * 256, 256)
            part[:, c] = (mixed[:, c] + dot(act[...], flat_r[:, c]) + sv[7:8, c]).astype(BF16)
            if near:
                er_tick(15 + n)
        for b in range(2):
            for m in range(4):
                n2[b * TOK + m * WT:b * TOK + (m + 1) * WT, :] = dot(
                    to_raster(rasq, m), part[b * TOK:(b + 1) * TOK, :]).astype(BF16)
        save = [load(b, n2.at[b * TOK:(b + 1) * TOK, :], o_out.at[b]) for b in range(2)]
        for c in save:
            c.start()
        if near:
            er_tick(18)
            gather.finish()
            rs.done("e", de, o_e, 6, range(1))
            rs.done("r", dr, o_r, 3, range(1))
        else:
            for c in (load(4, de, o_e), load(5, dr, o_r)):
                c.start()
                c.wait()
        for c in save:
            c.wait()

    nz, ny, nx, rw_rows = w.shape[:4]
    rr_rows = r.shape[3]
    vm = pltpu.VMEM
    pl.run_scoped(feed_forward, vm((ROWS, D), BF16),
                  vm((D, ROWS), BF16), vm((ROWS, FF), BF16), vm((ROWS, 256), F32), vm((ROWS, 256), F32), vm((ROWS, 256), BF16),
                  vm((nz, ny, nx, rw_rows, FF), BF16), vm((nz, ny, nx, rr_rows, D), BF16))

    tw = ew

    def attention(dt, triple, ml, datt, xt, xn, xp, qs, dos, st, raw, pt, bgrad, accbuf, t4g, sum_keep, psem):
        loads = [load(0, att_h, xn), load(1, triple_h, triple), load(2, xp_h, xp)]
        loads += [load(4 + c, w.at[:, :, :, :, lanes(c * HALF, TM_HALF)], tw.at[:, :, :, :, lanes(c * TM_HALF, TM_HALF)])
                  for c in range(2)]
        for c in loads:
            c.start()

        def fetch(step):
            return pltpu.make_async_copy(pt_h.at[(2 - step // 8) * 8 + step % 8], pt.at[step % 2], psem.at[step % 2])

        fetch(0).start()

        def ert_tick(t):
            if near:
                for kind, i, s in events(t):
                    rs.advance(kind, {"e": None, "r": None, "t": dt}[kind], {"e": o_e, "r": o_r, "t": o_t}[kind], i, s)

        def ln2b(i, _):
            rows = window(i)
            hat, inv = stats(mixed[rows, :])
            g = dn2[rows, :]
            small[5:6, :] += jnp.sum(g * hat, axis=0, keepdims=True)
            small[6:7, :] += jnp.sum(g, axis=0, keepdims=True)
            m = dop[rows, :].astype(F32) + norm_back(hat, inv, sv[5:6, :], g)
            small[4:5, :] += jnp.sum(m, axis=0, keepdims=True)
            mixed[rows, :] = m
            ml[rows, :] = m.astype(BF16)
            return 0

        lax.fori_loop(0, 8, ln2b, 0)
        ert_tick(19)
        for c in loads:
            c.wait()
        tf_ = Flat(tw)

        def put(parts, v):
            at = 0
            for h, lo, n in parts:
                dt[:, :, :, :, lanes(h * TM_HALF + lo, n)] = v[:, at:at + n].reshape(dt.shape[:4] + (n,))
                at += n

        xt[...] = xn[...].T
        for n in range(3):
            c = lanes(n * 256, 256)
            put(MERGE_COLS[n], dot(xt[...], ml[:, c]).astype(BF16))
        merge = jnp.concatenate([tw[:, :, :, :, lanes(1152, 384)], tw[:, :, :, :, lanes(TM_HALF + 1152, 384)]], axis=-1)
        merge = merge.reshape(D, D)
        for n in range(3):
            datt[:, n * 256:(n + 1) * 256] = dot(ml[...], merge[n * 256:(n + 1) * 256], NT).astype(BF16)
        ert_tick(20)
        if near:
            slots_a[pc.c, 0:4, :] = small[4:8, :]
            slots_a[pc.c, 4:8, :] = small[8:12, :]
            sum_a.start()
        again = load(0, normed_h, xn)
        again.start()
        again.wait()
        xt[...] = xn[...].T

        def t_tick(t):
            for s in range(5, -1, -1):
                q = t - 22 - s
                if isinstance(t, int):
                    if q % 2 == 0 and 0 <= q // 2 <= 2:
                        k = q // 2
                        for i in range(3 - k - k // 2, 5 - 2 * k + k // 2):
                            rs.advance("t", dt, o_t, i, s)
                else:
                    k = q // 2

                    def run(k=k, s=s):
                        lax.fori_loop(3 - k - k // 2, 5 - 2 * k + k // 2,
                                      lambda i, _: (rs.advance("t", dt, o_t, i, s), 0)[1], 0)

                    pl.when(jnp.logical_and(q >= 0, lax.rem(q + 20, 2) == 0))(run)

        def one(step, g):
            i = step % 8
            b, v = i // 4, i % 4
            rows = window(i)
            col = lambda k: lanes(g * D + k * GW, GW)
            slot = step % 2

            @pl.when(step < 23)
            def _():
                fetch(step + 1).start()

            valid = raster[v] < counts[b]
            vq = jnp.concatenate([valid, valid], axis=1)
            da = datt[rows, lanes(g * GW, GW)]
            da = jnp.where(vq, da.astype(F32), 0.0).astype(BF16)
            head_stack(qs, triple[rows, col(0)])
            head_stack(dos, da)
            st[...] = dot(triple[rows, col(2)], dos[...], NT)
            fetch(step).wait()
            for n in range(9):
                c = lanes(n * 128, 128)
                p = pt[slot, :, c].astype(F32)
                d = st[:, c]
                inner = jnp.sum(p * d, axis=0, keepdims=True)
                s = p * (d - inner)
                bgrad[n] += s
                raw[:, c] = (s * SCALE).astype(BF16)
            key = triple[rows, col(1)]
            triple[rows, col(2)] = dot(pt[slot], dos[...]).astype(BF16)
            triple[rows, col(1)] = dot(raw[...], qs[...]).astype(BF16)
            triple[rows, col(0)] = head_pick(dot(raw[...], key, TN)).astype(BF16)

        def half_group(q, _):
            g = 2 - q // 2

            @pl.when(q % 2 == 0)
            def _():
                bgrad[...] = jnp.zeros(bgrad.shape, F32)

            lax.fori_loop(0, 4, lambda j, _: (one(q * 4 + j, g), 0)[1], 0)

            @pl.when(q % 2 == 1)
            def _():
                gather_bias(g, bgrad, accbuf, t4g)
                for k, parts in enumerate(group_cols(g)):
                    v = triple[:, lanes(g * D + k * GW, GW)]
                    if k != 1:
                        small[2 + k // 2:3 + k // 2, lanes(g * GW, GW)] = jnp.sum(v.astype(F32), axis=0, keepdims=True)
                    put(parts, dot(xt[...], v).astype(BF16))

            if near:
                for t in range(21, 27):
                    if events(t):
                        pl.when(q == t - 21)(lambda t=t: ert_tick(t))
                t_tick(21 + q)
                for m in range(4):
                    k = (q - 2 - m) // 2

                    def more(k=k, m=m):
                        total = sum_g(2 - k).advance(m)
                        if total is not None:
                            sums_g[2 - k] = total

                    pl.when(jnp.logical_and(q - 2 - m >= 0, lax.rem(q + 10 - m, 2) == 0))(more)
                for m, at in enumerate((0, 2, 4)):
                    pl.when(q == at)(lambda m=m: sum_a.advance(m) and None)

                @pl.when(q % 2 == 1)
                def _():
                    own = slots_g.at[g, pc.c]
                    own[...] = jnp.zeros(own.shape, F32)
                    own[0:8, 0:4 * WT] = t4g[pl.ds(aligned(g * GH, GH), GH), :]
                    for k in range(2):
                        own[8 + k:9 + k, 0:GW] = small[2 + k:3 + k, lanes(g * GW, GW)]
                    sum_g(g).start()
            return 0

        lax.fori_loop(0, 2 * GROUPS, half_group, 0)
        def group_sum(g, m):
            total = sum_g(g).advance(m)
            if total is not None:
                sums_g[g] = total

        for n in range(3):
            rows = [tw[:, :, :, :, lanes(h * TM_HALF + lo, m)].reshape(D, m)[n * 256:(n + 1) * 256]
                    for g in range(GROUPS) for p in group_cols(g) for h, lo, m in p]
            dn2[:, n * 256:(n + 1) * 256] = dot(triple[...], jnp.concatenate(rows, axis=1), NT)
            if near and n < 2:
                ert_tick(27 + n)
                t_tick(27 + n)
                group_sum(0, n)
                group_sum(1, n + 2)
        if near:
            total_a = sum_a.advance(3)
            sum_keep[...] = total_a

        def ln1b(i, _):
            rows = window(i)
            hat, inv = stats(xp[rows, :].astype(F32))
            g = dn2[rows, :]
            late[0:1, :] += jnp.sum(g * hat, axis=0, keepdims=True)
            late[1:2, :] += jnp.sum(g, axis=0, keepdims=True)
            ml[rows, :] = (mixed[rows, :] + norm_back(hat, inv, sv[0:1, :], g)).astype(BF16)
            return 0

        late[...] = jnp.zeros(late.shape, F32)
        lax.fori_loop(0, 8, ln1b, 0)
        if near:
            slots_l[pc.c] = late[0:2, :]
            sum_l.start()
            ert_tick(29)
            t_tick(29)
            group_sum(0, 2)
        for b in range(2):
            for m in range(4):
                part[b * TOK + m * WT:b * TOK + (m + 1) * WT, :] = dot(
                    to_raster(rasq, m), ml[b * TOK:(b + 1) * TOK, :]).astype(BF16)
            load(b, part.at[b * TOK:(b + 1) * TOK, :], o_dx.at[b]).start()
            if near:
                sum_l.advance(b)
                if b == 0:
                    t_tick(30)
        if near:
            group_sum(0, 3)
            sum_l.advance(2)
            t_tick(31)
            total_l = sum_l.advance(3)
            dev = pc.z * (2 * pc.ny * pc.nx) + (pc.y * pc.nx + pc.x) * 2 + pc.c
            n = o_small.shape[1]
            shift = lax.rem(D - dev * n, D)
            biases = [jnp.concatenate([sums_g[g, 8 + k:9 + k, 0:GW] for g in range(GROUPS)], axis=1) for k in range(2)]
            rows = jnp.concatenate([total_l] + biases + [sum_keep[0:4, :]], axis=0)
            o_small[...] = pltpu.roll(rows, shift, axis=1)[:, 0:n]
            wide_n = o_deb.shape[1]
            per = D // wide_n
            row = sum_keep[pl.ds(4 + dev // per, 1), :]
            o_deb[...] = pltpu.roll(row, lax.rem(D - lax.rem(dev, per) * wide_n, D), axis=1)[:, 0:wide_n]
            for g in range(GROUPS):
                o_t4[g * GH:(g + 1) * GH, :] = sums_g[g, 0:8, 0:4 * WT]
            rs.done("e", None, o_e, 6, range(1, 5))
            rs.done("r", None, o_r, 3, range(1, 5))
            rs.done("t", dt, o_t, 6, range(5))
            sum_a.done()
            sum_l.done()
            for g in range(GROUPS):
                sum_g(g).done()
        else:
            o_small[0:2, :] = late[0:2]
            o_small[2:8, :] = small[2:8, :]
            for k in range(4):
                o_deb[0:1, k * D:(k + 1) * D] = small[8 + k:9 + k, :]
            o_t4[...] = t4g[...]
            save = load(4, dt, o_t)
            save.start()
            save.wait()
        for b in range(2):
            load(b, part.at[b * TOK:(b + 1) * TOK, :], o_dx.at[b]).wait()

    pl.run_scoped(attention, vm((nz, ny, nx, rw_rows, 2 * TM_HALF), BF16),
                  vm((ROWS, 3 * D), BF16), vm((ROWS, D), BF16), vm((ROWS, D), BF16), vm((D, ROWS), BF16), vm((ROWS, D), BF16),
                  vm((ROWS, D), BF16), vm((QL, GW), BF16), vm((QL, GW), BF16), vm((WT, QL), F32), vm((WT, QL), BF16),
                  vm((2, WT, QL), BF16), vm((9, WT, 128), F32), vm((2, 16, QL), F32),
                  vm((HEADS, 4 * WT), F32), vm((8, D), F32), pltpu.SemaphoreType.DMA((2,)))


def backward(near, dims, counts, do, w, r, own_ew, own_er, triple, pt, att, mixed, n2, normed, xp, sv, eb):
    nz, ny, nx = dims if near else (1, 1, 1)
    if not near:
        w, r = w.reshape(1, 1, 1, D, -1), r.reshape(1, 1, 1, FF, D)
    rw, rr = w.shape[3], r.shape[3]
    peers = max(nz, ny, nx, 2) - 1
    vm = pltpu.VMEM
    dma = pltpu.SemaphoreType.DMA
    bufs = []
    for count, n in ((6, rw), (6, rw), (3, rr // 2)) if near else ((1, 16),) * 3:
        bufs += [vm((count, 2, nz, ny, nx, n, 128), BF16), vm((count, 2, max(ny - 1, 1), nz, nx, n, 128), BF16),
                 vm((count, 2, max(nx - 1, 1), nz, n, 128), BF16), vm((count, 2, max(nz - 1, 1), n, 128), BF16),
                 vm((count, 2, n, 128), F32)]
    n_slots = 2 + nz + ny + nx
    if near:
        outs = [((rw // 2, 2 * TM_HALF), F32), ((rw // 2, FF), F32), ((rr // 2, D), F32), ((8, rw // 2), F32), ((1, rr // 2), F32)]
    else:
        outs = [((1, 1, 1, D, 2 * TM_HALF), BF16), ((1, 1, 1, D, FF), BF16), ((1, 1, 1, FF, D), BF16), ((8, D), F32), ((1, FF), F32)]
    outs = [((2, TOK, D), BF16), ((2, TOK, D), BF16)] + outs + [((HEADS, 4 * WT), F32)]
    params = dict(collective_id=1, has_side_effects=True) if near else {}
    return pl.pallas_call(
        functools.partial(backward_kernel, near, dims),
        out_shape=[jax.ShapeDtypeStruct(s, d) for s, d in outs],
        in_specs=[SM, VM, VM, VM, ANY, ANY, VM, VM] + [ANY] * 7 + [VM] * 2,
        out_specs=[ANY] * 2 + ([VM] * 3 if near else [ANY] * 3) + [VM] * 3,
        scratch_shapes=[vm((nz, ny, nx, rw, FF), BF16), vm((nz, ny, nx, rr, D), BF16), vm((ROWS, D), BF16), vm((ROWS, D), F32),
                        vm((ROWS, D), F32), vm((ROWS, D), BF16)] + bufs
        + [vm((n_slots, 8, D), F32), vm((GROUPS, n_slots, 16, 640), F32), vm((8, D), F32), vm((n_slots, 2, D), F32),
           vm((GROUPS, 16, 640), F32), vm((16, D), F32),
           dma((6, 4, peers)), dma((6, 4, peers)), dma((15, 2, 5, peers)), dma((15, 2, 5, peers)), dma((5, 4, peers)),
           dma((5, 4, peers)), dma((6,))],
        name="backward",
        compiler_params=pltpu.CompilerParams(vmem_limit_bytes=VMEM_LIMIT, **params),
    )(counts, jnp.asarray(RASTER_L), jnp.asarray(RASTER_Q), do, w, r, own_ew, own_er, triple, pt, att, mixed, n2, normed, xp, sv,
      eb)


def finish_kernel(near, target, t, e, r, small, deb, t4, triple, merge, expand, reduce, table, *vectors):
    if near:
        for g in range(GROUPS):
            for k, parts in enumerate(group_cols(g)):
                at = k * D + g * GW
                for h, lo, n in parts:
                    triple[:, at:at + n] = t[:, h * TM_HALF + lo:h * TM_HALF + lo + n]
                    at += n
        for c in range(2):
            merge[:, c * D // 2:(c + 1) * D // 2] = t[:, c * TM_HALF + 1152:(c + 1) * TM_HALF]
            for s in range(2):
                expand[:, s * FF_HALF + c * FF_PART:s * FF_HALF + (c + 1) * FF_PART] = (
                    e[:, c * FF_HALF + s * FF_PART:c * FF_HALF + (s + 1) * FF_PART])
        reduce[...] = r[...]
    for k, v in enumerate(vectors[:8]):
        v[...] = small[k, :]
    vectors[8][...] = deb[0, :]
    table[...] = lax.dot_general(onehot(target), t4[...], NT, precision=lax.Precision.HIGHEST,
                                 preferred_element_type=F32)


def weights_in_pieces(triple_weight, merge_weight, expand_weight):
    halves = []
    for c in range(2):
        for g in range(GROUPS):
            q, k, v = (triple_weight[:, i * D + g * GW:i * D + (g + 1) * GW] for i in range(3))
            halves += [q, k[:, :128]] if c == 0 else [k[:, 128:], v]
        halves.append(merge_weight[:, c * D // 2:(c + 1) * D // 2])
        halves += [expand_weight[:, s * FF_HALF + c * FF_PART:s * FF_HALF + (c + 1) * FF_PART] for s in range(2)]
    return jnp.concatenate(halves, axis=1)


def shards(dims, block_input, valid_counts, output_cotangent, triple_weight, merge_weight, expand_weight, reduce_weight,
           first_gain, first_shift, query_bias, value_bias, merge_bias, second_gain, second_shift, expand_bias,
           reduce_bias, position_table):
    counts = valid_counts[:, 0]
    rows = triple_weight.shape[0]
    near = rows % 8 == 0 and dims[0] % 4 == 0 and dims[1] == dims[2]
    if near:
        given = (triple_weight, merge_weight, expand_weight, reduce_weight, first_gain, first_shift, query_bias, value_bias,
                 merge_bias, second_gain, second_shift, reduce_bias, expand_bias)
    else:
        small = jnp.stack([first_gain, first_shift, query_bias, value_bias, merge_bias, second_gain, second_shift,
                           reduce_bias])
        gather = lambda v, axis: lax.all_gather(v.astype(BF16), AXES, axis=axis, tiled=True)
        given = (gather(weights_in_pieces(triple_weight, merge_weight, expand_weight), 0), gather(reduce_weight, 0),
                 gather(small, 1).astype(F32), jnp.broadcast_to(gather(expand_bias, 0).astype(F32)[None], (8, FF)))
    o_w, o_r, triple, pt, att, mixed, n2, normed, xp, sv, eb, own_ew, own_er = forward(
        near, dims, counts, block_input[:, 0], position_table, *given)
    if not near:
        o_w, o_r = given[:2]
    out, dx, gt, ge, gr, gs, gb, t4 = backward(near, dims, counts, output_cotangent[:, 0], o_w, o_r, own_ew, own_er, triple, pt,
                                               att, mixed, n2, normed, xp, sv, eb)
    if not near:
        scatter = lambda v, axis: lax.psum_scatter(v.astype(F32), AXES, scatter_dimension=axis, tiled=True)
        gt, ge, gr = scatter(gt.reshape(D, -1), 0), scatter(ge.reshape(D, -1), 0), scatter(gr.reshape(FF, D), 0)
        gs, gb, t4 = scatter(gs, 1), scatter(gb, 1), lax.psum(t4, AXES)
    n, rr = expand_bias.shape[0], reduce_weight.shape[0]
    tr, mg, ex, re, table, *vec = call(
        functools.partial(finish_kernel, True),
        [((rows, 3 * D), F32), ((rows, D), F32), ((rows, FF), F32), ((rr, D), F32), ((EXT * EXT, HEADS), F32)]
        + [((rows,), F32)] * 8 + [((n,), F32)],
        [], [jnp.asarray(TARGET), gt, ge, gr, gs, gb, t4], "finish")
    return (out[:, None], dx[:, None], tr, mg, ex, re, *vec[:7], vec[8], vec[7], table)


def solution(mesh):
    image = P(None, AXES, None, None)
    rows = P(AXES, None)
    vec = P(AXES)
    return jax.shard_map(
        functools.partial(shards, mesh_dims(mesh)), mesh=mesh,
        in_specs=(image, P(None, AXES), image) + (rows,) * 4 + (vec,) * 9 + (P(),),
        out_specs=(image, image) + (rows,) * 4 + (vec,) * 9 + (P(),),
        check_vma=False)
```

```python
import math
import functools

import numpy as np
import jax
import jax.numpy as jnp
from jax import lax
from jax.experimental import pallas as pl
from jax.experimental.pallas import tpu as pltpu
from jax.sharding import PartitionSpec as P

D = 768
FF = 3072
HEADS = 24
HEAD_DIM = 32
WIN = 12
SIDE = 24
SHIFT = 6
TOK = SIDE * SIDE
ROWS = 2 * TOK
WT = WIN * WIN
EXT = 2 * WIN - 1
GROUPS = 3
GH = HEADS // GROUPS
GW = GH * HEAD_DIM
QL = GH * WT
SCALE = HEAD_DIM ** -0.5
MASKED = -1e30
EPS = 1e-5
F32 = jnp.float32
BF16 = jnp.bfloat16
VMEM_LIMIT = 63 << 20
AXES = ("dp", "fsdp")
MESH = pl.DeviceIdType.MESH
ANY = pl.BlockSpec(memory_space=pl.ANY)
VM = pl.BlockSpec(memory_space=pltpu.VMEM)
SM = pl.BlockSpec(memory_space=pltpu.SMEM)
every = slice(None)

NN = (((1,), (0,)), ((), ()))
NT = (((1,), (1,)), ((), ()))
TN = (((0,), (0,)), ((), ()))


def dot(a, b, dims=NN):
    return lax.dot_general(a, b, dims, preferred_element_type=F32)


def layout_constants():
    j = np.arange(WT)
    reg = lambda c: (c >= SIDE - WIN).astype(np.int32) + (c >= SIDE - SHIFT).astype(np.int32)
    raster, label = np.zeros((4, WT), np.int32), np.zeros((4, WT), np.int32)
    for w in range(4):
        rr = (w // 2) * WIN + j // WIN
        rc = (w % 2) * WIN + j % WIN
        raster[w] = ((rr + SHIFT) % SIDE) * SIDE + (rc + SHIFT) % SIDE
        label[w] = reg(rr) * 3 + reg(rc)
    target = np.full((4, WT), -1, np.int32)
    for p in range(4):
        r = j // WIN + (WIN - 1 if p // 2 == 0 else -1)
        s = j % WIN + (WIN - 1 if p % 2 == 0 else -1)
        target[p] = np.where((r >= 0) & (s >= 0), r * EXT + s, -1)
    spread = lambda v: np.broadcast_to(v.reshape(1, TOK), (8, TOK)).astype(np.int32)
    return np.broadcast_to(np.tile(label, (1, GH))[:, None, :], (4, 8, QL)).astype(np.int32), spread(target), spread(raster)


LABEL_Q, TARGET, RASTER_Q = layout_constants()


def fill_places(raster, label=None):
    j = lax.broadcasted_iota(jnp.int32, (WT, 128), 0)
    a = (j * 171) >> 11
    c = j - a * WIN
    reg = lambda v: (v >= SIDE - WIN).astype(jnp.int32) + (v >= SIDE - SHIFT).astype(jnp.int32)
    turn = lambda v: jnp.where(v >= SIDE - SHIFT, v + SHIFT - SIDE, v + SHIFT)
    for w in range(4):
        rr, rc = a + (w // 2) * WIN, c + (w % 2) * WIN
        raster[w] = turn(rr) * SIDE + turn(rc)
        if label is not None:
            label[w] = reg(rr) * 3 + reg(rc)


def lane_iota(shape):
    return lax.broadcasted_iota(jnp.int32, shape, len(shape) - 1)


def aligned(v, n):
    return v if isinstance(v, int) else pl.multiple_of(v, n)


def lanes(start, width):
    return pl.ds(aligned(start, 128), width)


def window(i):
    return pl.ds(aligned(i * WT, WT), WT)


def to_window(raster, w):
    return (raster[w][:, 0:1] == lane_iota((WT, TOK))).astype(BF16)


def to_raster(raster_q, m):
    t = lax.broadcasted_iota(jnp.int32, (WT, TOK), 0) + m * WT
    return (raster_q[0:1, :] == t).astype(BF16)


def stats(x):
    mean = jnp.mean(x, axis=-1, keepdims=True)
    center = x - mean
    var = jnp.mean(center * center, axis=-1, keepdims=True)
    inv = lax.rsqrt(var + EPS)
    return center * inv, inv


def head_stack(dst, x):
    lane = lane_iota(x.shape) // HEAD_DIM
    zero = jnp.zeros_like(x)
    for h in range(GH):
        dst[h * WT:(h + 1) * WT, :] = jnp.where(lane == h, x, zero)


def head_pick(o):
    lane = lane_iota((WT, GW)) // HEAD_DIM
    out = jnp.where(lane == 0, o[0:WT], 0.0)
    for h in range(1, GH):
        out = jnp.where(lane == h, o[h * WT:(h + 1) * WT], out)
    return out


def onehot(target_ref):
    t = lax.broadcasted_iota(jnp.int32, (EXT * EXT, 4 * WT), 0)
    return (t == target_ref[0:1, :]).astype(F32)


def table_rows(table_ref, target_ref, t4):
    t4[...] = lax.dot_general(table_ref[...], onehot(target_ref), NN,
                              precision=lax.Precision.HIGHEST, preferred_element_type=F32) * (1.0 / SCALE)


def spread_bias(g, t4, bias, rowbuf):
    a_of = (lane_iota((1, QL)) % WT) // WIN
    c_of = lane_iota((16, QL)) % WIN
    rows = []
    for p in range(4):
        acc = jnp.zeros((1, QL), F32)
        for h in range(GH):
            piece = t4[pl.ds(g * GH + h, 1), p * WT:(p + 1) * WT]
            piece = jnp.concatenate([piece, jnp.zeros((1, QL - WT), F32)], axis=1)
            acc = acc + (pltpu.roll(piece, h * WT, axis=1) if h else piece)
        rows.append(acc)
    for s in range(2):
        for b in range(WIN):
            pos = pltpu.roll(rows[s], WIN * b, axis=1) if b else rows[s]
            neg = pltpu.roll(rows[2 + s], (WIN * b - WT) % QL, axis=1)
            rowbuf[s, b:b + 1, :] = jnp.where(a_of >= b, pos, neg)
    for d in range(WIN):
        pos = pltpu.roll(rowbuf[0], d, axis=1) if d else rowbuf[0]
        neg = pltpu.roll(rowbuf[1], (d - WIN) % QL, axis=1)
        both = jnp.where(c_of >= d, pos, neg)
        for n in range(9):
            bias[g * 9 + n, pl.ds(d, WIN, stride=WIN), :] = both[0:WIN, n * 128:(n + 1) * 128]


def gather_bias(g, bgrad, accbuf, t4):
    a_of = (lane_iota((1, QL)) % WT) // WIN
    c_of = lane_iota((WIN, QL)) % WIN
    pos = jnp.zeros((WIN, QL), F32)
    neg = jnp.zeros((WIN, QL), F32)
    for d in range(WIN):
        r = jnp.concatenate([bgrad[n, pl.ds(d, WIN, stride=WIN), :] for n in range(9)], axis=1)
        p = jnp.where(c_of >= d, r, 0.0)
        pos = pos + (pltpu.roll(p, QL - d, axis=1) if d else p)
        if d:
            neg = neg + pltpu.roll(jnp.where(c_of < d, r, 0.0), WIN - d, axis=1)
    accbuf[0, 0:WIN, :] = pos
    accbuf[1, 0:WIN, :] = neg
    for s in range(2):
        pp = jnp.zeros((1, QL), F32)
        nn = jnp.zeros((1, QL), F32)
        for b in range(WIN):
            r = accbuf[s, b:b + 1, :]
            p = jnp.where(a_of >= b, r, 0.0)
            pp = pp + (pltpu.roll(p, QL - WIN * b, axis=1) if b else p)
            if b:
                nn = nn + pltpu.roll(jnp.where(a_of < b, r, 0.0), WT - WIN * b, axis=1)
        for part, row in ((s, pp), (2 + s, nn)):
            for h in range(GH):
                moved = pltpu.roll(row, QL - h * WT, axis=1) if h else row
                t4[pl.ds(g * GH + h, 1), part * WT:(part + 1) * WT] = moved[:, 0:WT]


ERF_SLOPE = 0.35
ERF_FIT = (0.19434814435164116, 0.235843067071591, -0.008625688056468914, 0.6849613674275746, -0.6811631064960405, 0.7727015621272543, -0.19806535099226122)


def gelu_pair(v):
    e = jnp.exp(v * v * -0.5)
    t = 1.0 / (1.0 + jnp.abs(v) * (ERF_SLOPE * math.sqrt(0.5)))
    poly = jnp.full_like(t, 0.5 * ERF_FIT[-1])
    for c in ERF_FIT[-2::-1]:
        poly = poly * t + 0.5 * c
    tail = poly * t * e
    cdf = jnp.where(v >= 0, 1.0 - tail, tail)
    return v * cdf, cdf + v * e * (1.0 / math.sqrt(2.0 * math.pi))


def norm_back(hat, inv, gain, grad):
    scaled = grad * gain
    return inv * (scaled - jnp.mean(scaled, axis=-1, keepdims=True)
                  - hat * jnp.mean(scaled * hat, axis=-1, keepdims=True))


class Place:
    def __init__(self, dims):
        self.nz, self.ny, self.nx = dims
        f = lax.axis_index("fsdp")
        self.z = lax.axis_index("dp")
        self.c = lax.rem(f, 2)
        self.x = lax.rem(f // 2, self.nx)
        self.y = f // (2 * self.nx)

    def size(self, axis):
        return {"z": self.nz, "y": self.ny, "x": self.nx, "c": 2}[axis]

    def at(self, axis):
        return {"z": self.z, "y": self.y, "x": self.x, "c": self.c}[axis]

    def step(self, axis, k):
        return lax.rem(self.at(axis) + k, self.size(axis))

    def back(self, axis, k):
        return self.step(axis, self.size(axis) - k)

    def device(self, axis, k):
        p = {a: (self.step(a, k) if a == axis else self.at(a)) for a in "zyxc"}
        return (p["z"], (p["y"] * self.nx + p["x"]) * 2 + p["c"])

    def greet(self):
        barrier = pltpu.get_barrier_semaphore()
        total = 0
        for axis in "czyx":
            for k in range(1, self.size(axis)):
                pl.semaphore_signal(barrier, inc=1, device_id=self.device(axis, k), device_id_type=MESH)
                total += 1
        pl.semaphore_wait(barrier, total)


def mesh_dims(mesh):
    chips = mesh.shape["fsdp"] // 2
    ny = max(n for n in range(1, chips + 1) if n * n <= chips and chips % n == 0)
    return mesh.shape["dp"], ny, chips // ny


class Swap:
    def __init__(self, place, axis, sems, src, dst, came, has=None):
        self.has = has
        self.place, self.axis, self.sems = place, axis, sems
        self.src, self.dst, self.came = src, dst, came

    def make(self, k, src, dst):
        return pltpu.make_async_remote_copy(
            src_ref=src(k), dst_ref=dst(k), send_sem=self.sems[0](k), recv_sem=self.sems[1](k),
            device_id=self.place.device(self.axis, k), device_id_type=MESH)

    def peers(self):
        return range(1, self.place.size(self.axis))

    def each(self, sender, act):
        for k in self.peers():
            if self.has is None:
                act(k)
            else:
                pl.when(self.has(sender(k)))(lambda k=k: act(k))

    def start(self):
        self.each(lambda k: self.place.at(self.axis), lambda k: self.make(k, self.src, self.dst).start())

    def arrive(self):
        self.each(lambda k: self.place.back(self.axis, k), lambda k: self.make(k, self.came, self.came).wait_recv())

    def done(self):
        self.each(lambda k: self.place.at(self.axis), lambda k: self.make(k, self.src, self.dst).wait_send())


def when(cond, body):
    if isinstance(cond, (bool, np.bool_)):
        if cond:
            body()
    else:
        pl.when(cond)(body)


def both(*conds):
    out = True
    for c in conds:
        if isinstance(c, (bool, np.bool_)):
            if not c:
                return False
        else:
            out = c if out is True else jnp.logical_and(out, c)
    return out


def call(kernel, outs, scratch, ins, name):
    return pl.pallas_call(
        kernel, out_shape=[jax.ShapeDtypeStruct(s, d) for s, d in outs], in_specs=[VM] * len(ins),
        out_specs=[VM] * len(outs), scratch_shapes=scratch, name=name,
        compiler_params=pltpu.CompilerParams(vmem_limit_bytes=VMEM_LIMIT))(*ins)


HALF = 4 * D
TM_HALF = 2 * D
FF_HALF = FF // 2
FF_PART = FF // 4


class Gather:
    def __init__(self, place, w, half, base, n_w, r, part, send, recv):
        self.place = place
        self.w, self.half, self.base, self.n_w, self.r, self.part = w, half, base, n_w, r, part
        self.send, self.recv = send, recv
        self.n = n_w + 3

    def block(self, wide, p, c):
        if wide:
            return (every, lanes(c * self.half + self.base + p * 256, 256))
        return (every, lanes(c * (D // 2) + p * 128, 128))

    def swap(self, wide, p, odd, s):
        pc = self.place
        ref = self.w if wide else self.r
        q = p if wide else self.n_w + p
        sems = (lambda k: self.send.at[q, s, k - 1], lambda k: self.recv.at[q, s, k - 1])
        blk = self.block(wide, p, pc.c)
        zs = every if wide else pl.ds(self.part * (pc.nz // 2), pc.nz // 2)
        at = lambda zz, yy, xx, b=blk: ref.at[(zz, yy, xx) + b]
        z, y, x = pc.z, pc.y, pc.x
        if s == 0:
            has = None if wide else (lambda zz: (zz >= pc.nz // 2) == (self.part == 1))
            own = lambda k: at(z, y, x)
            return Swap(pc, "z", sems, own, own, lambda k: at(pc.back("z", k), y, x), has)
        if s == 3:
            mine = lambda k: at(zs, every, every)
            return Swap(pc, "c", sems, mine, mine, lambda k: at(zs, every, every, self.block(wide, p, 1 - pc.c)))
        first = "y" if odd else "x"
        if s == 1:
            own = lambda k: at(zs, y, x)
            if first == "x":
                return Swap(pc, "x", sems, own, own, lambda k: at(zs, y, pc.back("x", k)))
            return Swap(pc, "y", sems, own, own, lambda k: at(zs, pc.back("y", k), x))
        if first == "x":
            own = lambda k: at(zs, y, every)
            return Swap(pc, "y", sems, own, own, lambda k: at(zs, pc.back("y", k), every))
        own = lambda k: at(zs, every, x)
        return Swap(pc, "x", sems, own, own, lambda k: at(zs, every, pc.back("x", k)))

    def on_piece(self, p, body):
        when(both(p >= 0, p < self.n_w), lambda: body(True, p))
        when(both(p >= self.n_w, p < self.n), lambda: body(False, p - self.n_w))

    def tick(self, u, odd, landed=None):
        def last(wide, p):
            self.swap(wide, p, odd, 3).arrive()
            if landed is not None:
                landed(wide, p)

        def step(s):
            def body(wide, p):
                if s:
                    self.swap(wide, p, odd, s - 1).arrive()
                self.swap(wide, p, odd, s).start()
            return body

        self.on_piece(u - 8, last)
        for s in (3, 2, 1, 0):
            self.on_piece(u - 2 * s, step(s))

    def finish(self):
        for q in range(self.n):
            for s in range(4):
                self.swap(q < self.n_w, q if q < self.n_w else q - self.n_w, q % 2 == 1, s).done()


def small_swap(pc, sb, send, recv, s):
    sems = (lambda k: send.at[s, k - 1], lambda k: recv.at[s, k - 1])
    at = lambda zz, yy, xx, c=pc.c: sb.at[zz, yy, xx, c]
    z, y, x = pc.z, pc.y, pc.x
    own = [lambda k: at(z, y, x), lambda k: at(every, y, x), lambda k: at(every, y, every),
           lambda k: at(every, every, every)][s]
    came = [lambda k: at(pc.back("z", k), y, x), lambda k: at(every, y, pc.back("x", k)),
            lambda k: at(every, pc.back("y", k), every), lambda k: at(every, every, every, 1 - pc.c)][s]
    return Swap(pc, "zxyc"[s], sems, own, own, came)


def place_small(sb, sv, eb, n_small, n_wide):
    nz, ny, nx = sb.shape[:3]
    for out, row0, width, total in ((sv, 0, n_small, D), (eb, 8, n_wide, FF)):
        tiles = [jnp.zeros((8, 128), F32) for _ in range(total // 128)]
        lane = lane_iota((8, 128))
        n = 0
        for q in range(nz * ny * nx):
            for c in range(2):
                blk = sb[q // (ny * nx), (q // nx) % ny, q % nx, c, row0:row0 + 8, :]
                tile, off = divmod(n * width, 128)
                moved = pltpu.roll(blk, off, axis=1) if off else blk
                end = off + width
                tiles[tile] = jnp.where((lane >= off) & (lane < min(end, 128)), moved, tiles[tile])
                if end > 128:
                    tiles[tile + 1] = jnp.where(lane < end - 128, moved, tiles[tile + 1])
                n += 1
        out[...] = jnp.concatenate(tiles, axis=1)


def group_cols(g):
    return (((0, g * 384, 256),), ((0, g * 384 + 256, 128), (1, g * 384, 128)), ((1, g * 384 + 128, 256),))


def merge_cols(n):
    return tuple((b // 3, 1152 + lax.rem(b, 3) * 128, 128) for b in (2 * n, 2 * n + 1))


def columns(ref, parts, half):
    take = [ref[:, lanes(h * half + lo, n)] for h, lo, n in parts]
    return take[0] if len(take) == 1 else jnp.concatenate(take, axis=1)


class Flat:
    def __init__(self, ref):
        self.ref = ref

    def __getitem__(self, idx):
        v = self.ref[:, :, :, :, idx[1]]
        return v.reshape(-1, v.shape[-1])


def own_halves(h):
    for g in range(GROUPS):
        yield 0, g * GW + h * 2 * D, g * 384 + h * 128, 256
        yield 0, D + g * GW + h * 128, g * 384 + 256 * (1 - h), 128
    yield 1, h * (D // 2), 1152, D // 2
    for s in range(2):
        yield 2, s * FF_HALF + h * FF_PART, TM_HALF + s * FF_PART, FF_PART
    yield 3, h * (D // 2), 0, D // 2


def forward_kernel(near, dims, counts, x, labq, target, table, *rest):
    n_in = 13 if near else 4
    given = rest[:n_in]
    (o_w, o_r, o_triple, o_pt, o_att, o_mixed, o_n2, o_normed, o_xp, sv, eb, o_ew, o_er,
     w, r, sb, stage_w, stage_r, xp, normed, triple, attended, mixed, n2, pt, t4, bias, rowbuf, qs, st, lk, raster, labk,
     send, recv, ssend, srecv, lsem, psem) = rest[n_in:]

    def keep(n, src, dst):
        return pltpu.make_async_copy(src, dst, lsem.at[n])

    if near:
        pc = Place(dims)
        gather = Gather(pc, w, HALF, 0, 9, r, 0, send, recv)

    def part_of(wide, p):
        zs = every if wide else pl.ds(0, dims[0] // 2)
        for c in range(2):
            n = 2 * (p if wide else 9 + p) + c
            blk = (zs, every, every) + gather.block(wide, p, c)
            yield (keep(n, w.at[blk], o_w.at[blk]) if wide else keep(n, r.at[blk], o_r.at[blk]))

    def landed(wide, p):
        for copy in part_of(wide, p):
            copy.start()

    def small_tick(u):
        if u:
            small_swap(pc, sb, ssend, srecv, u // 2 - 1).arrive()
        if u < 8:
            small_swap(pc, sb, ssend, srecv, u // 2).start()

    if near:
        pc.greet()
        own, vectors = given[:4], given[4:]
        first = []
        for i, ((n, src, dst, width), (_, _, back, _)) in enumerate(zip(own_halves(1 - pc.c), own_halves(pc.c))):
            ref, stage = own[n], (stage_r if n == 3 else stage_w)
            rows = lambda c, m=ref.shape[0]: pl.ds(aligned(c * m, 8), m)
            sems = (lambda k, i=i: ssend.at[4 + i, 0], lambda k, i=i: srecv.at[4 + i, 0])
            first.append(Swap(pc, "c", sems, lambda k, v=ref.at[:, lanes(src, width)]: v,
                              lambda k, v=stage.at[rows(pc.c), lanes(dst, width)]: v,
                              lambda k, v=stage.at[rows(1 - pc.c), lanes(back, width)]: v))
        for s in first:
            s.start()
        sb[pc.z, pc.y, pc.x, pc.c] = jnp.zeros((16, 128), F32)
        for k, v in enumerate(vectors):
            sb[pc.z, pc.y, pc.x, pc.c, k, 0:v.shape[0]] = v[...].astype(BF16).astype(F32)
        for n, src, dst, width in own_halves(pc.c):
            ref, stage = own[n], (stage_r if n == 3 else stage_w)
            stage[pl.ds(aligned(pc.c * ref.shape[0], 8), ref.shape[0]), lanes(dst, width)] = ref[:, lanes(src, width)]
        for s in first[:-1]:
            s.arrive()
        w[pc.z, pc.y, pc.x, :, lanes(pc.c * HALF, HALF)] = stage_w[...].astype(BF16)
        gather.tick(0, False)
        small_tick(0)
        gather.tick(1, True)
        first[-1].arrive()
        r[pc.z, pc.y, pc.x, :, lanes(pc.c * (D // 2), D // 2)] = stage_r[...].astype(BF16)
        o_ew[...] = stage_w[:, TM_HALF + FF_PART:HALF].astype(BF16)
        o_er[...] = stage_r[...].astype(BF16)
    else:
        wown, rown, sv_in, eb_in = given
        loads = [keep(0, wown, w), keep(1, rown, r)]
        for c in loads:
            c.start()
        for c in loads:
            c.wait()
        sv[...] = sv_in[...]
        eb[...] = eb_in[...]

    def permute(i, _):
        xp[window(i), :] = dot(to_window(raster, i % 4), x[i // 4]).astype(BF16)
        return 0

    fill_places(raster, labk)
    table_rows(table, target, t4)

    def prologue(u, _):
        if near:
            for odd in range(2):
                pl.when(u % 2 == odd)(lambda odd=odd: gather.tick(u, odd == 1, landed))
            for k in range(1, 5):
                pl.when(u == 2 * k)(lambda k=k: small_tick(2 * k))

        @pl.when(u < 5)
        def _():
            spread_bias(u - 2, t4, bias, rowbuf)

        @pl.when(jnp.logical_and(u >= 5, u < 9))
        def _():
            lax.fori_loop(2 * (u - 5), 2 * (u - 4), permute, 0)

        return 0

    lax.fori_loop(2, 10, prologue, 0)
    if near:
        place_small(sb, sv, eb, given[0].shape[0], given[3].shape[0])

    def ln1(i, _):
        hat, _i = stats(xp[window(i), :].astype(F32))
        normed[window(i), :] = (hat * sv[0:1, :] + sv[1:2, :]).astype(BF16)
        return 0

    lax.fori_loop(0, 8, ln1, 0)
    keep(24, xp, o_xp).start()
    keep(25, normed, o_normed).start()
    wf = Flat(w)

    def attn(t, i, g):
        b, v = i // 4, i % 4
        rows = window(i)
        col = lambda k: lanes(g * D + k * GW, GW)
        valid = raster[v] < counts[b]
        lk[...] = jnp.where(valid, labk[v], -1)
        head_stack(qs, triple[rows, col(0)])
        st[...] = dot(triple[rows, col(1)], qs[...], NT)
        slot = t % 2
        for n in range(9):
            c = lanes(n * 128, 128)
            s = st[:, c] + bias[g * 9 + n]
            s = jnp.where(lk[...] == labq[v, 0:1, c], s, MASKED)
            m = jnp.max(s, axis=0, keepdims=True)
            e = jnp.exp((s - m) * SCALE)
            tot = jnp.sum(e, axis=0, keepdims=True)
            pt[slot, :, c] = (e * (1.0 / tot)).astype(BF16)
        pltpu.make_async_copy(pt.at[slot], o_pt.at[g * 8 + i], psem.at[slot]).start()
        out = head_pick(dot(pt[slot], triple[rows, col(2)], TN))
        vq = jnp.concatenate([valid, valid], axis=1)
        attended[rows, lanes(g * GW, GW)] = jnp.where(vq, out, 0.0).astype(BF16)

    def quarter(q, _):
        g = q // 4

        @pl.when(q % 4 == 0)
        def _():
            for k, parts in enumerate(group_cols(g)):
                v = dot(normed[...], columns(wf, parts, HALF))
                if k != 1:
                    v = v + sv[2 + k // 2:3 + k // 2, lanes(g * GW, GW)]
                triple[:, lanes(g * D + k * GW, GW)] = v.astype(BF16)

        def one(j, _):
            step = q * 2 + j

            @pl.when(step >= 2)
            def _():
                pltpu.make_async_copy(pt.at[step % 2], o_pt.at[0], psem.at[step % 2]).wait()

            attn(step, step % 8, g)
            return 0

        lax.fori_loop(0, 2, one, 0)
        if near:
            for odd in range(2):
                pl.when(q % 2 == odd)(lambda odd=odd: gather.tick(10 + q, odd == 1, landed))
        return 0

    lax.fori_loop(0, 4 * GROUPS, quarter, 0)
    keep(26, triple, o_triple).start()
    keep(27, attended, o_att).start()
    def merge(n, _):
        cols = lanes(n * 256, 256)
        v = dot(attended[...], columns(wf, merge_cols(n), HALF))
        mixed[:, cols] = xp[:, cols].astype(F32) + v + sv[4:5, cols]
        return 0

    lax.fori_loop(0, 3, merge, 0)
    keep(28, mixed, o_mixed).start()

    def ln2(i, _):
        hat, _i = stats(mixed[window(i), :])
        n2[window(i), :] = (hat * sv[5:6, :] + sv[6:7, :]).astype(BF16)
        return 0

    lax.fori_loop(0, 8, ln2, 0)
    keep(29, n2, o_n2).start()
    if near:
        gather.finish()
        for s in first:
            s.done()
        for s in range(4):
            small_swap(pc, sb, ssend, srecv, s).done()
        for q in range(12):
            for copy in part_of(q < 9, q if q < 9 else q - 9):
                copy.wait()
    for n, src, dst in ((24, xp, o_xp), (25, normed, o_normed), (26, triple, o_triple), (27, attended, o_att),
                        (28, mixed, o_mixed), (29, n2, o_n2)):
        keep(n, src, dst).wait()
    for slot in range(2):
        pltpu.make_async_copy(pt.at[slot], o_pt.at[0], psem.at[slot]).wait()


def forward(near, dims, counts, x, table, *given):
    nz, ny, nx = dims if near else (1, 1, 1)
    rw, rr = (given[0].shape[0] * 2, given[3].shape[0] * 2) if near else (D, FF)
    peers = max(nz, ny, nx, 2) - 1
    full_w, full_r = (nz, ny, nx, rw, 2 * HALF), (nz, ny, nx, rr, D)
    tiny = (8, 128)
    outs = [(full_w if near else tiny, BF16), (full_r if near else tiny, BF16), ((ROWS, 3 * D), BF16),
            ((8 * GROUPS, WT, QL), BF16), ((ROWS, D), BF16), ((ROWS, D), F32), ((ROWS, D), BF16), ((ROWS, D), BF16),
            ((ROWS, D), BF16), ((8, D), F32), ((8, FF), F32), ((rw, FF_PART) if near else tiny, BF16),
            ((rr, D // 2) if near else tiny, BF16)]
    if not near:
        given = (given[0].reshape(full_w), given[1].reshape(full_r)) + given[2:]
    vm = pltpu.VMEM
    dma = pltpu.SemaphoreType.DMA
    scratch = [vm(full_w, BF16), vm(full_r, BF16), vm((nz, ny, nx, 2, 16, 128), F32), vm((rw if near else 8, HALF), F32),
               vm((rr if near else 8, D // 2), F32), vm((ROWS, D), BF16), vm((ROWS, D), BF16), vm((ROWS, 3 * D), BF16),
               vm((ROWS, D), BF16), vm((ROWS, D), F32), vm((ROWS, D), BF16), vm((2, WT, QL), BF16),
               vm((HEADS, 4 * WT), F32), vm((GROUPS * 9, WT, 128), F32), vm((2, 16, QL), F32), vm((QL, GW), BF16),
               vm((WT, QL), F32), vm((WT, 128), jnp.int32), vm((4, WT, 128), jnp.int32), vm((4, WT, 128), jnp.int32),
               dma((12, 4, peers)), dma((12, 4, peers)), dma((14, peers)), dma((14, peers)), dma((30,)), dma((2,))]
    params = dict(collective_id=0, has_side_effects=True) if near else {}
    return pl.pallas_call(
        functools.partial(forward_kernel, near, dims),
        out_shape=[jax.ShapeDtypeStruct(s, d) for s, d in outs],
        in_specs=[SM] + [VM] * 4 + ([VM] * 13 if near else [ANY, ANY, VM, VM]),
        out_specs=[ANY] * 9 + [VM] * 4,
        scratch_shapes=scratch, name="forward",
        compiler_params=pltpu.CompilerParams(vmem_limit_bytes=VMEM_LIMIT, **params),
    )(counts, x, jnp.asarray(LABEL_Q), jnp.asarray(TARGET), table.T,
      *given)


class Scatter:
    def __init__(self, place, bufs, send, recv):
        self.place = place
        self.bufs, self.send, self.recv = bufs, send, recv

    def src(self, kind, g, i, ab, c):
        if kind == "r":
            n = g.shape[3] // 2
            return g.at[every, every, every, pl.ds(ab * n, n), lanes(c * (D // 2) + i * 128, 128)]
        return g.at[every, every, every, every, lanes(c * FF_HALF + i * 256 + ab * 128, 128)]

    def swap(self, kind, g, out, i, ab, s):
        pc = self.place
        r0, r1, r2, r3, fin = self.bufs[kind]
        q = {"e": 0, "t": 6, "r": 12}[kind] + i
        sems = (lambda k: self.send.at[q, ab, s, k - 1], lambda k: self.recv.at[q, ab, s, k - 1])
        first, second = ("y", "x") if ab == 0 else ("x", "y")
        if s == 0:
            to = lambda k: r0.at[i, ab]
            return Swap(pc, "c", sems, lambda k: self.src(kind, g, i, ab, 1 - pc.c), to, to)
        if s == 1:
            to = lambda k: r1.at[i, ab, k - 1]
            at = lambda k: (every, pc.step("y", k), every) if first == "y" else (every, every, pc.step("x", k))
            return Swap(pc, first, sems, lambda k: r0.at[(i, ab) + at(k)], to, to)
        if s == 2:
            to = lambda k: r2.at[i, ab, k - 1]
            return Swap(pc, second, sems, lambda k: r1.at[i, ab, 0, every, pc.step(second, k)], to, to)
        if s == 3:
            to = lambda k: r3.at[i, ab, k - 1]
            return Swap(pc, "z", sems, lambda k: r2.at[i, ab, 0, pc.step("z", k)], to, to)
        n = out.shape[0]
        if kind == "r":
            cols = lambda c: lanes(c * (D // 2) + i * 128, 128)
            return Swap(pc, "c", sems, lambda k: fin.at[i, 1 - pc.c], lambda k: out.at[:, cols(pc.c)],
                        lambda k: out.at[:, cols(1 - pc.c)])
        cols = lambda c: lanes(c * FF_HALF + i * 256 + ab * 128, 128)
        return Swap(pc, "c", sems, lambda k: fin.at[i, ab, pl.ds(aligned((1 - pc.c) * n, 8), n), :],
                    lambda k: out.at[:, cols(pc.c)], lambda k: out.at[:, cols(1 - pc.c)])

    def advance(self, kind, g, out, i, s):
        pc = self.place
        r0, r1, r2, r3, fin = self.bufs[kind]
        if s == 5:
            for ab in range(1 if kind == "r" else 2):
                self.swap(kind, g, out, i, ab, 4).arrive()
            return
        for ab in range(2):
            first, second = ("y", "x") if ab == 0 else ("x", "y")
            if s:
                self.swap(kind, g, out, i, ab, s - 1).arrive()
            if s == 1:
                n = r0.shape[-2]

                def add(z, _):
                    if kind == "r":
                        own = g[z, :, :, ab * n:(ab + 1) * n, lanes(pc.c * (D // 2) + i * 128, 128)]
                    else:
                        own = g[z, :, :, :, lanes(pc.c * FF_HALF + i * 256 + ab * 128, 128)]
                    r0[i, ab, z] = (r0[i, ab, z].astype(F32) + own.astype(F32)).astype(BF16)
                    return 0

                lax.fori_loop(0, pc.nz, add, 0)
            if s == 2:
                at = (every, pc.y, every) if first == "y" else (every, every, pc.x)
                v = r0[(i, ab) + at].astype(F32)
                for k in range(pc.size(first) - 1):
                    v = v + r1[i, ab, k].astype(F32)
                r1[i, ab, 0] = v.astype(BF16)
            if s == 3:
                v = r1[i, ab, 0, :, pc.at(second)].astype(F32)
                for k in range(pc.size(second) - 1):
                    v = v + r2[i, ab, k].astype(F32)
                r2[i, ab, 0] = v.astype(BF16)
            if s == 4:
                v = r2[i, ab, 0, pc.z].astype(F32)
                for k in range(pc.nz - 1):
                    v = v + r3[i, ab, k].astype(F32)
                fin[i, ab] = v
                if kind != "r":
                    n = out.shape[0]
                    out[:, lanes(pc.c * FF_HALF + i * 256 + ab * 128, 128)] = fin[i, ab, pl.ds(aligned(pc.c * n, 8), n), :]
            if s < 4 or kind != "r":
                self.swap(kind, g, out, i, ab, s).start()
        if s == 4 and kind == "r":
            out[:, lanes(pc.c * (D // 2) + i * 128, 128)] = fin[i, pc.c]
            self.swap(kind, g, out, i, 0, 4).start()

    def done(self, kind, g, out, pieces, steps):
        for i in range(pieces):
            for s in steps:
                for ab in range(1 if (kind == "r" and s == 4) else 2):
                    self.swap(kind, g, out, i, ab, s).done()


class SmallSum:
    def __init__(self, place, slots, send, recv):
        self.place, self.slots, self.send, self.recv = place, slots, send, recv

    def base(self, i):
        return sum(self.place.size(a) for a in "cyxz"[:i])

    def swap(self, i):
        pc, a = self.place, "cyxz"[i]
        sems = (lambda k: self.send.at[i, k - 1], lambda k: self.recv.at[i, k - 1])
        me = lambda k: self.slots.at[self.base(i) + pc.at(a)]
        return Swap(pc, a, sems, me, me, lambda k: self.slots.at[self.base(i) + pc.back(a, k)])

    def start(self):
        self.swap(0).start()

    def advance(self, i):
        self.swap(i).arrive()
        s = self.slots[self.base(i)]
        for k in range(1, self.place.size("cyxz"[i])):
            s = s + self.slots[self.base(i) + k]
        if i == 3:
            return s
        self.slots[self.base(i + 1) + self.place.at("cyxz"[i + 1])] = s
        self.swap(i + 1).start()

    def done(self):
        for i in range(4):
            self.swap(i).done()


def events(t):
    out = [("e", i, s) for i in range(6) for s in range(6) if 2 * i + 1 + 2 * s == t and t >= 12]
    for i, at in enumerate(((12, 14, 16, 18, 20, 22), (13, 15, 17, 19, 21, 23), (14, 15, 18, 20, 22, 24))):
        out += [("r", i, s) for s in range(6) if at[s] == t]
    return out + [("t", 5, s) for s in range(6) if 16 + 2 * s == t]


def backward_kernel(near, dims, counts, rasq, do, w, r, own_ew, own_er, triple_h, pt_h, att_h, mixed_h, n2_h, normed_h,
                    xp_h, sv, eb, o_out, o_dx, o_act, o_t, o_e, o_r, o_small, o_deb, o_t4,
                    raster, ew, rw, dop, dn2, mixed, part, e0, e1, e2, e3, ef, t0, t1, t2, t3, tf, b0, b1, b2, b3, bf, slots_a, slots_g, late, slots_l, sums_g, smalls,
                    gsend, grecv, send, recv, ssend, srecv, lsem):
    def load(n, src, dst):
        return pltpu.make_async_copy(src, dst, lsem.at[n])

    if near:
        pc = Place(dims)
        rs = Scatter(pc, {"e": (e0, e1, e2, e3, ef), "t": (t0, t1, t2, t3, tf), "r": (b0, b1, b2, b3, bf)}, send, recv)
        sum_a = SmallSum(pc, slots_a, ssend.at[0], srecv.at[0])
        sum_l = SmallSum(pc, slots_l, ssend.at[1], srecv.at[1])
        sum_g = lambda g: SmallSum(pc, slots_g.at[g], ssend.at[2 + g], srecv.at[2 + g])
        pc.greet()
    else:
        pc = None
    small = smalls
    fill_places(raster)
    small[...] = jnp.zeros(small.shape, F32)

    def feed_forward(n2, n2t, act, hs, ds, hl, de, dr):
        half_z = dims[0] // 2
        loads = [load(0, n2_h, n2), load(3, mixed_h, mixed)]
        if near:
            for c in range(2):
                a, b = lanes(c * HALF + TM_HALF, FF_PART), lanes(c * FF_HALF, FF_PART)
                loads.append(load(4 + c, w.at[:, :, :, :, a], ew.at[:, :, :, :, b]))
            loads.append(load(2, r.at[0:half_z], rw.at[0:half_z]))
        else:
            for c in range(2):
                a, b = lanes(c * HALF + TM_HALF, FF_HALF), lanes(c * FF_HALF, FF_HALF)
                loads.append(load(4 + c, w.at[:, :, :, :, a], ew.at[:, :, :, :, b]))
            loads.append(load(2, r, rw))
        for c in loads:
            c.start()
        if near:
            gather = Gather(pc, ew, FF_HALF, FF_PART, 3, rw, 1, gsend, grecv)
            ew[pc.z, pc.y, pc.x, :, lanes(pc.c * FF_HALF + FF_PART, FF_PART)] = own_ew[...]

            @pl.when(pc.z >= half_z)
            def _():
                rw[pc.z, pc.y, pc.x, :, lanes(pc.c * (D // 2), D // 2)] = own_er[...]

            gather.tick(0, False)
            gather.tick(1, True)

        def permute(i, _):
            dop[window(i), :] = dot(to_window(raster, i % 4), do[i // 4]).astype(BF16)
            return 0

        lax.fori_loop(0, 8, permute, 0)
        for c in loads:
            c.wait()
        n2t[...] = n2[...].T
        dn2[...] = jnp.zeros(dn2.shape, F32)
        small[7:8, :] = jnp.sum(dop[...].astype(F32), axis=0, keepdims=True)
        nz, ny, nx, rr = rw.shape[:4]
        per = FF // 256

        def rows_of(n0):
            return flat_r[pl.ds(aligned(n0, 256), 256), :]

        flat_r = rw.reshape(FF, D)
        fe, fde = Flat(ew), de

        def chunk(j, _):
            s, k = j // 6, j % 6
            c, off = k % 2, k // 2
            col = lanes(c * FF_HALF + s * FF_PART + off * 256, 256)
            n0 = s * FF_HALF + c * FF_PART + off * 256
            nat = lanes(n0, 256)
            weights = fe[:, col]
            rows = rows_of(n0)
            hs[...] = dot(n2[...], weights)
            ds[...] = dot(dop[...], rows, NT)
            bias = eb[0:1, nat]
            total = jnp.zeros((8, 256), F32)
            for m in range(18):
                rr_ = pl.ds(m * 64, 64)
                a, slope = gelu_pair(hs[rr_, :] + bias)
                act[rr_, nat] = a.astype(BF16)
                hg = ds[rr_, :] * slope
                for q in range(8):
                    total = total + hg[q * 8:(q + 1) * 8]
                hl[rr_, :] = hg.astype(BF16)
            small[pl.ds(8 + s * 2 + c, 1), lanes(off * 256, 256)] = jnp.sum(total, axis=0, keepdims=True)
            de[:, :, :, :, col] = dot(n2t[...], hl[...]).astype(BF16).reshape(de.shape[:4] + (256,))
            for n in range(3):
                cc = lanes(n * 256, 256)
                dn2[:, cc] += dot(hl[...], weights[n * 256:(n + 1) * 256], NT)
            if near:
                gather.tick(2 + 2 * j, False)
                gather.tick(3 + 2 * j, True)
                for step in range(5, -1, -1):
                    i = j // 2 - step
                    pl.when(jnp.logical_and(lax.rem(j, 2) == 1, i >= 0))(
                        lambda i=i, step=step: rs.advance("e", de, o_e, i, step))
            return 0

        lax.fori_loop(0, per, chunk, 0)

        def er_tick(t):
            for kind, i, s in events(t):
                rs.advance(kind, de if kind == "e" else dr, o_e if kind == "e" else o_r, i, s)

        spill = load(6, act, o_act)
        spill.start()
        flat_dr = dr.reshape(FF, D)

        def reduce_part(n, _):
            def quarter(m, _):
                two = jnp.concatenate([dop[:, lanes(n * 128, 128)], dop[:, lanes(D // 2 + n * 128, 128)]], axis=1)
                v = dot(act[:, lanes(m * D, D)], two, TN).astype(BF16)
                rows = pl.ds(aligned(m * D, D), D)
                flat_dr[rows, lanes(n * 128, 128)] = v[:, :128]
                flat_dr[rows, lanes(D // 2 + n * 128, 128)] = v[:, 128:]
                return 0

            lax.fori_loop(0, 4, quarter, 0)
            if near:
                for t in range(3):
                    pl.when(n == t)(lambda t=t: er_tick(12 + t))
            return 0

        lax.fori_loop(0, 3, reduce_part, 0)

        def ln2b(i, _):
            rows = window(i)
            hat, inv = stats(mixed[rows, :])
            g = dn2[rows, :]
            small[5:6, :] += jnp.sum(g * hat, axis=0, keepdims=True)
            small[6:7, :] += jnp.sum(g, axis=0, keepdims=True)
            m = dop[rows, :].astype(F32) + norm_back(hat, inv, sv[5:6, :], g)
            small[4:5, :] += jnp.sum(m, axis=0, keepdims=True)
            mixed[rows, :] = m
            part[rows, :] = m.astype(BF16)
            return 0

        lax.fori_loop(0, 8, ln2b, 0)
        if near:
            er_tick(15)
            gather.finish()
            rs.done("e", de, o_e, 6, range(1))
            rs.done("r", dr, o_r, 3, range(1))
        else:
            for c in (load(4, de, o_e), load(5, dr, o_r)):
                c.start()
                c.wait()
        spill.wait()

    nz, ny, nx, rw_rows = w.shape[:4]
    rr_rows = r.shape[3]
    vm = pltpu.VMEM
    pl.run_scoped(feed_forward, vm((ROWS, D), BF16),
                  vm((D, ROWS), BF16), vm((ROWS, FF), BF16), vm((ROWS, 256), F32), vm((ROWS, 256), F32), vm((ROWS, 256), BF16),
                  vm((nz, ny, nx, rw_rows, FF), BF16), vm((nz, ny, nx, rr_rows, D), BF16))
    tw = ew
    flat_tw = tw.reshape(D, FF)
    flat_r = rw.reshape(FF, D)

    def after_feed_forward(dt, triple, ml, xp, t4g, sum_keep):
        def ert_tick(t):
            if near:
                for kind, i, s in events(t):
                    rs.advance(kind, {"e": None, "r": None, "t": dt}[kind], {"e": o_e, "r": o_r, "t": o_t}[kind], i, s)

        def put(parts, v):
            at = 0
            for h, lo, n in parts:
                dt[:, :, :, :, lanes(h * TM_HALF + lo, n)] = v[:, at:at + n].reshape(dt.shape[:4] + (n,))
                at += n

        def group_sum(g, m):
            total = sum_g(g).advance(m)
            if total is not None:
                sums_g[g] = total

        def t_tick(t):
            for s in range(5, -1, -1):
                q = t - 19 - s
                if isinstance(t, int):
                    if q % 2 == 0 and 0 <= q // 2 <= 2:
                        k = q // 2
                        for i in range(3 - k - k // 2, 5 - 2 * k + k // 2):
                            rs.advance("t", dt, o_t, i, s)
                else:
                    k = q // 2

                    def run(k=k, s=s):
                        lax.fori_loop(3 - k - k // 2, 5 - 2 * k + k // 2,
                                      lambda i, _: (rs.advance("t", dt, o_t, i, s), 0)[1], 0)

                    pl.when(jnp.logical_and(q >= 0, lax.rem(q + 20, 2) == 0))(run)

        def attention(datt, xt, xn, qs, dos, st, raw, pt, bgrad, accbuf, psem):
            loads = [load(0, att_h, xn), load(1, triple_h, triple), load(2, xp_h, xp)]
            loads += [load(4 + c, w.at[:, :, :, :, lanes(c * HALF, TM_HALF)], tw.at[:, :, :, :, lanes(c * TM_HALF, TM_HALF)])
                      for c in range(2)]
            for c in loads:
                c.start()

            def fetch(step):
                return pltpu.make_async_copy(pt_h.at[(2 - step // 8) * 8 + step % 8], pt.at[step % 2], psem.at[step % 2])

            fetch(0).start()
            for c in loads:
                c.wait()
            xt[...] = xn[...].T
            again = load(0, normed_h, xn)
            again.start()

            def merge_grad(n, _):
                put(merge_cols(n), dot(xt[...], part[:, lanes(n * 256, 256)]).astype(BF16))
                return 0

            lax.fori_loop(0, 3, merge_grad, 0)
            ert_tick(16)

            def merge_back(n, _):
                rows = pl.ds(aligned(n * 256, 256), 256)
                m = jnp.concatenate([flat_tw[rows, 1152:TM_HALF], flat_tw[rows, TM_HALF + 1152:]], axis=1)
                datt[:, lanes(n * 256, 256)] = dot(part[...], m, NT).astype(BF16)
                return 0

            lax.fori_loop(0, 3, merge_back, 0)
            again.wait()
            xt[...] = xn[...].T
            ert_tick(17)
            if near:
                slots_a[pc.c, 0:4, :] = small[4:8, :]
                slots_a[pc.c, 4:8, :] = small[8:12, :]
                sum_a.start()

            def one(step, g):
                i = step % 8
                b, v = i // 4, i % 4
                rows = window(i)
                col = lambda k: lanes(g * D + k * GW, GW)
                slot = step % 2

                @pl.when(step < 23)
                def _():
                    fetch(step + 1).start()

                valid = raster[v] < counts[b]
                vq = jnp.concatenate([valid, valid], axis=1)
                da = datt[rows, lanes(g * GW, GW)]
                da = jnp.where(vq, da.astype(F32), 0.0).astype(BF16)
                head_stack(qs, triple[rows, col(0)])
                head_stack(dos, da)
                st[...] = dot(triple[rows, col(2)], dos[...], NT)
                fetch(step).wait()
                for n in range(9):
                    c = lanes(n * 128, 128)
                    p = pt[slot, :, c].astype(F32)
                    d = st[:, c]
                    inner = jnp.sum(p * d, axis=0, keepdims=True)
                    s = p * (d - inner)
                    bgrad[n] += s
                    raw[:, c] = (s * SCALE).astype(BF16)
                key = triple[rows, col(1)]
                triple[rows, col(2)] = dot(pt[slot], dos[...]).astype(BF16)
                triple[rows, col(1)] = dot(raw[...], qs[...]).astype(BF16)
                triple[rows, col(0)] = head_pick(dot(raw[...], key, TN)).astype(BF16)

            def half_group(q, _):
                g = 2 - q // 2

                @pl.when(q % 2 == 0)
                def _():
                    bgrad[...] = jnp.zeros(bgrad.shape, F32)

                lax.fori_loop(0, 4, lambda j, _: (one(q * 4 + j, g), 0)[1], 0)

                @pl.when(q % 2 == 1)
                def _():
                    gather_bias(g, bgrad, accbuf, t4g)
                    for k, parts in enumerate(group_cols(g)):
                        v = triple[:, lanes(g * D + k * GW, GW)]
                        if k != 1:
                            small[2 + k // 2:3 + k // 2, lanes(g * GW, GW)] = jnp.sum(v.astype(F32), axis=0, keepdims=True)
                        put(parts, dot(xt[...], v).astype(BF16))

                if near:
                    for t in range(18, 24):
                        if events(t):
                            pl.when(q == t - 18)(lambda t=t: ert_tick(t))
                    t_tick(18 + q)
                    for m in range(4):
                        k = (q - 2 - m) // 2

                        def more(k=k, m=m):
                            total = sum_g(2 - k).advance(m)
                            if total is not None:
                                sums_g[2 - k] = total

                        pl.when(jnp.logical_and(q - 2 - m >= 0, lax.rem(q + 10 - m, 2) == 0))(more)
                    for m, at in enumerate((0, 2, 4)):
                        pl.when(q == at)(lambda m=m: sum_a.advance(m) and None)

                    @pl.when(q % 2 == 1)
                    def _():
                        own = slots_g.at[g, pc.c]
                        own[...] = jnp.zeros(own.shape, F32)
                        own[0:8, 0:4 * WT] = t4g[pl.ds(aligned(g * GH, GH), GH), :]
                        for k in range(2):
                            own[8 + k:9 + k, 0:GW] = small[2 + k:3 + k, lanes(g * GW, GW)]
                        sum_g(g).start()
                return 0

            lax.fori_loop(0, 2 * GROUPS, half_group, 0)
        def rest(act):
            again = load(0, o_act, act)
            again.start()

            def normed_grad(n, _):
                rows = pl.ds(aligned(n * 256, 256), 256)
                weights = jnp.concatenate([flat_tw[rows, h * TM_HALF + lo:h * TM_HALF + lo + m]
                                           for g in range(GROUPS) for p in group_cols(g) for h, lo, m in p], axis=1)
                dn2[:, lanes(n * 256, 256)] = dot(triple[...], weights, NT)
                if near:
                    for t in range(2):
                        @pl.when(n == t)
                        def _(t=t):
                            ert_tick(24 + t)
                            t_tick(24 + t)
                            group_sum(0, t)
                            group_sum(1, t + 2)
                return 0

            lax.fori_loop(0, 3, normed_grad, 0)

            def ln1b(i, _):
                rows = window(i)
                hat, inv = stats(xp[rows, :].astype(F32))
                g = dn2[rows, :]
                late[0:1, :] += jnp.sum(g * hat, axis=0, keepdims=True)
                late[1:2, :] += jnp.sum(g, axis=0, keepdims=True)
                ml[rows, :] = (mixed[rows, :] + norm_back(hat, inv, sv[0:1, :], g)).astype(BF16)
                return 0

            late[...] = jnp.zeros(late.shape, F32)
            lax.fori_loop(0, 8, ln1b, 0)
            if near:
                slots_l[pc.c] = late[0:2, :]
                sum_l.start()
                ert_tick(26)
                t_tick(26)
                group_sum(0, 2)
                sum_keep[...] = sum_a.advance(3)
            mixed_again = load(3, mixed_h, mixed)
            mixed_again.start()

            def back_to_raster(src, dst):
                def block(k, _):
                    b, m = k // 4, k % 4
                    dst[window(k), :] = dot(to_raster(rasq, m), src[pl.ds(aligned(b * TOK, TOK), TOK), :]).astype(BF16)
                    return 0

                lax.fori_loop(0, 8, block, 0)

            back_to_raster(ml, part)
            saves = [load(4 + b, part.at[b * TOK:(b + 1) * TOK, :], o_dx.at[b]) for b in range(2)]
            for c in saves:
                c.start()
            if near:
                t_tick(27)
                group_sum(0, 3)
                sum_l.advance(0)
            again.wait()
            mixed_again.wait()

            def output(n, _):
                c = lanes(n * 256, 256)
                ml[:, c] = (mixed[:, c] + dot(act[...], flat_r[:, c]) + sv[7:8, c]).astype(BF16)
                if near:
                    for t in range(2):
                        @pl.when(n == t)
                        def _(t=t):
                            t_tick(28 + t)
                            sum_l.advance(1 + t)
                return 0

            lax.fori_loop(0, 3, output, 0)
            back_to_raster(ml, dop)
            more = [load(b, dop.at[b * TOK:(b + 1) * TOK, :], o_out.at[b]) for b in range(2)]
            for c in more:
                c.start()
            if near:
                total_l = sum_l.advance(3)
                dev = pc.z * (2 * pc.ny * pc.nx) + (pc.y * pc.nx + pc.x) * 2 + pc.c
                n = o_small.shape[1]
                shift = lax.rem(D - dev * n, D)
                biases = [jnp.concatenate([sums_g[g, 8 + k:9 + k, 0:GW] for g in range(GROUPS)], axis=1) for k in range(2)]
                rows = jnp.concatenate([total_l] + biases + [sum_keep[0:4, :]], axis=0)
                o_small[...] = pltpu.roll(rows, shift, axis=1)[:, 0:n]
                wide_n = o_deb.shape[1]
                per = D // wide_n
                row = sum_keep[pl.ds(4 + dev // per, 1), :]
                o_deb[...] = pltpu.roll(row, lax.rem(D - lax.rem(dev, per) * wide_n, D), axis=1)[:, 0:wide_n]
                for g in range(GROUPS):
                    o_t4[g * GH:(g + 1) * GH, :] = sums_g[g, 0:8, 0:4 * WT]
                rs.done("e", None, o_e, 6, range(1, 5))
                rs.done("r", None, o_r, 3, range(1, 5))
                rs.done("t", dt, o_t, 6, range(5))
                sum_a.done()
                sum_l.done()
                for g in range(GROUPS):
                    sum_g(g).done()
            else:
                o_small[0:2, :] = late[0:2]
                o_small[2:8, :] = small[2:8, :]
                for k in range(4):
                    o_deb[0:1, k * D:(k + 1) * D] = small[8 + k:9 + k, :]
                o_t4[...] = t4g[...]
                save = load(3, dt, o_t)
                save.start()
                save.wait()
            for c in saves + more:
                c.wait()

        pl.run_scoped(attention, vm((ROWS, D), BF16), vm((D, ROWS), BF16), vm((ROWS, D), BF16), vm((QL, GW), BF16),
                      vm((QL, GW), BF16), vm((WT, QL), F32), vm((WT, QL), BF16), vm((2, WT, QL), BF16), vm((9, WT, 128), F32),
                      vm((2, 16, QL), F32), pltpu.SemaphoreType.DMA((2,)))
        pl.run_scoped(rest, vm((ROWS, FF), BF16))

    pl.run_scoped(after_feed_forward, vm((nz, ny, nx, rw_rows, 2 * TM_HALF), BF16), vm((ROWS, 3 * D), BF16),
                  vm((ROWS, D), BF16), vm((ROWS, D), BF16), vm((HEADS, 4 * WT), F32), vm((8, D), F32))


def backward(near, dims, counts, do, w, r, own_ew, own_er, triple, pt, att, mixed, n2, normed, xp, sv, eb):
    nz, ny, nx = dims if near else (1, 1, 1)
    if not near:
        w, r = w.reshape(1, 1, 1, D, -1), r.reshape(1, 1, 1, FF, D)
    rw, rr = w.shape[3], r.shape[3]
    peers = max(nz, ny, nx, 2) - 1
    vm = pltpu.VMEM
    dma = pltpu.SemaphoreType.DMA
    bufs = []
    for count, n in ((6, rw), (6, rw), (3, rr // 2)) if near else ((1, 16),) * 3:
        bufs += [vm((count, 2, nz, ny, nx, n, 128), BF16), vm((count, 2, max(ny - 1, 1), nz, nx, n, 128), BF16),
                 vm((count, 2, max(nx - 1, 1), nz, n, 128), BF16), vm((count, 2, max(nz - 1, 1), n, 128), BF16),
                 vm((count, 2, n, 128), F32)]
    n_slots = 2 + nz + ny + nx
    if near:
        outs = [((rw // 2, 2 * TM_HALF), F32), ((rw // 2, FF), F32), ((rr // 2, D), F32), ((8, rw // 2), F32), ((1, rr // 2), F32)]
    else:
        outs = [((1, 1, 1, D, 2 * TM_HALF), BF16), ((1, 1, 1, D, FF), BF16), ((1, 1, 1, FF, D), BF16), ((8, D), F32), ((1, FF), F32)]
    outs = [((2, TOK, D), BF16), ((2, TOK, D), BF16), ((ROWS, FF), BF16)] + outs + [((HEADS, 4 * WT), F32)]
    params = dict(collective_id=1, has_side_effects=True) if near else {}
    return pl.pallas_call(
        functools.partial(backward_kernel, near, dims),
        out_shape=[jax.ShapeDtypeStruct(s, d) for s, d in outs],
        in_specs=[SM, VM, VM, ANY, ANY, VM, VM] + [ANY] * 7 + [VM] * 2,
        out_specs=[ANY] * 3 + ([VM] * 3 if near else [ANY] * 3) + [VM] * 3,
        scratch_shapes=[vm((4, WT, 128), jnp.int32), vm((nz, ny, nx, rw, FF), BF16), vm((nz, ny, nx, rr, D), BF16), vm((ROWS, D), BF16), vm((ROWS, D), F32),
                        vm((ROWS, D), F32), vm((ROWS, D), BF16)] + bufs
        + [vm((n_slots, 8, D), F32), vm((GROUPS, n_slots, 16, 640), F32), vm((8, D), F32), vm((n_slots, 2, D), F32),
           vm((GROUPS, 16, 640), F32), vm((16, D), F32),
           dma((6, 4, peers)), dma((6, 4, peers)), dma((15, 2, 5, peers)), dma((15, 2, 5, peers)), dma((5, 4, peers)),
           dma((5, 4, peers)), dma((7,))],
        name="backward",
        compiler_params=pltpu.CompilerParams(vmem_limit_bytes=VMEM_LIMIT, **params),
    )(counts, jnp.asarray(RASTER_Q), do, w, r, own_ew, own_er, triple, pt, att, mixed, n2, normed, xp, sv,
      eb)


def finish_kernel(target, out_h, dx_h, t, e, r, small, deb, t4, out, dx, triple, merge, expand, reduce, table, *rest):
    vectors = rest
    out[...] = out_h[...]
    dx[...] = dx_h[...]
    for g in range(GROUPS):
        for k, parts in enumerate(group_cols(g)):
            at = k * D + g * GW
            for h, lo, n in parts:
                triple[:, at:at + n] = t[:, h * TM_HALF + lo:h * TM_HALF + lo + n]
                at += n
    for c in range(2):
        merge[:, c * D // 2:(c + 1) * D // 2] = t[:, c * TM_HALF + 1152:(c + 1) * TM_HALF]
        for s in range(2):
            expand[:, s * FF_HALF + c * FF_PART:s * FF_HALF + (c + 1) * FF_PART] = (
                e[:, c * FF_HALF + s * FF_PART:c * FF_HALF + (s + 1) * FF_PART])
    reduce[...] = r[...]
    for k, v in enumerate(vectors[:8]):
        v[...] = small[k, :]
    vectors[8][...] = deb[0, :]
    table[...] = lax.dot_general(t4[...], onehot(target), NT, precision=lax.Precision.HIGHEST,
                                 preferred_element_type=F32)


def weights_in_pieces(triple_weight, merge_weight, expand_weight):
    halves = []
    for c in range(2):
        for g in range(GROUPS):
            q, k, v = (triple_weight[:, i * D + g * GW:i * D + (g + 1) * GW] for i in range(3))
            halves += [q, k[:, :128]] if c == 0 else [k[:, 128:], v]
        halves.append(merge_weight[:, c * D // 2:(c + 1) * D // 2])
        halves += [expand_weight[:, s * FF_HALF + c * FF_PART:s * FF_HALF + (c + 1) * FF_PART] for s in range(2)]
    return jnp.concatenate(halves, axis=1)


def shards(dims, block_input, valid_counts, output_cotangent, triple_weight, merge_weight, expand_weight, reduce_weight,
           first_gain, first_shift, query_bias, value_bias, merge_bias, second_gain, second_shift, expand_bias,
           reduce_bias, position_table):
    counts = valid_counts[:, 0]
    rows = triple_weight.shape[0]
    near = rows % 8 == 0 and dims[0] % 4 == 0 and dims[1] == dims[2]
    if near:
        given = (triple_weight, merge_weight, expand_weight, reduce_weight, first_gain, first_shift, query_bias, value_bias,
                 merge_bias, second_gain, second_shift, reduce_bias, expand_bias)
    else:
        small = jnp.stack([first_gain, first_shift, query_bias, value_bias, merge_bias, second_gain, second_shift,
                           reduce_bias])
        gather = lambda v, axis: lax.all_gather(v.astype(BF16), AXES, axis=axis, tiled=True)
        given = (gather(weights_in_pieces(triple_weight, merge_weight, expand_weight), 0), gather(reduce_weight, 0),
                 gather(small, 1).astype(F32), jnp.broadcast_to(gather(expand_bias, 0).astype(F32)[None], (8, FF)))
    o_w, o_r, triple, pt, att, mixed, n2, normed, xp, sv, eb, own_ew, own_er = forward(
        near, dims, counts, block_input[:, 0], position_table, *given)
    if not near:
        o_w, o_r = given[:2]
    out, dx, _, gt, ge, gr, gs, gb, t4 = backward(near, dims, counts, output_cotangent[:, 0], o_w, o_r, own_ew, own_er, triple, pt,
                                               att, mixed, n2, normed, xp, sv, eb)
    if not near:
        scatter = lambda v, axis: lax.psum_scatter(v.astype(F32), AXES, scatter_dimension=axis, tiled=True)
        gt, ge, gr = scatter(gt.reshape(D, -1), 0), scatter(ge.reshape(D, -1), 0), scatter(gr.reshape(FF, D), 0)
        gs, gb, t4 = scatter(gs, 1), scatter(gb, 1), lax.psum(t4, AXES)
    n, rr = expand_bias.shape[0], reduce_weight.shape[0]
    image = jax.ShapeDtypeStruct((2, TOK, D), BF16)
    shapes = [(rows, 3 * D), (rows, D), (rows, FF), (rr, D), (HEADS, EXT * EXT)] + [(rows,)] * 8 + [(n,)]
    out, dx, tr, mg, ex, re, table, *vec = pl.pallas_call(
        finish_kernel, out_shape=[image, image] + [jax.ShapeDtypeStruct(s, F32) for s in shapes],
        in_specs=[VM] * 9, out_specs=[VM] * (2 + len(shapes)), name="finish",
        compiler_params=pltpu.CompilerParams(vmem_limit_bytes=VMEM_LIMIT),
    )(jnp.asarray(TARGET), out, dx, gt, ge, gr, gs, gb, t4)
    return (out[:, None], dx[:, None], tr, mg, ex, re, *vec[:7], vec[8], vec[7], table.T)


def solution(mesh):
    image = P(None, AXES, None, None)
    rows = P(AXES, None)
    vec = P(AXES)
    return jax.shard_map(
        functools.partial(shards, mesh_dims(mesh)), mesh=mesh,
        in_specs=(image, P(None, AXES), image) + (rows,) * 4 + (vec,) * 9 + (P(),),
        out_specs=(image, image) + (rows,) * 4 + (vec,) * 9 + (P(),),
        check_vma=False)
```

```python
import math
import functools

import numpy as np
import jax
import jax.numpy as jnp
from jax import lax
from jax.experimental import pallas as pl
from jax.experimental.pallas import tpu as pltpu
from jax.sharding import PartitionSpec as P

D = 768
FF = 3072
HEADS = 24
HEAD_DIM = 32
WIN = 12
SIDE = 24
SHIFT = 6
TOK = SIDE * SIDE
ROWS = 2 * TOK
WT = WIN * WIN
EXT = 2 * WIN - 1
GROUPS = 3
GH = HEADS // GROUPS
GW = GH * HEAD_DIM
QL = GH * WT
SCALE = HEAD_DIM ** -0.5
MASKED = -1e30
EPS = 1e-5
F32 = jnp.float32
BF16 = jnp.bfloat16
VMEM_LIMIT = 63 << 20
AXES = ("dp", "fsdp")
MESH = pl.DeviceIdType.MESH
ANY = pl.BlockSpec(memory_space=pl.ANY)
VM = pl.BlockSpec(memory_space=pltpu.VMEM)
SM = pl.BlockSpec(memory_space=pltpu.SMEM)
every = slice(None)

NN = (((1,), (0,)), ((), ()))
NT = (((1,), (1,)), ((), ()))
TN = (((0,), (0,)), ((), ()))


def dot(a, b, dims=NN):
    return lax.dot_general(a, b, dims, preferred_element_type=F32)


def layout_constants():
    j = np.arange(WT)
    reg = lambda c: (c >= SIDE - WIN).astype(np.int32) + (c >= SIDE - SHIFT).astype(np.int32)
    raster, label = np.zeros((4, WT), np.int32), np.zeros((4, WT), np.int32)
    for w in range(4):
        rr = (w // 2) * WIN + j // WIN
        rc = (w % 2) * WIN + j % WIN
        raster[w] = ((rr + SHIFT) % SIDE) * SIDE + (rc + SHIFT) % SIDE
        label[w] = reg(rr) * 3 + reg(rc)
    target = np.full((4, WT), -1, np.int32)
    for p in range(4):
        r = j // WIN + (WIN - 1 if p // 2 == 0 else -1)
        s = j % WIN + (WIN - 1 if p % 2 == 0 else -1)
        target[p] = np.where((r >= 0) & (s >= 0), r * EXT + s, -1)
    spread = lambda v: np.broadcast_to(v.reshape(1, TOK), (8, TOK)).astype(np.int32)
    return np.broadcast_to(np.tile(label, (1, GH))[:, None, :], (4, 8, QL)).astype(np.int32), spread(target), spread(raster)


LABEL_Q, TARGET, RASTER_Q = layout_constants()


def fill_places(raster, label=None):
    j = lax.broadcasted_iota(jnp.int32, (WT, 128), 0)
    a = (j * 171) >> 11
    c = j - a * WIN
    reg = lambda v: (v >= SIDE - WIN).astype(jnp.int32) + (v >= SIDE - SHIFT).astype(jnp.int32)
    turn = lambda v: jnp.where(v >= SIDE - SHIFT, v + SHIFT - SIDE, v + SHIFT)
    for w in range(4):
        rr, rc = a + (w // 2) * WIN, c + (w % 2) * WIN
        raster[w] = turn(rr) * SIDE + turn(rc)
        if label is not None:
            label[w] = reg(rr) * 3 + reg(rc)


def lane_iota(shape):
    return lax.broadcasted_iota(jnp.int32, shape, len(shape) - 1)


def aligned(v, n):
    return v if isinstance(v, int) else pl.multiple_of(v, n)


def lanes(start, width):
    return pl.ds(aligned(start, 128), width)


def window(i):
    return pl.ds(aligned(i * WT, WT), WT)


def to_window(raster, w):
    return (raster[w][:, 0:1] == lane_iota((WT, TOK))).astype(BF16)


def to_raster(raster_q, m):
    t = lax.broadcasted_iota(jnp.int32, (WT, TOK), 0) + m * WT
    return (raster_q[0:1, :] == t).astype(BF16)


def stats(x):
    mean = jnp.mean(x, axis=-1, keepdims=True)
    center = x - mean
    var = jnp.mean(center * center, axis=-1, keepdims=True)
    inv = lax.rsqrt(var + EPS)
    return center * inv, inv


def head_stack(dst, x):
    lane = lane_iota(x.shape) // HEAD_DIM
    zero = jnp.zeros_like(x)
    for h in range(GH):
        dst[h * WT:(h + 1) * WT, :] = jnp.where(lane == h, x, zero)


def head_pick(o):
    lane = lane_iota((WT, GW)) // HEAD_DIM
    out = jnp.where(lane == 0, o[0:WT], 0.0)
    for h in range(1, GH):
        out = jnp.where(lane == h, o[h * WT:(h + 1) * WT], out)
    return out


def onehot(target_ref):
    t = lax.broadcasted_iota(jnp.int32, (EXT * EXT, 4 * WT), 0)
    return (t == target_ref[0:1, :]).astype(F32)


def table_rows(table_ref, target_ref, t4):
    t4[...] = lax.dot_general(table_ref[...], onehot(target_ref), NN,
                              precision=lax.Precision.HIGHEST, preferred_element_type=F32) * (1.0 / SCALE)


def spread_bias(g, t4, bias, rowbuf):
    a_of = (lane_iota((1, QL)) % WT) // WIN
    c_of = lane_iota((16, QL)) % WIN
    rows = []
    for p in range(4):
        acc = jnp.zeros((1, QL), F32)
        for h in range(GH):
            piece = t4[pl.ds(g * GH + h, 1), p * WT:(p + 1) * WT]
            piece = jnp.concatenate([piece, jnp.zeros((1, QL - WT), F32)], axis=1)
            acc = acc + (pltpu.roll(piece, h * WT, axis=1) if h else piece)
        rows.append(acc)
    for s in range(2):
        for b in range(WIN):
            pos = pltpu.roll(rows[s], WIN * b, axis=1) if b else rows[s]
            neg = pltpu.roll(rows[2 + s], (WIN * b - WT) % QL, axis=1)
            rowbuf[s, b:b + 1, :] = jnp.where(a_of >= b, pos, neg)
    for d in range(WIN):
        pos = pltpu.roll(rowbuf[0], d, axis=1) if d else rowbuf[0]
        neg = pltpu.roll(rowbuf[1], (d - WIN) % QL, axis=1)
        both = jnp.where(c_of >= d, pos, neg)
        for n in range(9):
            bias[g * 9 + n, pl.ds(d, WIN, stride=WIN), :] = both[0:WIN, n * 128:(n + 1) * 128]


def gather_bias(g, bgrad, accbuf, t4):
    a_of = (lane_iota((1, QL)) % WT) // WIN
    c_of = lane_iota((WIN, QL)) % WIN
    pos = jnp.zeros((WIN, QL), F32)
    neg = jnp.zeros((WIN, QL), F32)
    for d in range(WIN):
        r = jnp.concatenate([bgrad[n, pl.ds(d, WIN, stride=WIN), :] for n in range(9)], axis=1)
        p = jnp.where(c_of >= d, r, 0.0)
        pos = pos + (pltpu.roll(p, QL - d, axis=1) if d else p)
        if d:
            neg = neg + pltpu.roll(jnp.where(c_of < d, r, 0.0), WIN - d, axis=1)
    accbuf[0, 0:WIN, :] = pos
    accbuf[1, 0:WIN, :] = neg
    for s in range(2):
        pp = jnp.zeros((1, QL), F32)
        nn = jnp.zeros((1, QL), F32)
        for b in range(WIN):
            r = accbuf[s, b:b + 1, :]
            p = jnp.where(a_of >= b, r, 0.0)
            pp = pp + (pltpu.roll(p, QL - WIN * b, axis=1) if b else p)
            if b:
                nn = nn + pltpu.roll(jnp.where(a_of < b, r, 0.0), WT - WIN * b, axis=1)
        for part, row in ((s, pp), (2 + s, nn)):
            for h in range(GH):
                moved = pltpu.roll(row, QL - h * WT, axis=1) if h else row
                t4[pl.ds(g * GH + h, 1), part * WT:(part + 1) * WT] = moved[:, 0:WT]


ERF_SLOPE = 0.35
ERF_FIT = (0.19434814435164116, 0.235843067071591, -0.008625688056468914, 0.6849613674275746, -0.6811631064960405, 0.7727015621272543, -0.19806535099226122)


def gelu_pair(v):
    e = jnp.exp(v * v * -0.5)
    t = 1.0 / (1.0 + jnp.abs(v) * (ERF_SLOPE * math.sqrt(0.5)))
    poly = jnp.full_like(t, 0.5 * ERF_FIT[-1])
    for c in ERF_FIT[-2::-1]:
        poly = poly * t + 0.5 * c
    tail = poly * t * e
    cdf = jnp.where(v >= 0, 1.0 - tail, tail)
    return v * cdf, cdf + v * e * (1.0 / math.sqrt(2.0 * math.pi))


def norm_back(hat, inv, gain, grad):
    scaled = grad * gain
    return inv * (scaled - jnp.mean(scaled, axis=-1, keepdims=True)
                  - hat * jnp.mean(scaled * hat, axis=-1, keepdims=True))


class Place:
    def __init__(self, dims):
        self.nz, self.ny, self.nx = dims
        f = lax.axis_index("fsdp")
        self.z = lax.axis_index("dp")
        self.c = lax.rem(f, 2)
        self.x = lax.rem(f // 2, self.nx)
        self.y = f // (2 * self.nx)

    def size(self, axis):
        return {"z": self.nz, "y": self.ny, "x": self.nx, "c": 2}[axis]

    def at(self, axis):
        return {"z": self.z, "y": self.y, "x": self.x, "c": self.c}[axis]

    def step(self, axis, k):
        return lax.rem(self.at(axis) + k, self.size(axis))

    def back(self, axis, k):
        return self.step(axis, self.size(axis) - k)

    def device(self, axis, k):
        p = {a: (self.step(a, k) if a == axis else self.at(a)) for a in "zyxc"}
        return (p["z"], (p["y"] * self.nx + p["x"]) * 2 + p["c"])

    def greet(self):
        barrier = pltpu.get_barrier_semaphore()
        total = 0
        for axis in "czyx":
            for k in range(1, self.size(axis)):
                pl.semaphore_signal(barrier, inc=1, device_id=self.device(axis, k), device_id_type=MESH)
                total += 1
        pl.semaphore_wait(barrier, total)


def mesh_dims(mesh):
    chips = mesh.shape["fsdp"] // 2
    ny = max(n for n in range(1, chips + 1) if n * n <= chips and chips % n == 0)
    return mesh.shape["dp"], ny, chips // ny


class Swap:
    def __init__(self, place, axis, sems, src, dst, came, has=None):
        self.has = has
        self.place, self.axis, self.sems = place, axis, sems
        self.src, self.dst, self.came = src, dst, came

    def make(self, k, src, dst):
        return pltpu.make_async_remote_copy(
            src_ref=src(k), dst_ref=dst(k), send_sem=self.sems[0](k), recv_sem=self.sems[1](k),
            device_id=self.place.device(self.axis, k), device_id_type=MESH)

    def peers(self):
        return range(1, self.place.size(self.axis))

    def each(self, sender, act):
        for k in self.peers():
            if self.has is None:
                act(k)
            else:
                pl.when(self.has(sender(k)))(lambda k=k: act(k))

    def start(self):
        self.each(lambda k: self.place.at(self.axis), lambda k: self.make(k, self.src, self.dst).start())

    def arrive(self):
        self.each(lambda k: self.place.back(self.axis, k), lambda k: self.make(k, self.came, self.came).wait_recv())

    def done(self):
        self.each(lambda k: self.place.at(self.axis), lambda k: self.make(k, self.src, self.dst).wait_send())


def when(cond, body):
    if isinstance(cond, (bool, np.bool_)):
        if cond:
            body()
    else:
        pl.when(cond)(body)


def both(*conds):
    out = True
    for c in conds:
        if isinstance(c, (bool, np.bool_)):
            if not c:
                return False
        else:
            out = c if out is True else jnp.logical_and(out, c)
    return out


def call(kernel, outs, scratch, ins, name):
    return pl.pallas_call(
        kernel, out_shape=[jax.ShapeDtypeStruct(s, d) for s, d in outs], in_specs=[VM] * len(ins),
        out_specs=[VM] * len(outs), scratch_shapes=scratch, name=name,
        compiler_params=pltpu.CompilerParams(vmem_limit_bytes=VMEM_LIMIT))(*ins)


HALF = 4 * D
TM_HALF = 2 * D
FF_HALF = FF // 2
FF_PART = FF // 4


class Gather:
    def __init__(self, place, w, half, base, n_w, r, part, send, recv):
        self.place = place
        self.w, self.half, self.base, self.n_w, self.r, self.part = w, half, base, n_w, r, part
        self.send, self.recv = send, recv
        self.n = n_w + 3

    def block(self, wide, p, c):
        if wide:
            return (every, lanes(c * self.half + self.base + p * 256, 256))
        return (every, lanes(c * (D // 2) + p * 128, 128))

    def swap(self, wide, p, odd, s):
        pc = self.place
        ref = self.w if wide else self.r
        q = p if wide else self.n_w + p
        sems = (lambda k: self.send.at[q, s, k - 1], lambda k: self.recv.at[q, s, k - 1])
        blk = self.block(wide, p, pc.c)
        zs = every if wide else pl.ds(self.part * (pc.nz // 2), pc.nz // 2)
        at = lambda zz, yy, xx, b=blk: ref.at[(zz, yy, xx) + b]
        z, y, x = pc.z, pc.y, pc.x
        if s == 0:
            has = None if wide else (lambda zz: (zz >= pc.nz // 2) == (self.part == 1))
            own = lambda k: at(z, y, x)
            return Swap(pc, "z", sems, own, own, lambda k: at(pc.back("z", k), y, x), has)
        if s == 3:
            mine = lambda k: at(zs, every, every)
            return Swap(pc, "c", sems, mine, mine, lambda k: at(zs, every, every, self.block(wide, p, 1 - pc.c)))
        first = "y" if odd else "x"
        if s == 1:
            own = lambda k: at(zs, y, x)
            if first == "x":
                return Swap(pc, "x", sems, own, own, lambda k: at(zs, y, pc.back("x", k)))
            return Swap(pc, "y", sems, own, own, lambda k: at(zs, pc.back("y", k), x))
        if first == "x":
            own = lambda k: at(zs, y, every)
            return Swap(pc, "y", sems, own, own, lambda k: at(zs, pc.back("y", k), every))
        own = lambda k: at(zs, every, x)
        return Swap(pc, "x", sems, own, own, lambda k: at(zs, every, pc.back("x", k)))

    def on_piece(self, p, body):
        when(both(p >= 0, p < self.n_w), lambda: body(True, p))
        when(both(p >= self.n_w, p < self.n), lambda: body(False, p - self.n_w))

    def tick(self, u, odd, landed=None):
        def last(wide, p):
            self.swap(wide, p, odd, 3).arrive()
            if landed is not None:
                landed(wide, p)

        def step(s):
            def body(wide, p):
                if s:
                    self.swap(wide, p, odd, s - 1).arrive()
                self.swap(wide, p, odd, s).start()
            return body

        self.on_piece(u - 8, last)
        for s in (3, 2, 1, 0):
            self.on_piece(u - 2 * s, step(s))

    def finish(self):
        for q in range(self.n):
            for s in range(4):
                self.swap(q < self.n_w, q if q < self.n_w else q - self.n_w, q % 2 == 1, s).done()


def small_swap(pc, sb, send, recv, s):
    sems = (lambda k: send.at[s, k - 1], lambda k: recv.at[s, k - 1])
    at = lambda zz, yy, xx, c=pc.c: sb.at[zz, yy, xx, c]
    z, y, x = pc.z, pc.y, pc.x
    own = [lambda k: at(z, y, x), lambda k: at(every, y, x), lambda k: at(every, y, every),
           lambda k: at(every, every, every)][s]
    came = [lambda k: at(pc.back("z", k), y, x), lambda k: at(every, y, pc.back("x", k)),
            lambda k: at(every, pc.back("y", k), every), lambda k: at(every, every, every, 1 - pc.c)][s]
    return Swap(pc, "zxyc"[s], sems, own, own, came)


def place_small(sb, sv, eb, n_small, n_wide):
    nz, ny, nx = sb.shape[:3]
    for out, row0, width, total in ((sv, 0, n_small, D), (eb, 8, n_wide, FF)):
        tiles = [jnp.zeros((8, 128), F32) for _ in range(total // 128)]
        lane = lane_iota((8, 128))
        n = 0
        for q in range(nz * ny * nx):
            for c in range(2):
                blk = sb[q // (ny * nx), (q // nx) % ny, q % nx, c, row0:row0 + 8, :]
                tile, off = divmod(n * width, 128)
                moved = pltpu.roll(blk, off, axis=1) if off else blk
                end = off + width
                tiles[tile] = jnp.where((lane >= off) & (lane < min(end, 128)), moved, tiles[tile])
                if end > 128:
                    tiles[tile + 1] = jnp.where(lane < end - 128, moved, tiles[tile + 1])
                n += 1
        out[...] = jnp.concatenate(tiles, axis=1)


def group_cols(g):
    return (((0, g * 384, 256),), ((0, g * 384 + 256, 128), (1, g * 384, 128)), ((1, g * 384 + 128, 256),))


def merge_cols(n):
    return tuple((b // 3, 1152 + lax.rem(b, 3) * 128, 128) for b in (2 * n, 2 * n + 1))


def columns(ref, parts, half):
    take = [ref[:, lanes(h * half + lo, n)] for h, lo, n in parts]
    return take[0] if len(take) == 1 else jnp.concatenate(take, axis=1)


class Flat:
    def __init__(self, ref):
        self.ref = ref

    def __getitem__(self, idx):
        v = self.ref[:, :, :, :, idx[1]]
        return v.reshape(-1, v.shape[-1])


def own_halves(h):
    for g in range(GROUPS):
        yield 0, g * GW + h * 2 * D, g * 384 + h * 128, 256
        yield 0, D + g * GW + h * 128, g * 384 + 256 * (1 - h), 128
    yield 1, h * (D // 2), 1152, D // 2
    for s in range(2):
        yield 2, s * FF_HALF + h * FF_PART, TM_HALF + s * FF_PART, FF_PART
    yield 3, h * (D // 2), 0, D // 2


def forward_kernel(near, dims, counts, x, labq, target, table, *rest):
    n_in = 13 if near else 4
    given = rest[:n_in]
    (o_w, o_r, o_triple, o_pt, o_att, o_mixed, o_n2, o_normed, o_xp, sv, eb, o_ew, o_er,
     w, r, sb, stage_w, stage_r, xp, normed, triple, attended, mixed, n2, pt, t4, bias, rowbuf, qs, st, lk, raster, labk,
     send, recv, ssend, srecv, lsem, psem) = rest[n_in:]

    def keep(n, src, dst):
        return pltpu.make_async_copy(src, dst, lsem.at[n])

    if near:
        pc = Place(dims)
        gather = Gather(pc, w, HALF, 0, 9, r, 0, send, recv)

    def part_of(wide, p):
        zs = every if wide else pl.ds(0, dims[0] // 2)
        for c in range(2):
            n = 2 * (p if wide else 9 + p) + c
            blk = (zs, every, every) + gather.block(wide, p, c)
            yield (keep(n, w.at[blk], o_w.at[blk]) if wide else keep(n, r.at[blk], o_r.at[blk]))

    def landed(wide, p):
        for copy in part_of(wide, p):
            copy.start()

    def small_tick(u):
        if u:
            small_swap(pc, sb, ssend, srecv, u // 2 - 1).arrive()
        if u < 8:
            small_swap(pc, sb, ssend, srecv, u // 2).start()

    if near:
        pc.greet()
        own, vectors = given[:4], given[4:]
        first = []
        for i, ((n, src, dst, width), (_, _, back, _)) in enumerate(zip(own_halves(1 - pc.c), own_halves(pc.c))):
            ref, stage = own[n], (stage_r if n == 3 else stage_w)
            rows = lambda c, m=ref.shape[0]: pl.ds(aligned(c * m, 8), m)
            sems = (lambda k, i=i: ssend.at[4 + i, 0], lambda k, i=i: srecv.at[4 + i, 0])
            first.append(Swap(pc, "c", sems, lambda k, v=ref.at[:, lanes(src, width)]: v,
                              lambda k, v=stage.at[rows(pc.c), lanes(dst, width)]: v,
                              lambda k, v=stage.at[rows(1 - pc.c), lanes(back, width)]: v))
        for s in first:
            s.start()
        sb[pc.z, pc.y, pc.x, pc.c] = jnp.zeros((16, 128), F32)
        for k, v in enumerate(vectors):
            sb[pc.z, pc.y, pc.x, pc.c, k, 0:v.shape[0]] = v[...].astype(BF16).astype(F32)
        for n, src, dst, width in own_halves(pc.c):
            ref, stage = own[n], (stage_r if n == 3 else stage_w)
            stage[pl.ds(aligned(pc.c * ref.shape[0], 8), ref.shape[0]), lanes(dst, width)] = ref[:, lanes(src, width)]
        for s in first[:-1]:
            s.arrive()
        w[pc.z, pc.y, pc.x, :, lanes(pc.c * HALF, HALF)] = stage_w[...].astype(BF16)
        gather.tick(0, False)
        small_tick(0)
        gather.tick(1, True)
        first[-1].arrive()
        r[pc.z, pc.y, pc.x, :, lanes(pc.c * (D // 2), D // 2)] = stage_r[...].astype(BF16)
        o_ew[...] = stage_w[:, TM_HALF + FF_PART:HALF].astype(BF16)
        o_er[...] = stage_r[...].astype(BF16)
    else:
        wown, rown, sv_in, eb_in = given
        loads = [keep(0, wown, w), keep(1, rown, r)]
        for c in loads:
            c.start()
        for c in loads:
            c.wait()
        sv[...] = sv_in[...]
        eb[...] = eb_in[...]

    def permute(i, _):
        xp[window(i), :] = dot(to_window(raster, i % 4), x[i // 4]).astype(BF16)
        return 0

    fill_places(raster, labk)
    table_rows(table, target, t4)

    def prologue(u, _):
        if near:
            for odd in range(2):
                pl.when(u % 2 == odd)(lambda odd=odd: gather.tick(u, odd == 1, landed))
            for k in range(1, 5):
                pl.when(u == 2 * k)(lambda k=k: small_tick(2 * k))

        @pl.when(u < 5)
        def _():
            spread_bias(u - 2, t4, bias, rowbuf)

        @pl.when(jnp.logical_and(u >= 5, u < 9))
        def _():
            lax.fori_loop(2 * (u - 5), 2 * (u - 4), permute, 0)

        return 0

    lax.fori_loop(2, 10, prologue, 0)
    if near:
        place_small(sb, sv, eb, given[0].shape[0], given[3].shape[0])

    def ln1(i, _):
        hat, _i = stats(xp[window(i), :].astype(F32))
        normed[window(i), :] = (hat * sv[0:1, :] + sv[1:2, :]).astype(BF16)
        return 0

    lax.fori_loop(0, 8, ln1, 0)
    keep(24, xp, o_xp).start()
    keep(25, normed, o_normed).start()
    wf = Flat(w)

    def products(i, g, u):
        rows, v = window(i), i % 4
        lk[u] = jnp.where(raster[v] < counts[i // 4], labk[v], -1)
        head_stack(qs.at[u], triple[rows, lanes(g * D, GW)])
        st[u] = dot(triple[rows, lanes(g * D + GW, GW)], qs[u], NT)

    def softmax(i, g, u):
        for n in range(9):
            c = lanes(n * 128, 128)
            s = st[u, :, c] + bias[g * 9 + n]
            s = jnp.where(lk[u] == labq[i % 4, 0:1, c], s, MASKED)
            m = jnp.max(s, axis=0, keepdims=True)
            e = jnp.exp((s - m) * SCALE)
            tot = jnp.sum(e, axis=0, keepdims=True)
            pt[u, :, c] = (e * (1.0 / tot)).astype(BF16)

    def attend(i, g, u):
        rows = window(i)
        pltpu.make_async_copy(pt.at[u], o_pt.at[g * 8 + i], psem.at[u]).start()
        out = head_pick(dot(pt[u], triple[rows, lanes(g * D + 2 * GW, GW)], TN))
        valid = raster[i % 4] < counts[i // 4]
        vq = jnp.concatenate([valid, valid], axis=1)
        attended[rows, lanes(g * GW, GW)] = jnp.where(vq, out, 0.0).astype(BF16)

    def quarter(q, _):
        g = q // 4

        @pl.when(q % 4 == 0)
        def _():
            for k, parts in enumerate(group_cols(g)):
                v = dot(normed[...], columns(wf, parts, HALF))
                if k != 1:
                    v = v + sv[2 + k // 2:3 + k // 2, lanes(g * GW, GW)]
                triple[:, lanes(g * D + k * GW, GW)] = v.astype(BF16)

        @pl.when(q >= 1)
        def _():
            for u in range(2):
                pltpu.make_async_copy(pt.at[u], o_pt.at[0], psem.at[u]).wait()

        i = 2 * lax.rem(q, 4)
        products(i, g, 0)
        products(i + 1, g, 1)
        softmax(i, g, 0)
        attend(i, g, 0)
        softmax(i + 1, g, 1)
        attend(i + 1, g, 1)
        if near:
            for odd in range(2):
                pl.when(q % 2 == odd)(lambda odd=odd: gather.tick(10 + q, odd == 1, landed))
        return 0

    lax.fori_loop(0, 4 * GROUPS, quarter, 0)
    keep(26, triple, o_triple).start()
    keep(27, attended, o_att).start()
    def merge(n, _):
        cols = lanes(n * 256, 256)
        v = dot(attended[...], columns(wf, merge_cols(n), HALF))
        mixed[:, cols] = xp[:, cols].astype(F32) + v + sv[4:5, cols]
        return 0

    lax.fori_loop(0, 3, merge, 0)
    keep(28, mixed, o_mixed).start()

    def ln2(i, _):
        hat, _i = stats(mixed[window(i), :])
        n2[window(i), :] = (hat * sv[5:6, :] + sv[6:7, :]).astype(BF16)
        return 0

    lax.fori_loop(0, 8, ln2, 0)
    keep(29, n2, o_n2).start()
    if near:
        gather.finish()
        for s in first:
            s.done()
        for s in range(4):
            small_swap(pc, sb, ssend, srecv, s).done()
        for q in range(12):
            for copy in part_of(q < 9, q if q < 9 else q - 9):
                copy.wait()
    for n, src, dst in ((24, xp, o_xp), (25, normed, o_normed), (26, triple, o_triple), (27, attended, o_att),
                        (28, mixed, o_mixed), (29, n2, o_n2)):
        keep(n, src, dst).wait()
    for slot in range(2):
        pltpu.make_async_copy(pt.at[slot], o_pt.at[0], psem.at[slot]).wait()


def forward(near, dims, counts, x, table, *given):
    nz, ny, nx = dims if near else (1, 1, 1)
    rw, rr = (given[0].shape[0] * 2, given[3].shape[0] * 2) if near else (D, FF)
    peers = max(nz, ny, nx, 2) - 1
    full_w, full_r = (nz, ny, nx, rw, 2 * HALF), (nz, ny, nx, rr, D)
    tiny = (8, 128)
    outs = [(full_w if near else tiny, BF16), (full_r if near else tiny, BF16), ((ROWS, 3 * D), BF16),
            ((8 * GROUPS, WT, QL), BF16), ((ROWS, D), BF16), ((ROWS, D), F32), ((ROWS, D), BF16), ((ROWS, D), BF16),
            ((ROWS, D), BF16), ((8, D), F32), ((8, FF), F32), ((rw, FF_PART) if near else tiny, BF16),
            ((rr, D // 2) if near else tiny, BF16)]
    if not near:
        given = (given[0].reshape(full_w), given[1].reshape(full_r)) + given[2:]
    vm = pltpu.VMEM
    dma = pltpu.SemaphoreType.DMA
    scratch = [vm(full_w, BF16), vm(full_r, BF16), vm((nz, ny, nx, 2, 16, 128), F32), vm((rw if near else 8, HALF), F32),
               vm((rr if near else 8, D // 2), F32), vm((ROWS, D), BF16), vm((ROWS, D), BF16), vm((ROWS, 3 * D), BF16),
               vm((ROWS, D), BF16), vm((ROWS, D), F32), vm((ROWS, D), BF16), vm((2, WT, QL), BF16),
               vm((HEADS, 4 * WT), F32), vm((GROUPS * 9, WT, 128), F32), vm((2, 16, QL), F32), vm((2, QL, GW), BF16),
               vm((2, WT, QL), F32), vm((2, WT, 128), jnp.int32), vm((4, WT, 128), jnp.int32), vm((4, WT, 128), jnp.int32),
               dma((12, 4, peers)), dma((12, 4, peers)), dma((14, peers)), dma((14, peers)), dma((30,)), dma((2,))]
    params = dict(collective_id=0, has_side_effects=True) if near else {}
    return pl.pallas_call(
        functools.partial(forward_kernel, near, dims),
        out_shape=[jax.ShapeDtypeStruct(s, d) for s, d in outs],
        in_specs=[SM] + [VM] * 4 + ([VM] * 13 if near else [ANY, ANY, VM, VM]),
        out_specs=[ANY] * 9 + [VM] * 4,
        scratch_shapes=scratch, name="forward",
        compiler_params=pltpu.CompilerParams(vmem_limit_bytes=VMEM_LIMIT, **params),
    )(counts, x, jnp.asarray(LABEL_Q), jnp.asarray(TARGET), table.T,
      *given)


class Scatter:
    def __init__(self, place, bufs, send, recv):
        self.place = place
        self.bufs, self.send, self.recv = bufs, send, recv

    def src(self, kind, g, i, ab, c):
        if kind == "r":
            n = g.shape[3] // 2
            return g.at[every, every, every, pl.ds(ab * n, n), lanes(c * (D // 2) + i * 128, 128)]
        return g.at[every, every, every, every, lanes(c * FF_HALF + i * 256 + ab * 128, 128)]

    def swap(self, kind, g, out, i, ab, s):
        pc = self.place
        r0, r1, r2, r3, fin = self.bufs[kind]
        q = {"e": 0, "t": 6, "r": 12}[kind] + i
        sems = (lambda k: self.send.at[q, ab, s, k - 1], lambda k: self.recv.at[q, ab, s, k - 1])
        first, second = ("y", "x") if ab == 0 else ("x", "y")
        if s == 0:
            to = lambda k: r0.at[i, ab]
            return Swap(pc, "c", sems, lambda k: self.src(kind, g, i, ab, 1 - pc.c), to, to)
        if s == 1:
            to = lambda k: r1.at[i, ab, k - 1]
            at = lambda k: (every, pc.step("y", k), every) if first == "y" else (every, every, pc.step("x", k))
            return Swap(pc, first, sems, lambda k: r0.at[(i, ab) + at(k)], to, to)
        if s == 2:
            to = lambda k: r2.at[i, ab, k - 1]
            return Swap(pc, second, sems, lambda k: r1.at[i, ab, 0, every, pc.step(second, k)], to, to)
        if s == 3:
            to = lambda k: r3.at[i, ab, k - 1]
            return Swap(pc, "z", sems, lambda k: r2.at[i, ab, 0, pc.step("z", k)], to, to)
        n = out.shape[0]
        if kind == "r":
            cols = lambda c: lanes(c * (D // 2) + i * 128, 128)
            return Swap(pc, "c", sems, lambda k: fin.at[i, 1 - pc.c], lambda k: out.at[:, cols(pc.c)],
                        lambda k: out.at[:, cols(1 - pc.c)])
        cols = lambda c: lanes(c * FF_HALF + i * 256 + ab * 128, 128)
        return Swap(pc, "c", sems, lambda k: fin.at[i, ab, pl.ds(aligned((1 - pc.c) * n, 8), n), :],
                    lambda k: out.at[:, cols(pc.c)], lambda k: out.at[:, cols(1 - pc.c)])

    def advance(self, kind, g, out, i, s):
        pc = self.place
        r0, r1, r2, r3, fin = self.bufs[kind]
        if s == 5:
            for ab in range(1 if kind == "r" else 2):
                self.swap(kind, g, out, i, ab, 4).arrive()
            return
        for ab in range(2):
            first, second = ("y", "x") if ab == 0 else ("x", "y")
            if s:
                self.swap(kind, g, out, i, ab, s - 1).arrive()
            if s == 1:
                n = r0.shape[-2]

                def add(z, _):
                    if kind == "r":
                        own = g[z, :, :, ab * n:(ab + 1) * n, lanes(pc.c * (D // 2) + i * 128, 128)]
                    else:
                        own = g[z, :, :, :, lanes(pc.c * FF_HALF + i * 256 + ab * 128, 128)]
                    r0[i, ab, z] = (r0[i, ab, z].astype(F32) + own.astype(F32)).astype(BF16)
                    return 0

                lax.fori_loop(0, pc.nz, add, 0)
            if s == 2:
                at = (every, pc.y, every) if first == "y" else (every, every, pc.x)
                v = r0[(i, ab) + at].astype(F32)
                for k in range(pc.size(first) - 1):
                    v = v + r1[i, ab, k].astype(F32)
                r1[i, ab, 0] = v.astype(BF16)
            if s == 3:
                v = r1[i, ab, 0, :, pc.at(second)].astype(F32)
                for k in range(pc.size(second) - 1):
                    v = v + r2[i, ab, k].astype(F32)
                r2[i, ab, 0] = v.astype(BF16)
            if s == 4:
                v = r2[i, ab, 0, pc.z].astype(F32)
                for k in range(pc.nz - 1):
                    v = v + r3[i, ab, k].astype(F32)
                fin[i, ab] = v
                if kind != "r":
                    n = out.shape[0]
                    out[:, lanes(pc.c * FF_HALF + i * 256 + ab * 128, 128)] = fin[i, ab, pl.ds(aligned(pc.c * n, 8), n), :]
            if s < 4 or kind != "r":
                self.swap(kind, g, out, i, ab, s).start()
        if s == 4 and kind == "r":
            out[:, lanes(pc.c * (D // 2) + i * 128, 128)] = fin[i, pc.c]
            self.swap(kind, g, out, i, 0, 4).start()

    def done(self, kind, g, out, pieces, steps):
        for i in range(pieces):
            for s in steps:
                for ab in range(1 if (kind == "r" and s == 4) else 2):
                    self.swap(kind, g, out, i, ab, s).done()


class SmallSum:
    def __init__(self, place, slots, send, recv):
        self.place, self.slots, self.send, self.recv = place, slots, send, recv

    def base(self, i):
        return sum(self.place.size(a) for a in "cyxz"[:i])

    def swap(self, i):
        pc, a = self.place, "cyxz"[i]
        sems = (lambda k: self.send.at[i, k - 1], lambda k: self.recv.at[i, k - 1])
        me = lambda k: self.slots.at[self.base(i) + pc.at(a)]
        return Swap(pc, a, sems, me, me, lambda k: self.slots.at[self.base(i) + pc.back(a, k)])

    def start(self):
        self.swap(0).start()

    def advance(self, i):
        self.swap(i).arrive()
        s = self.slots[self.base(i)]
        for k in range(1, self.place.size("cyxz"[i])):
            s = s + self.slots[self.base(i) + k]
        if i == 3:
            return s
        self.slots[self.base(i + 1) + self.place.at("cyxz"[i + 1])] = s
        self.swap(i + 1).start()

    def done(self):
        for i in range(4):
            self.swap(i).done()


def events(t):
    out = [("e", i, s) for i in range(6) for s in range(6) if 2 * i + 1 + 2 * s == t and t >= 12]
    for i, at in enumerate(((12, 14, 16, 18, 20, 22), (13, 15, 17, 19, 21, 23), (14, 15, 18, 20, 22, 24))):
        out += [("r", i, s) for s in range(6) if at[s] == t]
    for pieces, at in (((5,), (16, 18, 20, 22, 24, 26)), ((3, 4), (19, 20, 22, 23, 25, 26)), ((2,), (21, 22, 24, 25, 27, 28)),
                       ((0, 1), (23, 24, 26, 27, 29, 30))):
        out += [("t", i, s) for i in pieces for s in range(6) if at[s] == t]
    return sorted(out, key=lambda e: -e[2])


def backward_kernel(near, dims, counts, rasq, do, w, r, own_ew, own_er, triple_h, pt_h, att_h, mixed_h, n2_h, normed_h,
                    xp_h, sv, eb, o_out, o_dx, o_act, o_t, o_e, o_r, o_small, o_deb, o_t4,
                    raster, ew, rw, dop, dn2, mixed, part, e0, e1, e2, e3, ef, t0, t1, t2, t3, tf, b0, b1, b2, b3, bf, slots_a, slots_g, late, slots_l, sums_g, smalls,
                    gsend, grecv, send, recv, ssend, srecv, lsem):
    def load(n, src, dst):
        return pltpu.make_async_copy(src, dst, lsem.at[n])

    if near:
        pc = Place(dims)
        rs = Scatter(pc, {"e": (e0, e1, e2, e3, ef), "t": (t0, t1, t2, t3, tf), "r": (b0, b1, b2, b3, bf)}, send, recv)
        sum_a = SmallSum(pc, slots_a, ssend.at[0], srecv.at[0])
        sum_l = SmallSum(pc, slots_l, ssend.at[1], srecv.at[1])
        sum_g = lambda g: SmallSum(pc, slots_g.at[g], ssend.at[2 + g], srecv.at[2 + g])
        pc.greet()
    else:
        pc = None
    small = smalls
    fill_places(raster)
    small[...] = jnp.zeros(small.shape, F32)

    def feed_forward(n2, n2t, act, hs, ds, hl, de, dr):
        half_z = dims[0] // 2
        loads = [load(0, n2_h, n2), load(3, mixed_h, mixed)]
        if near:
            for c in range(2):
                a, b = lanes(c * HALF + TM_HALF, FF_PART), lanes(c * FF_HALF, FF_PART)
                loads.append(load(4 + c, w.at[:, :, :, :, a], ew.at[:, :, :, :, b]))
            loads.append(load(2, r.at[0:half_z], rw.at[0:half_z]))
        else:
            for c in range(2):
                a, b = lanes(c * HALF + TM_HALF, FF_HALF), lanes(c * FF_HALF, FF_HALF)
                loads.append(load(4 + c, w.at[:, :, :, :, a], ew.at[:, :, :, :, b]))
            loads.append(load(2, r, rw))
        for c in loads:
            c.start()
        if near:
            gather = Gather(pc, ew, FF_HALF, FF_PART, 3, rw, 1, gsend, grecv)
            ew[pc.z, pc.y, pc.x, :, lanes(pc.c * FF_HALF + FF_PART, FF_PART)] = own_ew[...]

            @pl.when(pc.z >= half_z)
            def _():
                rw[pc.z, pc.y, pc.x, :, lanes(pc.c * (D // 2), D // 2)] = own_er[...]

            gather.tick(0, False)
            gather.tick(1, True)

        def permute(i, _):
            dop[window(i), :] = dot(to_window(raster, i % 4), do[i // 4]).astype(BF16)
            return 0

        lax.fori_loop(0, 8, permute, 0)
        if near:
            gather.tick(2, False)
            gather.tick(3, True)
        for c in loads:
            c.wait()
        n2t[...] = n2[...].T
        dn2[...] = jnp.zeros(dn2.shape, F32)
        small[7:8, :] = jnp.sum(dop[...].astype(F32), axis=0, keepdims=True)
        nz, ny, nx, rr = rw.shape[:4]
        per = FF // 256

        def rows_of(n0):
            return flat_r[pl.ds(aligned(n0, 256), 256), :]

        flat_r = rw.reshape(FF, D)
        fe, fde = Flat(ew), de

        def chunk(j, _):
            s, k = j // 6, j % 6
            c, off = k % 2, k // 2
            col = lanes(c * FF_HALF + s * FF_PART + off * 256, 256)
            n0 = s * FF_HALF + c * FF_PART + off * 256
            nat = lanes(n0, 256)
            weights = fe[:, col]
            rows = rows_of(n0)
            bias = eb[0:1, nat]
            total = jnp.zeros((8, 256), F32)

            def products(m):
                rows_m = pl.ds(m * 288, 288)
                hs[rows_m, :] = dot(n2[rows_m, :], weights)
                ds[rows_m, :] = dot(dop[rows_m, :], rows, NT)

            def gate(m, total):
                for q in range(288 // 32):
                    rr_ = pl.ds(m * 288 + q * 32, 32)
                    a, slope = gelu_pair(hs[rr_, :] + bias)
                    act[rr_, nat] = a.astype(BF16)
                    hg = ds[rr_, :] * slope
                    for p in range(4):
                        total = total + hg[p * 8:(p + 1) * 8]
                    hl[rr_, :] = hg.astype(BF16)
                return total

            products(0)
            for m in range(4):
                if m + 1 < 4:
                    products(m + 1)
                total = gate(m, total)
            small[pl.ds(8 + s * 2 + c, 1), lanes(off * 256, 256)] = jnp.sum(total, axis=0, keepdims=True)
            de[:, :, :, :, col] = dot(n2t[...], hl[...]).astype(BF16).reshape(de.shape[:4] + (256,))
            for n in range(3):
                cc = lanes(n * 256, 256)
                dn2[:, cc] += dot(hl[...], weights[n * 256:(n + 1) * 256], NT)
            if near:
                gather.tick(4 + 2 * j, False)
                gather.tick(5 + 2 * j, True)
                for step in range(5, -1, -1):
                    i = j // 2 - step
                    pl.when(jnp.logical_and(lax.rem(j, 2) == 1, i >= 0))(
                        lambda i=i, step=step: rs.advance("e", de, o_e, i, step))
            return 0

        lax.fori_loop(0, per, chunk, 0)

        def er_tick(t):
            for kind, i, s in events(t):
                rs.advance(kind, de if kind == "e" else dr, o_e if kind == "e" else o_r, i, s)

        spill = load(6, act, o_act)
        spill.start()
        flat_dr = dr.reshape(FF, D)

        def reduce_part(n, _):
            def quarter(m, _):
                two = jnp.concatenate([dop[:, lanes(n * 128, 128)], dop[:, lanes(D // 2 + n * 128, 128)]], axis=1)
                v = dot(act[:, lanes(m * D, D)], two, TN).astype(BF16)
                rows = pl.ds(aligned(m * D, D), D)
                flat_dr[rows, lanes(n * 128, 128)] = v[:, :128]
                flat_dr[rows, lanes(D // 2 + n * 128, 128)] = v[:, 128:]
                return 0

            lax.fori_loop(0, 4, quarter, 0)
            if near:
                for t in range(3):
                    pl.when(n == t)(lambda t=t: er_tick(12 + t))
            return 0

        lax.fori_loop(0, 3, reduce_part, 0)

        def ln2b(i, _):
            rows = window(i)
            hat, inv = stats(mixed[rows, :])
            g = dn2[rows, :]
            small[5:6, :] += jnp.sum(g * hat, axis=0, keepdims=True)
            small[6:7, :] += jnp.sum(g, axis=0, keepdims=True)
            m = dop[rows, :].astype(F32) + norm_back(hat, inv, sv[5:6, :], g)
            small[4:5, :] += jnp.sum(m, axis=0, keepdims=True)
            mixed[rows, :] = m
            part[rows, :] = m.astype(BF16)
            return 0

        lax.fori_loop(0, 8, ln2b, 0)
        if near:
            er_tick(15)
            gather.finish()
            rs.done("e", de, o_e, 6, range(1))
            rs.done("r", dr, o_r, 3, range(1))
        else:
            for c in (load(4, de, o_e), load(5, dr, o_r)):
                c.start()
                c.wait()
        spill.wait()

    nz, ny, nx, rw_rows = w.shape[:4]
    rr_rows = r.shape[3]
    vm = pltpu.VMEM
    pl.run_scoped(feed_forward, vm((ROWS, D), BF16),
                  vm((D, ROWS), BF16), vm((ROWS, FF), BF16), vm((ROWS, 256), F32), vm((ROWS, 256), F32), vm((ROWS, 256), BF16),
                  vm((nz, ny, nx, rw_rows, FF), BF16), vm((nz, ny, nx, rr_rows, D), BF16))
    tw = ew
    flat_tw = tw.reshape(D, FF)
    flat_r = rw.reshape(FF, D)

    def after_feed_forward(dt, triple, ml, xp, t4g, sum_keep):
        def ert_tick(t):
            if near:
                for kind, i, s in events(t):
                    rs.advance(kind, {"e": None, "r": None, "t": dt}[kind], {"e": o_e, "r": o_r, "t": o_t}[kind], i, s)

        def put(parts, v):
            at = 0
            for h, lo, n in parts:
                dt[:, :, :, :, lanes(h * TM_HALF + lo, n)] = v[:, at:at + n].reshape(dt.shape[:4] + (n,))
                at += n

        def group_sum(g, m):
            total = sum_g(g).advance(m)
            if total is not None:
                sums_g[g] = total

        def attention(datt, xt, xn, qs, dos, st, raw, pt, bgrad, accbuf, psem):
            loads = [load(0, att_h, xn), load(1, triple_h, triple), load(2, xp_h, xp)]
            loads += [load(4 + c, w.at[:, :, :, :, lanes(c * HALF, TM_HALF)], tw.at[:, :, :, :, lanes(c * TM_HALF, TM_HALF)])
                      for c in range(2)]
            for c in loads:
                c.start()

            def fetch(step):
                return pltpu.make_async_copy(pt_h.at[(2 - step // 8) * 8 + step % 8], pt.at[step % 4], psem.at[step % 4])

            fetch(0).start()
            fetch(1).start()
            for c in loads:
                c.wait()
            xt[...] = xn[...].T
            again = load(0, normed_h, xn)
            again.start()

            def merge_grad(n, _):
                put(merge_cols(n), dot(xt[...], part[:, lanes(n * 256, 256)]).astype(BF16))
                return 0

            lax.fori_loop(0, 3, merge_grad, 0)
            ert_tick(16)

            def merge_back(n, _):
                rows = pl.ds(aligned(n * 256, 256), 256)
                m = jnp.concatenate([flat_tw[rows, 1152:TM_HALF], flat_tw[rows, TM_HALF + 1152:]], axis=1)
                datt[:, lanes(n * 256, 256)] = dot(part[...], m, NT).astype(BF16)
                return 0

            lax.fori_loop(0, 3, merge_back, 0)
            again.wait()
            xt[...] = xn[...].T
            ert_tick(17)
            if near:
                slots_a[pc.c, 0:4, :] = small[4:8, :]
                slots_a[pc.c, 4:8, :] = small[8:12, :]
                sum_a.start()

            def place_of(step):
                i = step % 8
                return window(i), raster[i % 4] < counts[i // 4]

            def products(step, g, u):
                rows, valid = place_of(step)
                vq = jnp.concatenate([valid, valid], axis=1)
                da = datt[rows, lanes(g * GW, GW)]
                da = jnp.where(vq, da.astype(F32), 0.0).astype(BF16)
                head_stack(qs.at[u], triple[rows, lanes(g * D, GW)])
                head_stack(dos.at[u], da)
                st[u] = dot(triple[rows, lanes(g * D + 2 * GW, GW)], dos[u], NT)

            def softmax_back(slot, u):
                for n in range(9):
                    c = lanes(n * 128, 128)
                    p = pt[slot, :, c].astype(F32)
                    d = st[u, :, c]
                    inner = jnp.sum(p * d, axis=0, keepdims=True)
                    s = p * (d - inner)
                    bgrad[n] += s
                    raw[u, :, c] = (s * SCALE).astype(BF16)

            def grads(step, g, slot, u):
                rows, _ = place_of(step)
                col = lambda k: lanes(g * D + k * GW, GW)
                key = triple[rows, col(1)]
                triple[rows, col(2)] = dot(pt[slot], dos[u]).astype(BF16)
                triple[rows, col(1)] = dot(raw[u], qs[u]).astype(BF16)
                triple[rows, col(0)] = head_pick(dot(raw[u], key, TN)).astype(BF16)

            def pair(p, g):
                step, slot = 2 * p, 2 * lax.rem(p, 2)

                @pl.when(p < 11)
                def _():
                    fetch(step + 2).start()
                    fetch(step + 3).start()

                products(step, g, 0)
                products(step + 1, g, 1)
                fetch(step).wait()
                fetch(step + 1).wait()
                softmax_back(slot, 0)
                grads(step, g, slot, 0)
                softmax_back(slot + 1, 1)
                grads(step + 1, g, slot + 1, 1)

            def half_group(q, _):
                g = 2 - q // 2

                @pl.when(q % 2 == 0)
                def _():
                    bgrad[...] = jnp.zeros(bgrad.shape, F32)

                lax.fori_loop(0, 2, lambda j, _: (pair(q * 2 + j, g), 0)[1], 0)

                @pl.when(q % 2 == 1)
                def _():
                    gather_bias(g, bgrad, accbuf, t4g)
                    for k, parts in enumerate(group_cols(g)):
                        v = triple[:, lanes(g * D + k * GW, GW)]
                        if k != 1:
                            small[2 + k // 2:3 + k // 2, lanes(g * GW, GW)] = jnp.sum(v.astype(F32), axis=0, keepdims=True)
                        put(parts, dot(xt[...], v).astype(BF16))

                if near:
                    for t in range(18, 24):
                        if events(t):
                            pl.when(q == t - 18)(lambda t=t: ert_tick(t))
                    for m in range(4):
                        k = (q - 2 - m) // 2

                        def more(k=k, m=m):
                            total = sum_g(2 - k).advance(m)
                            if total is not None:
                                sums_g[2 - k] = total

                        pl.when(jnp.logical_and(q - 2 - m >= 0, lax.rem(q + 10 - m, 2) == 0))(more)
                    for m, at in enumerate((0, 2, 4)):
                        pl.when(q == at)(lambda m=m: sum_a.advance(m) and None)

                    @pl.when(q % 2 == 1)
                    def _():
                        own = slots_g.at[g, pc.c]
                        own[...] = jnp.zeros(own.shape, F32)
                        own[0:8, 0:4 * WT] = t4g[pl.ds(aligned(g * GH, GH), GH), :]
                        for k in range(2):
                            own[8 + k:9 + k, 0:GW] = small[2 + k:3 + k, lanes(g * GW, GW)]
                        sum_g(g).start()
                return 0

            lax.fori_loop(0, 2 * GROUPS, half_group, 0)
        def rest(act):
            again = load(0, o_act, act)
            again.start()

            def normed_grad(n, _):
                rows = pl.ds(aligned(n * 256, 256), 256)
                weights = jnp.concatenate([flat_tw[rows, h * TM_HALF + lo:h * TM_HALF + lo + m]
                                           for g in range(GROUPS) for p in group_cols(g) for h, lo, m in p], axis=1)
                dn2[:, lanes(n * 256, 256)] = dot(triple[...], weights, NT)
                if near:
                    for t in range(2):
                        @pl.when(n == t)
                        def _(t=t):
                            ert_tick(24 + t)
                            group_sum(1, t + 2)
                            if t == 1:
                                group_sum(0, 0)
                return 0

            lax.fori_loop(0, 3, normed_grad, 0)

            def ln1b(i, _):
                rows = window(i)
                hat, inv = stats(xp[rows, :].astype(F32))
                g = dn2[rows, :]
                late[0:1, :] += jnp.sum(g * hat, axis=0, keepdims=True)
                late[1:2, :] += jnp.sum(g, axis=0, keepdims=True)
                ml[rows, :] = (mixed[rows, :] + norm_back(hat, inv, sv[0:1, :], g)).astype(BF16)
                return 0

            late[...] = jnp.zeros(late.shape, F32)
            lax.fori_loop(0, 8, ln1b, 0)
            if near:
                slots_l[pc.c] = late[0:2, :]
                sum_l.start()
                ert_tick(26)
                group_sum(0, 1)
                sum_keep[...] = sum_a.advance(3)
            mixed_again = load(3, mixed_h, mixed)
            mixed_again.start()

            def back_to_raster(src, dst):
                def block(k, _):
                    b, m = k // 4, k % 4
                    dst[window(k), :] = dot(to_raster(rasq, m), src[pl.ds(aligned(b * TOK, TOK), TOK), :]).astype(BF16)
                    return 0

                lax.fori_loop(0, 8, block, 0)

            back_to_raster(ml, part)
            saves = [load(4 + b, part.at[b * TOK:(b + 1) * TOK, :], o_dx.at[b]) for b in range(2)]
            for c in saves:
                c.start()
            if near:
                ert_tick(27)
                group_sum(0, 2)
                sum_l.advance(0)
            again.wait()
            mixed_again.wait()

            def output(n, _):
                c = lanes(n * 256, 256)
                ml[:, c] = (mixed[:, c] + dot(act[...], flat_r[:, c]) + sv[7:8, c]).astype(BF16)
                if near:
                    for t in range(2):
                        @pl.when(n == t)
                        def _(t=t):
                            ert_tick(28 + t)
                            if t == 0:
                                group_sum(0, 3)
                            sum_l.advance(1 + t)
                return 0

            lax.fori_loop(0, 3, output, 0)
            back_to_raster(ml, dop)
            more = [load(b, dop.at[b * TOK:(b + 1) * TOK, :], o_out.at[b]) for b in range(2)]
            for c in more:
                c.start()
            if near:
                ert_tick(30)
                total_l = sum_l.advance(3)
                dev = pc.z * (2 * pc.ny * pc.nx) + (pc.y * pc.nx + pc.x) * 2 + pc.c
                n = o_small.shape[1]
                shift = lax.rem(D - dev * n, D)
                biases = [jnp.concatenate([sums_g[g, 8 + k:9 + k, 0:GW] for g in range(GROUPS)], axis=1) for k in range(2)]
                rows = jnp.concatenate([total_l] + biases + [sum_keep[0:4, :]], axis=0)
                o_small[...] = pltpu.roll(rows, shift, axis=1)[:, 0:n]
                wide_n = o_deb.shape[1]
                per = D // wide_n
                row = sum_keep[pl.ds(4 + dev // per, 1), :]
                o_deb[...] = pltpu.roll(row, lax.rem(D - lax.rem(dev, per) * wide_n, D), axis=1)[:, 0:wide_n]
                for g in range(GROUPS):
                    o_t4[g * GH:(g + 1) * GH, :] = sums_g[g, 0:8, 0:4 * WT]
                rs.done("e", None, o_e, 6, range(1, 5))
                rs.done("r", None, o_r, 3, range(1, 5))
                rs.done("t", dt, o_t, 6, range(5))
                sum_a.done()
                sum_l.done()
                for g in range(GROUPS):
                    sum_g(g).done()
            else:
                o_small[0:2, :] = late[0:2]
                o_small[2:8, :] = small[2:8, :]
                for k in range(4):
                    o_deb[0:1, k * D:(k + 1) * D] = small[8 + k:9 + k, :]
                o_t4[...] = t4g[...]
                save = load(3, dt, o_t)
                save.start()
                save.wait()
            for c in saves + more:
                c.wait()

        pl.run_scoped(attention, vm((ROWS, D), BF16), vm((D, ROWS), BF16), vm((ROWS, D), BF16), vm((2, QL, GW), BF16),
                      vm((2, QL, GW), BF16), vm((2, WT, QL), F32), vm((2, WT, QL), BF16), vm((4, WT, QL), BF16),
                      vm((9, WT, 128), F32), vm((2, 16, QL), F32), pltpu.SemaphoreType.DMA((4,)))
        pl.run_scoped(rest, vm((ROWS, FF), BF16))

    pl.run_scoped(after_feed_forward, vm((nz, ny, nx, rw_rows, 2 * TM_HALF), BF16), vm((ROWS, 3 * D), BF16),
                  vm((ROWS, D), BF16), vm((ROWS, D), BF16), vm((HEADS, 4 * WT), F32), vm((8, D), F32))


def backward(near, dims, counts, do, w, r, own_ew, own_er, triple, pt, att, mixed, n2, normed, xp, sv, eb):
    nz, ny, nx = dims if near else (1, 1, 1)
    if not near:
        w, r = w.reshape(1, 1, 1, D, -1), r.reshape(1, 1, 1, FF, D)
    rw, rr = w.shape[3], r.shape[3]
    peers = max(nz, ny, nx, 2) - 1
    vm = pltpu.VMEM
    dma = pltpu.SemaphoreType.DMA
    bufs = []
    for count, n in ((6, rw), (6, rw), (3, rr // 2)) if near else ((1, 16),) * 3:
        bufs += [vm((count, 2, nz, ny, nx, n, 128), BF16), vm((count, 2, max(ny - 1, 1), nz, nx, n, 128), BF16),
                 vm((count, 2, max(nx - 1, 1), nz, n, 128), BF16), vm((count, 2, max(nz - 1, 1), n, 128), BF16),
                 vm((count, 2, n, 128), F32)]
    n_slots = 2 + nz + ny + nx
    if near:
        outs = [((rw // 2, 2 * TM_HALF), F32), ((rw // 2, FF), F32), ((rr // 2, D), F32), ((8, rw // 2), F32), ((1, rr // 2), F32)]
    else:
        outs = [((1, 1, 1, D, 2 * TM_HALF), BF16), ((1, 1, 1, D, FF), BF16), ((1, 1, 1, FF, D), BF16), ((8, D), F32), ((1, FF), F32)]
    outs = [((2, TOK, D), BF16), ((2, TOK, D), BF16), ((ROWS, FF), BF16)] + outs + [((HEADS, 4 * WT), F32)]
    params = dict(collective_id=1, has_side_effects=True) if near else {}
    return pl.pallas_call(
        functools.partial(backward_kernel, near, dims),
        out_shape=[jax.ShapeDtypeStruct(s, d) for s, d in outs],
        in_specs=[SM, VM, VM, ANY, ANY, VM, VM] + [ANY] * 7 + [VM] * 2,
        out_specs=[ANY] * 3 + ([VM] * 3 if near else [ANY] * 3) + [VM] * 3,
        scratch_shapes=[vm((4, WT, 128), jnp.int32), vm((nz, ny, nx, rw, FF), BF16), vm((nz, ny, nx, rr, D), BF16), vm((ROWS, D), BF16), vm((ROWS, D), F32),
                        vm((ROWS, D), F32), vm((ROWS, D), BF16)] + bufs
        + [vm((n_slots, 8, D), F32), vm((GROUPS, n_slots, 16, 640), F32), vm((8, D), F32), vm((n_slots, 2, D), F32),
           vm((GROUPS, 16, 640), F32), vm((16, D), F32),
           dma((6, 4, peers)), dma((6, 4, peers)), dma((15, 2, 5, peers)), dma((15, 2, 5, peers)), dma((5, 4, peers)),
           dma((5, 4, peers)), dma((7,))],
        name="backward",
        compiler_params=pltpu.CompilerParams(vmem_limit_bytes=VMEM_LIMIT, **params),
    )(counts, jnp.asarray(RASTER_Q), do, w, r, own_ew, own_er, triple, pt, att, mixed, n2, normed, xp, sv,
      eb)


def finish_kernel(target, out_h, dx_h, t, e, r, small, deb, t4, out, dx, triple, merge, expand, reduce, table, *rest):
    vectors = rest
    out[...] = out_h[...]
    dx[...] = dx_h[...]
    for g in range(GROUPS):
        for k, parts in enumerate(group_cols(g)):
            at = k * D + g * GW
            for h, lo, n in parts:
                triple[:, at:at + n] = t[:, h * TM_HALF + lo:h * TM_HALF + lo + n]
                at += n
    for c in range(2):
        merge[:, c * D // 2:(c + 1) * D // 2] = t[:, c * TM_HALF + 1152:(c + 1) * TM_HALF]
        for s in range(2):
            expand[:, s * FF_HALF + c * FF_PART:s * FF_HALF + (c + 1) * FF_PART] = (
                e[:, c * FF_HALF + s * FF_PART:c * FF_HALF + (s + 1) * FF_PART])
    reduce[...] = r[...]
    for k, v in enumerate(vectors[:8]):
        v[...] = small[k, :]
    vectors[8][...] = deb[0, :]
    table[...] = lax.dot_general(t4[...], onehot(target), NT, precision=lax.Precision.HIGHEST,
                                 preferred_element_type=F32)


def weights_in_pieces(triple_weight, merge_weight, expand_weight):
    halves = []
    for c in range(2):
        for g in range(GROUPS):
            q, k, v = (triple_weight[:, i * D + g * GW:i * D + (g + 1) * GW] for i in range(3))
            halves += [q, k[:, :128]] if c == 0 else [k[:, 128:], v]
        halves.append(merge_weight[:, c * D // 2:(c + 1) * D // 2])
        halves += [expand_weight[:, s * FF_HALF + c * FF_PART:s * FF_HALF + (c + 1) * FF_PART] for s in range(2)]
    return jnp.concatenate(halves, axis=1)


def shards(dims, block_input, valid_counts, output_cotangent, triple_weight, merge_weight, expand_weight, reduce_weight,
           first_gain, first_shift, query_bias, value_bias, merge_bias, second_gain, second_shift, expand_bias,
           reduce_bias, position_table):
    counts = valid_counts[:, 0]
    rows = triple_weight.shape[0]
    near = rows % 8 == 0 and dims[0] % 4 == 0 and dims[1] == dims[2]
    if near:
        given = (triple_weight, merge_weight, expand_weight, reduce_weight, first_gain, first_shift, query_bias, value_bias,
                 merge_bias, second_gain, second_shift, reduce_bias, expand_bias)
    else:
        small = jnp.stack([first_gain, first_shift, query_bias, value_bias, merge_bias, second_gain, second_shift,
                           reduce_bias])
        gather = lambda v, axis: lax.all_gather(v.astype(BF16), AXES, axis=axis, tiled=True)
        given = (gather(weights_in_pieces(triple_weight, merge_weight, expand_weight), 0), gather(reduce_weight, 0),
                 gather(small, 1).astype(F32), jnp.broadcast_to(gather(expand_bias, 0).astype(F32)[None], (8, FF)))
    o_w, o_r, triple, pt, att, mixed, n2, normed, xp, sv, eb, own_ew, own_er = forward(
        near, dims, counts, block_input[:, 0], position_table, *given)
    if not near:
        o_w, o_r = given[:2]
    out, dx, _, gt, ge, gr, gs, gb, t4 = backward(near, dims, counts, output_cotangent[:, 0], o_w, o_r, own_ew, own_er, triple, pt,
                                               att, mixed, n2, normed, xp, sv, eb)
    if not near:
        scatter = lambda v, axis: lax.psum_scatter(v.astype(F32), AXES, scatter_dimension=axis, tiled=True)
        gt, ge, gr = scatter(gt.reshape(D, -1), 0), scatter(ge.reshape(D, -1), 0), scatter(gr.reshape(FF, D), 0)
        gs, gb, t4 = scatter(gs, 1), scatter(gb, 1), lax.psum(t4, AXES)
    n, rr = expand_bias.shape[0], reduce_weight.shape[0]
    image = jax.ShapeDtypeStruct((2, TOK, D), BF16)
    shapes = [(rows, 3 * D), (rows, D), (rows, FF), (rr, D), (HEADS, EXT * EXT)] + [(rows,)] * 8 + [(n,)]
    out, dx, tr, mg, ex, re, table, *vec = pl.pallas_call(
        finish_kernel, out_shape=[image, image] + [jax.ShapeDtypeStruct(s, F32) for s in shapes],
        in_specs=[VM] * 9, out_specs=[VM] * (2 + len(shapes)), name="finish",
        compiler_params=pltpu.CompilerParams(vmem_limit_bytes=VMEM_LIMIT),
    )(jnp.asarray(TARGET), out, dx, gt, ge, gr, gs, gb, t4)
    return (out[:, None], dx[:, None], tr, mg, ex, re, *vec[:7], vec[8], vec[7], table.T)


def solution(mesh):
    image = P(None, AXES, None, None)
    rows = P(AXES, None)
    vec = P(AXES)
    return jax.shard_map(
        functools.partial(shards, mesh_dims(mesh)), mesh=mesh,
        in_specs=(image, P(None, AXES), image) + (rows,) * 4 + (vec,) * 9 + (P(),),
        out_specs=(image, image) + (rows,) * 4 + (vec,) * 9 + (P(),),
        check_vma=False)
```

```python
import math
import functools

import numpy as np
import jax
import jax.numpy as jnp
from jax import lax
from jax.experimental import pallas as pl
from jax.experimental.pallas import tpu as pltpu
from jax.sharding import PartitionSpec as P

D = 768
FF = 3072
HEADS = 24
HEAD_DIM = 32
WIN = 12
SIDE = 24
SHIFT = 6
TOK = SIDE * SIDE
ROWS = 2 * TOK
WT = WIN * WIN
EXT = 2 * WIN - 1
GROUPS = 3
GH = HEADS // GROUPS
GW = GH * HEAD_DIM
QL = GH * WT
SCALE = HEAD_DIM ** -0.5
MASKED = -1e30
EPS = 1e-5
F32 = jnp.float32
BF16 = jnp.bfloat16
VMEM_LIMIT = 63 << 20
AXES = ("dp", "fsdp")
MESH = pl.DeviceIdType.MESH
ANY = pl.BlockSpec(memory_space=pl.ANY)
VM = pl.BlockSpec(memory_space=pltpu.VMEM)
SM = pl.BlockSpec(memory_space=pltpu.SMEM)
every = slice(None)

NN = (((1,), (0,)), ((), ()))
NT = (((1,), (1,)), ((), ()))
TN = (((0,), (0,)), ((), ()))


def dot(a, b, dims=NN):
    return lax.dot_general(a, b, dims, preferred_element_type=F32)


def layout_constants():
    j = np.arange(WT)
    reg = lambda c: (c >= SIDE - WIN).astype(np.int32) + (c >= SIDE - SHIFT).astype(np.int32)
    raster, label = np.zeros((4, WT), np.int32), np.zeros((4, WT), np.int32)
    for w in range(4):
        rr = (w // 2) * WIN + j // WIN
        rc = (w % 2) * WIN + j % WIN
        raster[w] = ((rr + SHIFT) % SIDE) * SIDE + (rc + SHIFT) % SIDE
        label[w] = reg(rr) * 3 + reg(rc)
    target = np.full((4, WT), -1, np.int32)
    for p in range(4):
        r = j // WIN + (WIN - 1 if p // 2 == 0 else -1)
        s = j % WIN + (WIN - 1 if p % 2 == 0 else -1)
        target[p] = np.where((r >= 0) & (s >= 0), r * EXT + s, -1)
    spread = lambda v: np.broadcast_to(v.reshape(1, TOK), (8, TOK)).astype(np.int32)
    return np.broadcast_to(np.tile(label, (1, GH))[:, None, :], (4, 8, QL)).astype(np.int32), spread(target), spread(raster)


LABEL_Q, TARGET, RASTER_Q = layout_constants()


def fill_places(raster, label=None):
    j = lax.broadcasted_iota(jnp.int32, (WT, 128), 0)
    a = (j * 171) >> 11
    c = j - a * WIN
    reg = lambda v: (v >= SIDE - WIN).astype(jnp.int32) + (v >= SIDE - SHIFT).astype(jnp.int32)
    turn = lambda v: jnp.where(v >= SIDE - SHIFT, v + SHIFT - SIDE, v + SHIFT)
    for w in range(4):
        rr, rc = a + (w // 2) * WIN, c + (w % 2) * WIN
        raster[w] = turn(rr) * SIDE + turn(rc)
        if label is not None:
            label[w] = reg(rr) * 3 + reg(rc)


def lane_iota(shape):
    return lax.broadcasted_iota(jnp.int32, shape, len(shape) - 1)


def aligned(v, n):
    return v if isinstance(v, int) else pl.multiple_of(v, n)


def lanes(start, width):
    return pl.ds(aligned(start, 128), width)


def window(i):
    return pl.ds(aligned(i * WT, WT), WT)


def to_window(raster, w):
    return (raster[w][:, 0:1] == lane_iota((WT, TOK))).astype(BF16)


def to_raster(raster_q, m):
    t = lax.broadcasted_iota(jnp.int32, (WT, TOK), 0) + m * WT
    return (raster_q[0:1, :] == t).astype(BF16)


def stats(x):
    mean = jnp.mean(x, axis=-1, keepdims=True)
    center = x - mean
    var = jnp.mean(center * center, axis=-1, keepdims=True)
    inv = lax.rsqrt(var + EPS)
    return center * inv, inv


def head_stack(dst, x):
    lane = lane_iota(x.shape) // HEAD_DIM
    zero = jnp.zeros_like(x)
    for h in range(GH):
        dst[h * WT:(h + 1) * WT, :] = jnp.where(lane == h, x, zero)


def head_pick(o):
    lane = lane_iota((WT, GW)) // HEAD_DIM
    out = jnp.where(lane == 0, o[0:WT], 0.0)
    for h in range(1, GH):
        out = jnp.where(lane == h, o[h * WT:(h + 1) * WT], out)
    return out


def onehot(target_ref):
    t = lax.broadcasted_iota(jnp.int32, (EXT * EXT, 4 * WT), 0)
    return (t == target_ref[0:1, :]).astype(F32)


def table_rows(table_ref, target_ref, t4):
    t4[...] = lax.dot_general(table_ref[...], onehot(target_ref), NN,
                              precision=lax.Precision.HIGHEST, preferred_element_type=F32) * (1.0 / SCALE)


def spread_bias(g, t4, bias, rowbuf):
    a_of = (lane_iota((1, QL)) % WT) // WIN
    c_of = lane_iota((16, QL)) % WIN
    rows = []
    for p in range(4):
        acc = jnp.zeros((1, QL), F32)
        for h in range(GH):
            piece = t4[pl.ds(g * GH + h, 1), p * WT:(p + 1) * WT]
            piece = jnp.concatenate([piece, jnp.zeros((1, QL - WT), F32)], axis=1)
            acc = acc + (pltpu.roll(piece, h * WT, axis=1) if h else piece)
        rows.append(acc)
    for s in range(2):
        for b in range(WIN):
            pos = pltpu.roll(rows[s], WIN * b, axis=1) if b else rows[s]
            neg = pltpu.roll(rows[2 + s], (WIN * b - WT) % QL, axis=1)
            rowbuf[s, b:b + 1, :] = jnp.where(a_of >= b, pos, neg)
    for d in range(WIN):
        pos = pltpu.roll(rowbuf[0], d, axis=1) if d else rowbuf[0]
        neg = pltpu.roll(rowbuf[1], (d - WIN) % QL, axis=1)
        both = jnp.where(c_of >= d, pos, neg)
        for n in range(9):
            bias[g * 9 + n, pl.ds(d, WIN, stride=WIN), :] = both[0:WIN, n * 128:(n + 1) * 128]


def gather_bias(g, bgrad, accbuf, t4):
    a_of = (lane_iota((1, QL)) % WT) // WIN
    c_of = lane_iota((WIN, QL)) % WIN
    pos = jnp.zeros((WIN, QL), F32)
    neg = jnp.zeros((WIN, QL), F32)
    for d in range(WIN):
        r = jnp.concatenate([bgrad[n, pl.ds(d, WIN, stride=WIN), :] for n in range(9)], axis=1)
        p = jnp.where(c_of >= d, r, 0.0)
        pos = pos + (pltpu.roll(p, QL - d, axis=1) if d else p)
        if d:
            neg = neg + pltpu.roll(jnp.where(c_of < d, r, 0.0), WIN - d, axis=1)
    accbuf[0, 0:WIN, :] = pos
    accbuf[1, 0:WIN, :] = neg
    for s in range(2):
        pp = jnp.zeros((1, QL), F32)
        nn = jnp.zeros((1, QL), F32)
        for b in range(WIN):
            r = accbuf[s, b:b + 1, :]
            p = jnp.where(a_of >= b, r, 0.0)
            pp = pp + (pltpu.roll(p, QL - WIN * b, axis=1) if b else p)
            if b:
                nn = nn + pltpu.roll(jnp.where(a_of < b, r, 0.0), WT - WIN * b, axis=1)
        for part, row in ((s, pp), (2 + s, nn)):
            for h in range(GH):
                moved = pltpu.roll(row, QL - h * WT, axis=1) if h else row
                t4[pl.ds(g * GH + h, 1), part * WT:(part + 1) * WT] = moved[:, 0:WT]


ERF_SLOPE = 0.35
ERF_FIT = (0.19434814435164116, 0.235843067071591, -0.008625688056468914, 0.6849613674275746, -0.6811631064960405, 0.7727015621272543, -0.19806535099226122)


def gelu_pair(v):
    e = jnp.exp(v * v * -0.5)
    t = 1.0 / (1.0 + jnp.abs(v) * (ERF_SLOPE * math.sqrt(0.5)))
    poly = jnp.full_like(t, 0.5 * ERF_FIT[-1])
    for c in ERF_FIT[-2::-1]:
        poly = poly * t + 0.5 * c
    tail = poly * t * e
    cdf = jnp.where(v >= 0, 1.0 - tail, tail)
    return v * cdf, cdf + v * e * (1.0 / math.sqrt(2.0 * math.pi))


def norm_back(hat, inv, gain, grad):
    scaled = grad * gain
    return inv * (scaled - jnp.mean(scaled, axis=-1, keepdims=True)
                  - hat * jnp.mean(scaled * hat, axis=-1, keepdims=True))


class Place:
    def __init__(self, dims):
        self.nz, self.ny, self.nx = dims
        f = lax.axis_index("fsdp")
        self.z = lax.axis_index("dp")
        self.c = lax.rem(f, 2)
        self.x = lax.rem(f // 2, self.nx)
        self.y = f // (2 * self.nx)

    def size(self, axis):
        return {"z": self.nz, "y": self.ny, "x": self.nx, "c": 2}[axis]

    def at(self, axis):
        return {"z": self.z, "y": self.y, "x": self.x, "c": self.c}[axis]

    def step(self, axis, k):
        return lax.rem(self.at(axis) + k, self.size(axis))

    def back(self, axis, k):
        return self.step(axis, self.size(axis) - k)

    def device(self, axis, k):
        p = {a: (self.step(a, k) if a == axis else self.at(a)) for a in "zyxc"}
        return (p["z"], (p["y"] * self.nx + p["x"]) * 2 + p["c"])

    def greet(self):
        barrier = pltpu.get_barrier_semaphore()
        total = 0
        for axis in "czyx":
            for k in range(1, self.size(axis)):
                pl.semaphore_signal(barrier, inc=1, device_id=self.device(axis, k), device_id_type=MESH)
                total += 1
        pl.semaphore_wait(barrier, total)


def mesh_dims(mesh):
    chips = mesh.shape["fsdp"] // 2
    ny = max(n for n in range(1, chips + 1) if n * n <= chips and chips % n == 0)
    return mesh.shape["dp"], ny, chips // ny


class Swap:
    def __init__(self, place, axis, sems, src, dst, came, has=None):
        self.has = has
        self.place, self.axis, self.sems = place, axis, sems
        self.src, self.dst, self.came = src, dst, came

    def make(self, k, src, dst):
        return pltpu.make_async_remote_copy(
            src_ref=src(k), dst_ref=dst(k), send_sem=self.sems[0](k), recv_sem=self.sems[1](k),
            device_id=self.place.device(self.axis, k), device_id_type=MESH)

    def peers(self):
        return range(1, self.place.size(self.axis))

    def each(self, sender, act):
        for k in self.peers():
            if self.has is None:
                act(k)
            else:
                pl.when(self.has(sender(k)))(lambda k=k: act(k))

    def start(self):
        self.each(lambda k: self.place.at(self.axis), lambda k: self.make(k, self.src, self.dst).start())

    def arrive(self):
        self.each(lambda k: self.place.back(self.axis, k), lambda k: self.make(k, self.came, self.came).wait_recv())

    def done(self):
        self.each(lambda k: self.place.at(self.axis), lambda k: self.make(k, self.src, self.dst).wait_send())


def when(cond, body):
    if isinstance(cond, (bool, np.bool_)):
        if cond:
            body()
    else:
        pl.when(cond)(body)


def both(*conds):
    out = True
    for c in conds:
        if isinstance(c, (bool, np.bool_)):
            if not c:
                return False
        else:
            out = c if out is True else jnp.logical_and(out, c)
    return out


def call(kernel, outs, scratch, ins, name):
    return pl.pallas_call(
        kernel, out_shape=[jax.ShapeDtypeStruct(s, d) for s, d in outs], in_specs=[VM] * len(ins),
        out_specs=[VM] * len(outs), scratch_shapes=scratch, name=name,
        compiler_params=pltpu.CompilerParams(vmem_limit_bytes=VMEM_LIMIT))(*ins)


HALF = 4 * D
TM_HALF = 2 * D
FF_HALF = FF // 2
FF_PART = FF // 4


class Gather:
    def __init__(self, place, w, half, base, n_w, r, part, send, recv):
        self.place = place
        self.w, self.half, self.base, self.n_w, self.r, self.part = w, half, base, n_w, r, part
        self.send, self.recv = send, recv
        self.n = n_w + 3

    def block(self, wide, p, c, ab=None):
        if wide:
            at, n = c * self.half + self.base + p * 256, 256
            return (every, lanes(at, n) if ab is None else lanes(at + ab * 128, 128))
        n = self.r.shape[3] // 2
        return (every if ab is None else pl.ds(ab * n, n), lanes(c * (D // 2) + p * 128, 128))

    def swaps(self, wide, p, s):
        return [self.swap(wide, p, s, ab) for ab in ((None,) if s in (0, 3) else (0, 1))]

    def swap(self, wide, p, s, ab):
        pc = self.place
        ref = self.w if wide else self.r
        q = p if wide else self.n_w + p
        n = {0: 0, 1: 1, 2: 3, 3: 5}[s] + (ab or 0)
        sems = (lambda k: self.send.at[q, n, k - 1], lambda k: self.recv.at[q, n, k - 1])
        blk = self.block(wide, p, pc.c, ab)
        zs = every if wide else pl.ds(self.part * (pc.nz // 2), pc.nz // 2)
        at = lambda zz, yy, xx, b=blk: ref.at[(zz, yy, xx) + b]
        z, y, x = pc.z, pc.y, pc.x
        if s == 0:
            has = None if wide else (lambda zz: (zz >= pc.nz // 2) == (self.part == 1))
            own = lambda k: at(z, y, x)
            return Swap(pc, "z", sems, own, own, lambda k: at(pc.back("z", k), y, x), has)
        if s == 3:
            mine = lambda k: at(zs, every, every)
            return Swap(pc, "c", sems, mine, mine, lambda k: at(zs, every, every, self.block(wide, p, 1 - pc.c)))
        first = "xy"[ab]
        if s == 1:
            own = lambda k: at(zs, y, x)
            if first == "x":
                return Swap(pc, "x", sems, own, own, lambda k: at(zs, y, pc.back("x", k)))
            return Swap(pc, "y", sems, own, own, lambda k: at(zs, pc.back("y", k), x))
        if first == "x":
            own = lambda k: at(zs, y, every)
            return Swap(pc, "y", sems, own, own, lambda k: at(zs, pc.back("y", k), every))
        own = lambda k: at(zs, every, x)
        return Swap(pc, "x", sems, own, own, lambda k: at(zs, every, pc.back("x", k)))

    def on_piece(self, p, body):
        when(both(p >= 0, p < self.n_w), lambda: body(True, p))
        when(both(p >= self.n_w, p < self.n), lambda: body(False, p - self.n_w))

    def tick(self, u, landed=None):
        def last(wide, p):
            for swap in self.swaps(wide, p, 3):
                swap.arrive()
            if landed is not None:
                landed(wide, p)

        def step(s):
            def body(wide, p):
                if s:
                    for swap in self.swaps(wide, p, s - 1):
                        swap.arrive()
                for swap in self.swaps(wide, p, s):
                    swap.start()
            return body

        self.on_piece(u - 8, last)
        for s in (3, 2, 1, 0):
            self.on_piece(u - 2 * s, step(s))

    def finish(self):
        for q in range(self.n):
            for s in range(4):
                for swap in self.swaps(q < self.n_w, q if q < self.n_w else q - self.n_w, s):
                    swap.done()


def small_swap(pc, sb, send, recv, s):
    sems = (lambda k: send.at[s, k - 1], lambda k: recv.at[s, k - 1])
    at = lambda zz, yy, xx, c=pc.c: sb.at[zz, yy, xx, c]
    z, y, x = pc.z, pc.y, pc.x
    own = [lambda k: at(z, y, x), lambda k: at(every, y, x), lambda k: at(every, y, every),
           lambda k: at(every, every, every)][s]
    came = [lambda k: at(pc.back("z", k), y, x), lambda k: at(every, y, pc.back("x", k)),
            lambda k: at(every, pc.back("y", k), every), lambda k: at(every, every, every, 1 - pc.c)][s]
    return Swap(pc, "zxyc"[s], sems, own, own, came)


def place_small(sb, sv, eb, n_small, n_wide):
    nz, ny, nx = sb.shape[:3]
    for out, row0, width, total in ((sv, 0, n_small, D), (eb, 8, n_wide, FF)):
        tiles = [jnp.zeros((8, 128), F32) for _ in range(total // 128)]
        lane = lane_iota((8, 128))
        n = 0
        for q in range(nz * ny * nx):
            for c in range(2):
                blk = sb[q // (ny * nx), (q // nx) % ny, q % nx, c, row0:row0 + 8, :]
                tile, off = divmod(n * width, 128)
                moved = pltpu.roll(blk, off, axis=1) if off else blk
                end = off + width
                tiles[tile] = jnp.where((lane >= off) & (lane < min(end, 128)), moved, tiles[tile])
                if end > 128:
                    tiles[tile + 1] = jnp.where(lane < end - 128, moved, tiles[tile + 1])
                n += 1
        out[...] = jnp.concatenate(tiles, axis=1)


def group_cols(g):
    return (((0, g * 384, 256),), ((0, g * 384 + 256, 128), (1, g * 384, 128)), ((1, g * 384 + 128, 256),))


def merge_cols(n):
    return tuple((b // 3, 1152 + lax.rem(b, 3) * 128, 128) for b in (2 * n, 2 * n + 1))


def columns(ref, parts, half):
    take = [ref[:, lanes(h * half + lo, n)] for h, lo, n in parts]
    return take[0] if len(take) == 1 else jnp.concatenate(take, axis=1)


class Flat:
    def __init__(self, ref):
        self.ref = ref

    def __getitem__(self, idx):
        v = self.ref[:, :, :, :, idx[1]]
        return v.reshape(-1, v.shape[-1])


def own_halves(h):
    for g in range(GROUPS):
        yield 0, g * GW + h * 2 * D, g * 384 + h * 128, 256
        yield 0, D + g * GW + h * 128, g * 384 + 256 * (1 - h), 128
    yield 1, h * (D // 2), 1152, D // 2
    for s in range(2):
        yield 2, s * FF_HALF + h * FF_PART, TM_HALF + s * FF_PART, FF_PART
    yield 3, h * (D // 2), 0, D // 2


def forward_kernel(near, dims, counts, x, labq, target, table, *rest):
    n_in = 13 if near else 4
    given = rest[:n_in]
    (o_w, o_r, o_triple, o_pt, o_att, o_mixed, o_n2, o_normed, o_xp, sv, eb, o_ew, o_er,
     w, r, sb, stage_w, stage_r, xp, normed, triple, attended, mixed, n2, pt, t4, bias, rowbuf, qs, st, lk, raster, labk,
     send, recv, ssend, srecv, lsem, psem) = rest[n_in:]

    def keep(n, src, dst):
        return pltpu.make_async_copy(src, dst, lsem.at[n])

    if near:
        pc = Place(dims)
        gather = Gather(pc, w, HALF, 0, 9, r, 0, send, recv)

    def part_of(wide, p):
        zs = every if wide else pl.ds(0, dims[0] // 2)
        for c in range(2):
            n = 2 * (p if wide else 9 + p) + c
            blk = (zs, every, every) + gather.block(wide, p, c)
            yield (keep(n, w.at[blk], o_w.at[blk]) if wide else keep(n, r.at[blk], o_r.at[blk]))

    def landed(wide, p):
        for copy in part_of(wide, p):
            copy.start()

    def small_tick(u):
        if u:
            small_swap(pc, sb, ssend, srecv, u // 2 - 1).arrive()
        if u < 8:
            small_swap(pc, sb, ssend, srecv, u // 2).start()

    if near:
        pc.greet()
        own, vectors = given[:4], given[4:]
        first = []
        for i, ((n, src, dst, width), (_, _, back, _)) in enumerate(zip(own_halves(1 - pc.c), own_halves(pc.c))):
            ref, stage = own[n], (stage_r if n == 3 else stage_w)
            rows = lambda c, m=ref.shape[0]: pl.ds(aligned(c * m, 8), m)
            sems = (lambda k, i=i: ssend.at[4 + i, 0], lambda k, i=i: srecv.at[4 + i, 0])
            first.append(Swap(pc, "c", sems, lambda k, v=ref.at[:, lanes(src, width)]: v,
                              lambda k, v=stage.at[rows(pc.c), lanes(dst, width)]: v,
                              lambda k, v=stage.at[rows(1 - pc.c), lanes(back, width)]: v))
        for s in first:
            s.start()
        sb[pc.z, pc.y, pc.x, pc.c] = jnp.zeros((16, 128), F32)
        for k, v in enumerate(vectors):
            sb[pc.z, pc.y, pc.x, pc.c, k, 0:v.shape[0]] = v[...].astype(BF16).astype(F32)
        for n, src, dst, width in own_halves(pc.c):
            ref, stage = own[n], (stage_r if n == 3 else stage_w)
            stage[pl.ds(aligned(pc.c * ref.shape[0], 8), ref.shape[0]), lanes(dst, width)] = ref[:, lanes(src, width)]
        for s in first[:-1]:
            s.arrive()
        w[pc.z, pc.y, pc.x, :, lanes(pc.c * HALF, HALF)] = stage_w[...].astype(BF16)
        gather.tick(0, landed)
        small_tick(0)
        gather.tick(1, landed)
        first[-1].arrive()
        r[pc.z, pc.y, pc.x, :, lanes(pc.c * (D // 2), D // 2)] = stage_r[...].astype(BF16)
        o_ew[...] = stage_w[:, TM_HALF + FF_PART:HALF].astype(BF16)
        o_er[...] = stage_r[...].astype(BF16)
    else:
        wown, rown, sv_in, eb_in = given
        loads = [keep(0, wown, w), keep(1, rown, r)]
        for c in loads:
            c.start()
        for c in loads:
            c.wait()
        sv[...] = sv_in[...]
        eb[...] = eb_in[...]

    def permute(i, _):
        xp[window(i), :] = dot(to_window(raster, i % 4), x[i // 4]).astype(BF16)
        return 0

    fill_places(raster, labk)
    table_rows(table, target, t4)

    def prologue(u, _):
        if near:
            gather.tick(u, landed)
            for k in range(1, 5):
                pl.when(u == 2 * k)(lambda k=k: small_tick(2 * k))

        @pl.when(u < 5)
        def _():
            spread_bias(u - 2, t4, bias, rowbuf)

        @pl.when(jnp.logical_and(u >= 5, u < 9))
        def _():
            lax.fori_loop(2 * (u - 5), 2 * (u - 4), permute, 0)

        return 0

    lax.fori_loop(2, 10, prologue, 0)
    if near:
        place_small(sb, sv, eb, given[0].shape[0], given[3].shape[0])

    def ln1(i, _):
        hat, _i = stats(xp[window(i), :].astype(F32))
        normed[window(i), :] = (hat * sv[0:1, :] + sv[1:2, :]).astype(BF16)
        return 0

    lax.fori_loop(0, 8, ln1, 0)
    keep(24, xp, o_xp).start()
    keep(25, normed, o_normed).start()
    wf = Flat(w)

    def products(i, g, u):
        rows, v = window(i), i % 4
        lk[u] = jnp.where(raster[v] < counts[i // 4], labk[v], -1)
        head_stack(qs.at[u], triple[rows, lanes(g * D, GW)])
        st[u] = dot(triple[rows, lanes(g * D + GW, GW)], qs[u], NT)

    def softmax(i, g, u):
        for n in range(9):
            c = lanes(n * 128, 128)
            s = st[u, :, c] + bias[g * 9 + n]
            s = jnp.where(lk[u] == labq[i % 4, 0:1, c], s, MASKED)
            m = jnp.max(s, axis=0, keepdims=True)
            e = jnp.exp((s - m) * SCALE)
            tot = jnp.sum(e, axis=0, keepdims=True)
            pt[u, :, c] = (e * (1.0 / tot)).astype(BF16)

    def attend(i, g, u):
        rows = window(i)
        pltpu.make_async_copy(pt.at[u], o_pt.at[g * 8 + i], psem.at[u]).start()
        out = head_pick(dot(pt[u], triple[rows, lanes(g * D + 2 * GW, GW)], TN))
        valid = raster[i % 4] < counts[i // 4]
        vq = jnp.concatenate([valid, valid], axis=1)
        attended[rows, lanes(g * GW, GW)] = jnp.where(vq, out, 0.0).astype(BF16)

    def quarter(q, _):
        g = q // 4

        @pl.when(q % 4 == 0)
        def _():
            for k, parts in enumerate(group_cols(g)):
                v = dot(normed[...], columns(wf, parts, HALF))
                if k != 1:
                    v = v + sv[2 + k // 2:3 + k // 2, lanes(g * GW, GW)]
                triple[:, lanes(g * D + k * GW, GW)] = v.astype(BF16)

        @pl.when(q >= 1)
        def _():
            for u in range(2):
                pltpu.make_async_copy(pt.at[u], o_pt.at[0], psem.at[u]).wait()

        i = 2 * lax.rem(q, 4)
        products(i, g, 0)
        products(i + 1, g, 1)
        softmax(i, g, 0)
        attend(i, g, 0)
        softmax(i + 1, g, 1)
        attend(i + 1, g, 1)
        if near:
            gather.tick(10 + q, landed)
        return 0

    lax.fori_loop(0, 4 * GROUPS, quarter, 0)
    keep(26, triple, o_triple).start()
    keep(27, attended, o_att).start()
    def merge(n, _):
        cols = lanes(n * 256, 256)
        v = dot(attended[...], columns(wf, merge_cols(n), HALF))
        mixed[:, cols] = xp[:, cols].astype(F32) + v + sv[4:5, cols]
        return 0

    lax.fori_loop(0, 3, merge, 0)
    keep(28, mixed, o_mixed).start()

    def ln2(i, _):
        hat, _i = stats(mixed[window(i), :])
        n2[window(i), :] = (hat * sv[5:6, :] + sv[6:7, :]).astype(BF16)
        return 0

    lax.fori_loop(0, 8, ln2, 0)
    keep(29, n2, o_n2).start()
    if near:
        gather.finish()
        for s in first:
            s.done()
        for s in range(4):
            small_swap(pc, sb, ssend, srecv, s).done()
        for q in range(12):
            for copy in part_of(q < 9, q if q < 9 else q - 9):
                copy.wait()
    for n, src, dst in ((24, xp, o_xp), (25, normed, o_normed), (26, triple, o_triple), (27, attended, o_att),
                        (28, mixed, o_mixed), (29, n2, o_n2)):
        keep(n, src, dst).wait()
    for slot in range(2):
        pltpu.make_async_copy(pt.at[slot], o_pt.at[0], psem.at[slot]).wait()


def forward(near, dims, counts, x, table, *given):
    nz, ny, nx = dims if near else (1, 1, 1)
    rw, rr = (given[0].shape[0] * 2, given[3].shape[0] * 2) if near else (D, FF)
    peers = max(nz, ny, nx, 2) - 1
    full_w, full_r = (nz, ny, nx, rw, 2 * HALF), (nz, ny, nx, rr, D)
    tiny = (8, 128)
    outs = [(full_w if near else tiny, BF16), (full_r if near else tiny, BF16), ((ROWS, 3 * D), BF16),
            ((8 * GROUPS, WT, QL), BF16), ((ROWS, D), BF16), ((ROWS, D), F32), ((ROWS, D), BF16), ((ROWS, D), BF16),
            ((ROWS, D), BF16), ((8, D), F32), ((8, FF), F32), ((rw, FF_PART) if near else tiny, BF16),
            ((rr, D // 2) if near else tiny, BF16)]
    if not near:
        given = (given[0].reshape(full_w), given[1].reshape(full_r)) + given[2:]
    vm = pltpu.VMEM
    dma = pltpu.SemaphoreType.DMA
    scratch = [vm(full_w, BF16), vm(full_r, BF16), vm((nz, ny, nx, 2, 16, 128), F32), vm((rw if near else 8, HALF), F32),
               vm((rr if near else 8, D // 2), F32), vm((ROWS, D), BF16), vm((ROWS, D), BF16), vm((ROWS, 3 * D), BF16),
               vm((ROWS, D), BF16), vm((ROWS, D), F32), vm((ROWS, D), BF16), vm((2, WT, QL), BF16),
               vm((HEADS, 4 * WT), F32), vm((GROUPS * 9, WT, 128), F32), vm((2, 16, QL), F32), vm((2, QL, GW), BF16),
               vm((2, WT, QL), F32), vm((2, WT, 128), jnp.int32), vm((4, WT, 128), jnp.int32), vm((4, WT, 128), jnp.int32),
               dma((12, 6, peers)), dma((12, 6, peers)), dma((14, peers)), dma((14, peers)), dma((30,)), dma((2,))]
    params = dict(collective_id=0, has_side_effects=True) if near else {}
    return pl.pallas_call(
        functools.partial(forward_kernel, near, dims),
        out_shape=[jax.ShapeDtypeStruct(s, d) for s, d in outs],
        in_specs=[SM] + [VM] * 4 + ([VM] * 13 if near else [ANY, ANY, VM, VM]),
        out_specs=[ANY] * 9 + [VM] * 4,
        scratch_shapes=scratch, name="forward",
        compiler_params=pltpu.CompilerParams(vmem_limit_bytes=VMEM_LIMIT, **params),
    )(counts, x, jnp.asarray(LABEL_Q), jnp.asarray(TARGET), table.T,
      *given)


class Scatter:
    def __init__(self, place, bufs, send, recv):
        self.place = place
        self.bufs, self.send, self.recv = bufs, send, recv

    def src(self, kind, g, i, ab, c):
        if kind == "r":
            n = g.shape[3] // 2
            return g.at[every, every, every, pl.ds(ab * n, n), lanes(c * (D // 2) + i * 128, 128)]
        return g.at[every, every, every, every, lanes(c * FF_HALF + i * 256 + ab * 128, 128)]

    def swap(self, kind, g, out, i, ab, s):
        pc = self.place
        r0, r1, r2, r3, fin = self.bufs[kind]
        q = {"e": 0, "t": 6, "r": 12}[kind] + i
        sems = (lambda k: self.send.at[q, ab, s, k - 1], lambda k: self.recv.at[q, ab, s, k - 1])
        first, second = ("y", "x") if ab == 0 else ("x", "y")
        if s == 0:
            to = lambda k: r0.at[i, ab]
            return Swap(pc, "c", sems, lambda k: self.src(kind, g, i, ab, 1 - pc.c), to, to)
        if s == 1:
            to = lambda k: r1.at[i, ab, k - 1]
            at = lambda k: (every, pc.step("y", k), every) if first == "y" else (every, every, pc.step("x", k))
            return Swap(pc, first, sems, lambda k: r0.at[(i, ab) + at(k)], to, to)
        if s == 2:
            to = lambda k: r2.at[i, ab, k - 1]
            return Swap(pc, second, sems, lambda k: r1.at[i, ab, 0, every, pc.step(second, k)], to, to)
        if s == 3:
            to = lambda k: r3.at[i, ab, k - 1]
            return Swap(pc, "z", sems, lambda k: r2.at[i, ab, 0, pc.step("z", k)], to, to)
        n = out.shape[0]
        if kind == "r":
            cols = lambda c: lanes(c * (D // 2) + i * 128, 128)
            return Swap(pc, "c", sems, lambda k: fin.at[i, 1 - pc.c], lambda k: out.at[:, cols(pc.c)],
                        lambda k: out.at[:, cols(1 - pc.c)])
        cols = lambda c: lanes(c * FF_HALF + i * 256 + ab * 128, 128)
        return Swap(pc, "c", sems, lambda k: fin.at[i, ab, pl.ds(aligned((1 - pc.c) * n, 8), n), :],
                    lambda k: out.at[:, cols(pc.c)], lambda k: out.at[:, cols(1 - pc.c)])

    def advance(self, kind, g, out, i, s):
        pc = self.place
        r0, r1, r2, r3, fin = self.bufs[kind]
        if s == 5:
            for ab in range(1 if kind == "r" else 2):
                self.swap(kind, g, out, i, ab, 4).arrive()
            return
        for ab in range(2):
            first, second = ("y", "x") if ab == 0 else ("x", "y")
            if s:
                self.swap(kind, g, out, i, ab, s - 1).arrive()
            if s == 1:
                n = r0.shape[-2]

                def add(z, _):
                    if kind == "r":
                        own = g[z, :, :, ab * n:(ab + 1) * n, lanes(pc.c * (D // 2) + i * 128, 128)]
                    else:
                        own = g[z, :, :, :, lanes(pc.c * FF_HALF + i * 256 + ab * 128, 128)]
                    r0[i, ab, z] = (r0[i, ab, z].astype(F32) + own.astype(F32)).astype(BF16)
                    return 0

                lax.fori_loop(0, pc.nz, add, 0)
            if s == 2:
                at = (every, pc.y, every) if first == "y" else (every, every, pc.x)
                v = r0[(i, ab) + at].astype(F32)
                for k in range(pc.size(first) - 1):
                    v = v + r1[i, ab, k].astype(F32)
                r1[i, ab, 0] = v.astype(BF16)
            if s == 3:
                v = r1[i, ab, 0, :, pc.at(second)].astype(F32)
                for k in range(pc.size(second) - 1):
                    v = v + r2[i, ab, k].astype(F32)
                r2[i, ab, 0] = v.astype(BF16)
            if s == 4:
                v = r2[i, ab, 0, pc.z].astype(F32)
                for k in range(pc.nz - 1):
                    v = v + r3[i, ab, k].astype(F32)
                fin[i, ab] = v
                if kind != "r":
                    n = out.shape[0]
                    out[:, lanes(pc.c * FF_HALF + i * 256 + ab * 128, 128)] = fin[i, ab, pl.ds(aligned(pc.c * n, 8), n), :]
            if s < 4 or kind != "r":
                self.swap(kind, g, out, i, ab, s).start()
        if s == 4 and kind == "r":
            out[:, lanes(pc.c * (D // 2) + i * 128, 128)] = fin[i, pc.c]
            self.swap(kind, g, out, i, 0, 4).start()

    def done(self, kind, g, out, pieces, steps):
        for i in range(pieces):
            for s in steps:
                for ab in range(1 if (kind == "r" and s == 4) else 2):
                    self.swap(kind, g, out, i, ab, s).done()


class SmallSum:
    def __init__(self, place, slots, send, recv):
        self.place, self.slots, self.send, self.recv = place, slots, send, recv

    def base(self, i):
        return sum(self.place.size(a) for a in "cyxz"[:i])

    def swap(self, i):
        pc, a = self.place, "cyxz"[i]
        sems = (lambda k: self.send.at[i, k - 1], lambda k: self.recv.at[i, k - 1])
        me = lambda k: self.slots.at[self.base(i) + pc.at(a)]
        return Swap(pc, a, sems, me, me, lambda k: self.slots.at[self.base(i) + pc.back(a, k)])

    def start(self):
        self.swap(0).start()

    def advance(self, i):
        self.swap(i).arrive()
        s = self.slots[self.base(i)]
        for k in range(1, self.place.size("cyxz"[i])):
            s = s + self.slots[self.base(i) + k]
        if i == 3:
            return s
        self.slots[self.base(i + 1) + self.place.at("cyxz"[i + 1])] = s
        self.swap(i + 1).start()

    def done(self):
        for i in range(4):
            self.swap(i).done()


def events(t):
    out = [("e", i, s) for i in range(6) for s in range(6) if 2 * i + 1 + 2 * s == t and t >= 12]
    for i, at in enumerate(((12, 14, 16, 18, 20, 22), (13, 15, 17, 19, 21, 23), (14, 15, 18, 20, 22, 24))):
        out += [("r", i, s) for s in range(6) if at[s] == t]
    for pieces, at in (((5,), (16, 18, 20, 22, 24, 26)), ((3, 4), (19, 20, 22, 23, 25, 26)), ((2,), (21, 22, 24, 25, 27, 28)),
                       ((0, 1), (23, 24, 26, 27, 29, 30))):
        out += [("t", i, s) for i in pieces for s in range(6) if at[s] == t]
    return sorted(out, key=lambda e: -e[2])


def backward_kernel(near, dims, counts, rasq, do, w, r, own_ew, own_er, triple_h, pt_h, att_h, mixed_h, n2_h, normed_h,
                    xp_h, sv, eb, o_out, o_dx, o_act, o_t, o_e, o_r, o_small, o_deb, o_t4,
                    raster, ew, rw, dop, dn2, mixed, part, e0, e1, e2, e3, ef, t0, t1, t2, t3, tf, b0, b1, b2, b3, bf, slots_a, slots_g, late, slots_l, smalls,
                    gsend, grecv, send, recv, ssend, srecv, lsem):
    def load(n, src, dst):
        return pltpu.make_async_copy(src, dst, lsem.at[n])

    if near:
        pc = Place(dims)
        rs = Scatter(pc, {"e": (e0, e1, e2, e3, ef), "t": (t0, t1, t2, t3, tf), "r": (b0, b1, b2, b3, bf)}, send, recv)
        sum_a = SmallSum(pc, slots_a, ssend.at[0], srecv.at[0])
        sum_l = SmallSum(pc, slots_l, ssend.at[1], srecv.at[1])
        sum_g = SmallSum(pc, slots_g, ssend.at[2], srecv.at[2])
        pc.greet()
    else:
        pc = None
    small = smalls
    fill_places(raster)
    small[...] = jnp.zeros(small.shape, F32)

    def feed_forward(n2, n2t, act, hs, ds, hl, de, dr):
        half_z = dims[0] // 2
        loads = [load(0, n2_h, n2), load(3, mixed_h, mixed)]
        if near:
            for c in range(2):
                a, b = lanes(c * HALF + TM_HALF, FF_PART), lanes(c * FF_HALF, FF_PART)
                loads.append(load(4 + c, w.at[:, :, :, :, a], ew.at[:, :, :, :, b]))
            loads.append(load(2, r.at[0:half_z], rw.at[0:half_z]))
        else:
            for c in range(2):
                a, b = lanes(c * HALF + TM_HALF, FF_HALF), lanes(c * FF_HALF, FF_HALF)
                loads.append(load(4 + c, w.at[:, :, :, :, a], ew.at[:, :, :, :, b]))
            loads.append(load(2, r, rw))
        for c in loads:
            c.start()
        if near:
            gather = Gather(pc, ew, FF_HALF, FF_PART, 3, rw, 1, gsend, grecv)
            ew[pc.z, pc.y, pc.x, :, lanes(pc.c * FF_HALF + FF_PART, FF_PART)] = own_ew[...]

            @pl.when(pc.z >= half_z)
            def _():
                rw[pc.z, pc.y, pc.x, :, lanes(pc.c * (D // 2), D // 2)] = own_er[...]

            gather.tick(0)
            gather.tick(1)

        def permute(i, _):
            dop[window(i), :] = dot(to_window(raster, i % 4), do[i // 4]).astype(BF16)
            return 0

        lax.fori_loop(0, 8, permute, 0)
        if near:
            gather.tick(2)
            gather.tick(3)
        for c in loads:
            c.wait()
        n2t[...] = n2[...].T
        dn2[...] = jnp.zeros(dn2.shape, F32)
        small[7:8, :] = jnp.sum(dop[...].astype(F32), axis=0, keepdims=True)
        nz, ny, nx, rr = rw.shape[:4]
        per = FF // 256

        def rows_of(n0):
            return flat_r[pl.ds(aligned(n0, 256), 256), :]

        flat_r = rw.reshape(FF, D)
        fe, fde = Flat(ew), de

        def chunk(j, _):
            s, k = j // 6, j % 6
            c, off = k % 2, k // 2
            col = lanes(c * FF_HALF + s * FF_PART + off * 256, 256)
            n0 = s * FF_HALF + c * FF_PART + off * 256
            nat = lanes(n0, 256)
            weights = fe[:, col]
            rows = rows_of(n0)
            bias = eb[0:1, nat]
            total = jnp.zeros((8, 256), F32)

            def products(m):
                rows_m = pl.ds(m * 288, 288)
                hs[rows_m, :] = dot(n2[rows_m, :], weights)
                ds[rows_m, :] = dot(dop[rows_m, :], rows, NT)

            def gate(m, total):
                for q in range(288 // 32):
                    rr_ = pl.ds(m * 288 + q * 32, 32)
                    a, slope = gelu_pair(hs[rr_, :] + bias)
                    act[rr_, nat] = a.astype(BF16)
                    hg = ds[rr_, :] * slope
                    for p in range(4):
                        total = total + hg[p * 8:(p + 1) * 8]
                    hl[rr_, :] = hg.astype(BF16)
                return total

            products(0)
            for m in range(4):
                if m + 1 < 4:
                    products(m + 1)
                total = gate(m, total)
            small[pl.ds(8 + s * 2 + c, 1), lanes(off * 256, 256)] = jnp.sum(total, axis=0, keepdims=True)
            de[:, :, :, :, col] = dot(n2t[...], hl[...]).astype(BF16).reshape(de.shape[:4] + (256,))
            for n in range(3):
                cc = lanes(n * 256, 256)
                dn2[:, cc] += dot(hl[...], weights[n * 256:(n + 1) * 256], NT)
            if near:
                gather.tick(4 + 2 * j)
                gather.tick(5 + 2 * j)
                for step in range(5, -1, -1):
                    i = j // 2 - step
                    pl.when(jnp.logical_and(lax.rem(j, 2) == 1, i >= 0))(
                        lambda i=i, step=step: rs.advance("e", de, o_e, i, step))
            return 0

        lax.fori_loop(0, per, chunk, 0)

        def er_tick(t):
            for kind, i, s in events(t):
                rs.advance(kind, de if kind == "e" else dr, o_e if kind == "e" else o_r, i, s)

        spill = load(6, act, o_act)
        spill.start()
        flat_dr = dr.reshape(FF, D)

        def reduce_part(n, _):
            def quarter(m, _):
                two = jnp.concatenate([dop[:, lanes(n * 128, 128)], dop[:, lanes(D // 2 + n * 128, 128)]], axis=1)
                v = dot(act[:, lanes(m * D, D)], two, TN).astype(BF16)
                rows = pl.ds(aligned(m * D, D), D)
                flat_dr[rows, lanes(n * 128, 128)] = v[:, :128]
                flat_dr[rows, lanes(D // 2 + n * 128, 128)] = v[:, 128:]
                return 0

            lax.fori_loop(0, 4, quarter, 0)
            if near:
                for t in range(3):
                    pl.when(n == t)(lambda t=t: er_tick(12 + t))
            return 0

        lax.fori_loop(0, 3, reduce_part, 0)

        def ln2b(i, _):
            rows = window(i)
            hat, inv = stats(mixed[rows, :])
            g = dn2[rows, :]
            small[5:6, :] += jnp.sum(g * hat, axis=0, keepdims=True)
            small[6:7, :] += jnp.sum(g, axis=0, keepdims=True)
            m = dop[rows, :].astype(F32) + norm_back(hat, inv, sv[5:6, :], g)
            small[4:5, :] += jnp.sum(m, axis=0, keepdims=True)
            mixed[rows, :] = m
            part[rows, :] = m.astype(BF16)
            return 0

        lax.fori_loop(0, 8, ln2b, 0)
        if near:
            er_tick(15)
            gather.finish()
            rs.done("e", de, o_e, 6, range(1))
            rs.done("r", dr, o_r, 3, range(1))
        else:
            for c in (load(4, de, o_e), load(5, dr, o_r)):
                c.start()
                c.wait()
        spill.wait()

    nz, ny, nx, rw_rows = w.shape[:4]
    rr_rows = r.shape[3]
    vm = pltpu.VMEM
    pl.run_scoped(feed_forward, vm((ROWS, D), BF16),
                  vm((D, ROWS), BF16), vm((ROWS, FF), BF16), vm((ROWS, 256), F32), vm((ROWS, 256), F32), vm((ROWS, 256), BF16),
                  vm((nz, ny, nx, rw_rows, FF), BF16), vm((nz, ny, nx, rr_rows, D), BF16))
    tw = ew
    flat_tw = tw.reshape(D, FF)
    flat_r = rw.reshape(FF, D)

    def after_feed_forward(dt, triple, ml, xp, t4g, sum_keep):
        def ert_tick(t):
            if near:
                for kind, i, s in events(t):
                    rs.advance(kind, {"e": None, "r": None, "t": dt}[kind], {"e": o_e, "r": o_r, "t": o_t}[kind], i, s)

        def put(parts, v):
            at = 0
            for h, lo, n in parts:
                dt[:, :, :, :, lanes(h * TM_HALF + lo, n)] = v[:, at:at + n].reshape(dt.shape[:4] + (n,))
                at += n

        def attention(datt, xt, xn, qs, dos, st, raw, pt, bgrad, accbuf, psem):
            loads = [load(0, att_h, xn), load(1, triple_h, triple), load(2, xp_h, xp)]
            loads += [load(4 + c, w.at[:, :, :, :, lanes(c * HALF, TM_HALF)], tw.at[:, :, :, :, lanes(c * TM_HALF, TM_HALF)])
                      for c in range(2)]
            for c in loads:
                c.start()

            def fetch(step):
                return pltpu.make_async_copy(pt_h.at[(2 - step // 8) * 8 + step % 8], pt.at[step % 4], psem.at[step % 4])

            fetch(0).start()
            fetch(1).start()
            for c in loads:
                c.wait()
            xt[...] = xn[...].T
            again = load(0, normed_h, xn)
            again.start()

            def merge_grad(n, _):
                put(merge_cols(n), dot(xt[...], part[:, lanes(n * 256, 256)]).astype(BF16))
                return 0

            lax.fori_loop(0, 3, merge_grad, 0)
            ert_tick(16)

            def merge_back(n, _):
                rows = pl.ds(aligned(n * 256, 256), 256)
                m = jnp.concatenate([flat_tw[rows, 1152:TM_HALF], flat_tw[rows, TM_HALF + 1152:]], axis=1)
                datt[:, lanes(n * 256, 256)] = dot(part[...], m, NT).astype(BF16)
                return 0

            lax.fori_loop(0, 3, merge_back, 0)
            again.wait()
            xt[...] = xn[...].T
            ert_tick(17)
            if near:
                slots_a[pc.c, 0:4, :] = small[4:8, :]
                slots_a[pc.c, 4:8, :] = small[8:12, :]
                sum_a.start()

            def place_of(step):
                i = step % 8
                return window(i), raster[i % 4] < counts[i // 4]

            def products(step, g, u):
                rows, valid = place_of(step)
                vq = jnp.concatenate([valid, valid], axis=1)
                da = datt[rows, lanes(g * GW, GW)]
                da = jnp.where(vq, da.astype(F32), 0.0).astype(BF16)
                head_stack(qs.at[u], triple[rows, lanes(g * D, GW)])
                head_stack(dos.at[u], da)
                st[u] = dot(triple[rows, lanes(g * D + 2 * GW, GW)], dos[u], NT)

            def softmax_back(slot, u):
                for n in range(9):
                    c = lanes(n * 128, 128)
                    p = pt[slot, :, c].astype(F32)
                    d = st[u, :, c]
                    inner = jnp.sum(p * d, axis=0, keepdims=True)
                    s = p * (d - inner)
                    bgrad[n] += s
                    raw[u, :, c] = (s * SCALE).astype(BF16)

            def grads(step, g, slot, u):
                rows, _ = place_of(step)
                col = lambda k: lanes(g * D + k * GW, GW)
                key = triple[rows, col(1)]
                triple[rows, col(2)] = dot(pt[slot], dos[u]).astype(BF16)
                triple[rows, col(1)] = dot(raw[u], qs[u]).astype(BF16)
                triple[rows, col(0)] = head_pick(dot(raw[u], key, TN)).astype(BF16)

            def pair(p, g):
                step, slot = 2 * p, 2 * lax.rem(p, 2)

                @pl.when(p < 11)
                def _():
                    fetch(step + 2).start()
                    fetch(step + 3).start()

                products(step, g, 0)
                products(step + 1, g, 1)
                fetch(step).wait()
                fetch(step + 1).wait()
                softmax_back(slot, 0)
                grads(step, g, slot, 0)
                softmax_back(slot + 1, 1)
                grads(step + 1, g, slot + 1, 1)

            def half_group(q, _):
                g = 2 - q // 2

                @pl.when(q % 2 == 0)
                def _():
                    bgrad[...] = jnp.zeros(bgrad.shape, F32)

                lax.fori_loop(0, 2, lambda j, _: (pair(q * 2 + j, g), 0)[1], 0)

                @pl.when(q % 2 == 1)
                def _():
                    gather_bias(g, bgrad, accbuf, t4g)
                    for k, parts in enumerate(group_cols(g)):
                        v = triple[:, lanes(g * D + k * GW, GW)]
                        if k != 1:
                            small[2 + k // 2:3 + k // 2, lanes(g * GW, GW)] = jnp.sum(v.astype(F32), axis=0, keepdims=True)
                        put(parts, dot(xt[...], v).astype(BF16))

                if near:
                    for t in range(18, 24):
                        if events(t):
                            pl.when(q == t - 18)(lambda t=t: ert_tick(t))
                    for m, at in enumerate((0, 2, 4)):
                        pl.when(q == at)(lambda m=m: sum_a.advance(m) and None)

                return 0

            lax.fori_loop(0, 2 * GROUPS, half_group, 0)
            if near:
                own = slots_g.at[pc.c]
                own[...] = jnp.zeros(own.shape, F32)
                own[:, 0:4 * WT] = t4g[...]
                sum_g.start()
        def rest(act):
            again = load(0, o_act, act)
            again.start()

            def normed_grad(n, _):
                rows = pl.ds(aligned(n * 256, 256), 256)
                weights = jnp.concatenate([flat_tw[rows, h * TM_HALF + lo:h * TM_HALF + lo + m]
                                           for g in range(GROUPS) for p in group_cols(g) for h, lo, m in p], axis=1)
                dn2[:, lanes(n * 256, 256)] = dot(triple[...], weights, NT)
                if near:
                    for t in range(2):
                        @pl.when(n == t)
                        def _(t=t):
                            ert_tick(24 + t)
                            if t == 1:
                                sum_g.advance(0)
                return 0

            lax.fori_loop(0, 3, normed_grad, 0)

            def ln1b(i, _):
                rows = window(i)
                hat, inv = stats(xp[rows, :].astype(F32))
                g = dn2[rows, :]
                late[0:1, :] += jnp.sum(g * hat, axis=0, keepdims=True)
                late[1:2, :] += jnp.sum(g, axis=0, keepdims=True)
                ml[rows, :] = (mixed[rows, :] + norm_back(hat, inv, sv[0:1, :], g)).astype(BF16)
                return 0

            late[...] = jnp.zeros(late.shape, F32)
            lax.fori_loop(0, 8, ln1b, 0)
            if near:
                slots_l[pc.c, 0:2, :] = late[0:2, :]
                slots_l[pc.c, 2:4, :] = small[2:4, :]
                sum_l.start()
                ert_tick(26)
                sum_g.advance(1)
                sum_keep[...] = sum_a.advance(3)
            mixed_again = load(3, mixed_h, mixed)
            mixed_again.start()

            def back_to_raster(src, dst):
                def block(k, _):
                    b, m = k // 4, k % 4
                    dst[window(k), :] = dot(to_raster(rasq, m), src[pl.ds(aligned(b * TOK, TOK), TOK), :]).astype(BF16)
                    return 0

                lax.fori_loop(0, 8, block, 0)

            back_to_raster(ml, part)
            saves = [load(4 + b, part.at[b * TOK:(b + 1) * TOK, :], o_dx.at[b]) for b in range(2)]
            for c in saves:
                c.start()
            if near:
                ert_tick(27)
                sum_g.advance(2)
                sum_l.advance(0)
            again.wait()
            mixed_again.wait()

            def output(n, _):
                c = lanes(n * 256, 256)
                ml[:, c] = (mixed[:, c] + dot(act[...], flat_r[:, c]) + sv[7:8, c]).astype(BF16)
                if near:
                    for t in range(2):
                        @pl.when(n == t)
                        def _(t=t):
                            ert_tick(28 + t)
                            sum_l.advance(1 + t)
                return 0

            lax.fori_loop(0, 3, output, 0)
            back_to_raster(ml, dop)
            more = [load(b, dop.at[b * TOK:(b + 1) * TOK, :], o_out.at[b]) for b in range(2)]
            for c in more:
                c.start()
            if near:
                ert_tick(30)
                total_g = sum_g.advance(3)
                total_l = sum_l.advance(3)
                dev = pc.z * (2 * pc.ny * pc.nx) + (pc.y * pc.nx + pc.x) * 2 + pc.c
                n = o_small.shape[1]
                shift = lax.rem(D - dev * n, D)
                rows = jnp.concatenate([total_l, sum_keep[0:4, :]], axis=0)
                o_small[...] = pltpu.roll(rows, shift, axis=1)[:, 0:n]
                wide_n = o_deb.shape[1]
                per = D // wide_n
                row = sum_keep[pl.ds(4 + dev // per, 1), :]
                o_deb[...] = pltpu.roll(row, lax.rem(D - lax.rem(dev, per) * wide_n, D), axis=1)[:, 0:wide_n]
                o_t4[...] = total_g[:, 0:4 * WT]
                rs.done("e", None, o_e, 6, range(1, 5))
                rs.done("r", None, o_r, 3, range(1, 5))
                rs.done("t", dt, o_t, 6, range(5))
                sum_a.done()
                sum_l.done()
                sum_g.done()
            else:
                o_small[0:2, :] = late[0:2]
                o_small[2:8, :] = small[2:8, :]
                for k in range(4):
                    o_deb[0:1, k * D:(k + 1) * D] = small[8 + k:9 + k, :]
                o_t4[...] = t4g[...]
                save = load(3, dt, o_t)
                save.start()
                save.wait()
            for c in saves + more:
                c.wait()

        pl.run_scoped(attention, vm((ROWS, D), BF16), vm((D, ROWS), BF16), vm((ROWS, D), BF16), vm((2, QL, GW), BF16),
                      vm((2, QL, GW), BF16), vm((2, WT, QL), F32), vm((2, WT, QL), BF16), vm((4, WT, QL), BF16),
                      vm((9, WT, 128), F32), vm((2, 16, QL), F32), pltpu.SemaphoreType.DMA((4,)))
        pl.run_scoped(rest, vm((ROWS, FF), BF16))

    pl.run_scoped(after_feed_forward, vm((nz, ny, nx, rw_rows, 2 * TM_HALF), BF16), vm((ROWS, 3 * D), BF16),
                  vm((ROWS, D), BF16), vm((ROWS, D), BF16), vm((HEADS, 4 * WT), F32), vm((8, D), F32))


def backward(near, dims, counts, do, w, r, own_ew, own_er, triple, pt, att, mixed, n2, normed, xp, sv, eb):
    nz, ny, nx = dims if near else (1, 1, 1)
    if not near:
        w, r = w.reshape(1, 1, 1, D, -1), r.reshape(1, 1, 1, FF, D)
    rw, rr = w.shape[3], r.shape[3]
    peers = max(nz, ny, nx, 2) - 1
    vm = pltpu.VMEM
    dma = pltpu.SemaphoreType.DMA
    bufs = []
    for count, n in ((6, rw), (6, rw), (3, rr // 2)) if near else ((1, 16),) * 3:
        bufs += [vm((count, 2, nz, ny, nx, n, 128), BF16), vm((count, 2, max(ny - 1, 1), nz, nx, n, 128), BF16),
                 vm((count, 2, max(nx - 1, 1), nz, n, 128), BF16), vm((count, 2, max(nz - 1, 1), n, 128), BF16),
                 vm((count, 2, n, 128), F32)]
    n_slots = 2 + nz + ny + nx
    if near:
        outs = [((rw // 2, 2 * TM_HALF), F32), ((rw // 2, FF), F32), ((rr // 2, D), F32), ((8, rw // 2), F32), ((1, rr // 2), F32)]
    else:
        outs = [((1, 1, 1, D, 2 * TM_HALF), BF16), ((1, 1, 1, D, FF), BF16), ((1, 1, 1, FF, D), BF16), ((8, D), F32), ((1, FF), F32)]
    outs = [((2, TOK, D), BF16), ((2, TOK, D), BF16), ((ROWS, FF), BF16)] + outs + [((HEADS, 4 * WT), F32)]
    params = dict(collective_id=1, has_side_effects=True) if near else {}
    return pl.pallas_call(
        functools.partial(backward_kernel, near, dims),
        out_shape=[jax.ShapeDtypeStruct(s, d) for s, d in outs],
        in_specs=[SM, VM, VM, ANY, ANY, VM, VM] + [ANY] * 7 + [VM] * 2,
        out_specs=[ANY] * 3 + ([VM] * 3 if near else [ANY] * 3) + [VM] * 3,
        scratch_shapes=[vm((4, WT, 128), jnp.int32), vm((nz, ny, nx, rw, FF), BF16), vm((nz, ny, nx, rr, D), BF16), vm((ROWS, D), BF16), vm((ROWS, D), F32),
                        vm((ROWS, D), F32), vm((ROWS, D), BF16)] + bufs
        + [vm((n_slots, 8, D), F32), vm((n_slots, HEADS, 640), F32), vm((8, D), F32), vm((n_slots, 4, D), F32),
           vm((16, D), F32),
           dma((6, 6, peers)), dma((6, 6, peers)), dma((15, 2, 5, peers)), dma((15, 2, 5, peers)), dma((3, 4, peers)),
           dma((3, 4, peers)), dma((7,))],
        name="backward",
        compiler_params=pltpu.CompilerParams(vmem_limit_bytes=VMEM_LIMIT, **params),
    )(counts, jnp.asarray(RASTER_Q), do, w, r, own_ew, own_er, triple, pt, att, mixed, n2, normed, xp, sv,
      eb)


def finish_kernel(target, out_h, dx_h, t, e, r, small, deb, t4, out, dx, triple, merge, expand, reduce, table, *rest):
    vectors = rest
    out[...] = out_h[...]
    dx[...] = dx_h[...]
    for g in range(GROUPS):
        for k, parts in enumerate(group_cols(g)):
            at = k * D + g * GW
            for h, lo, n in parts:
                triple[:, at:at + n] = t[:, h * TM_HALF + lo:h * TM_HALF + lo + n]
                at += n
    for c in range(2):
        merge[:, c * D // 2:(c + 1) * D // 2] = t[:, c * TM_HALF + 1152:(c + 1) * TM_HALF]
        for s in range(2):
            expand[:, s * FF_HALF + c * FF_PART:s * FF_HALF + (c + 1) * FF_PART] = (
                e[:, c * FF_HALF + s * FF_PART:c * FF_HALF + (s + 1) * FF_PART])
    reduce[...] = r[...]
    for k, v in enumerate(vectors[:8]):
        v[...] = small[k, :]
    vectors[8][...] = deb[0, :]
    table[...] = lax.dot_general(t4[...], onehot(target), NT, precision=lax.Precision.HIGHEST,
                                 preferred_element_type=F32)


def weights_in_pieces(triple_weight, merge_weight, expand_weight):
    halves = []
    for c in range(2):
        for g in range(GROUPS):
            q, k, v = (triple_weight[:, i * D + g * GW:i * D + (g + 1) * GW] for i in range(3))
            halves += [q, k[:, :128]] if c == 0 else [k[:, 128:], v]
        halves.append(merge_weight[:, c * D // 2:(c + 1) * D // 2])
        halves += [expand_weight[:, s * FF_HALF + c * FF_PART:s * FF_HALF + (c + 1) * FF_PART] for s in range(2)]
    return jnp.concatenate(halves, axis=1)


def shards(dims, block_input, valid_counts, output_cotangent, triple_weight, merge_weight, expand_weight, reduce_weight,
           first_gain, first_shift, query_bias, value_bias, merge_bias, second_gain, second_shift, expand_bias,
           reduce_bias, position_table):
    counts = valid_counts[:, 0]
    rows = triple_weight.shape[0]
    near = rows % 8 == 0 and dims[0] % 4 == 0 and dims[1] == dims[2]
    if near:
        given = (triple_weight, merge_weight, expand_weight, reduce_weight, first_gain, first_shift, query_bias, value_bias,
                 merge_bias, second_gain, second_shift, reduce_bias, expand_bias)
    else:
        small = jnp.stack([first_gain, first_shift, query_bias, value_bias, merge_bias, second_gain, second_shift,
                           reduce_bias])
        gather = lambda v, axis: lax.all_gather(v.astype(BF16), AXES, axis=axis, tiled=True)
        given = (gather(weights_in_pieces(triple_weight, merge_weight, expand_weight), 0), gather(reduce_weight, 0),
                 gather(small, 1).astype(F32), jnp.broadcast_to(gather(expand_bias, 0).astype(F32)[None], (8, FF)))
    o_w, o_r, triple, pt, att, mixed, n2, normed, xp, sv, eb, own_ew, own_er = forward(
        near, dims, counts, block_input[:, 0], position_table, *given)
    if not near:
        o_w, o_r = given[:2]
    out, dx, _, gt, ge, gr, gs, gb, t4 = backward(near, dims, counts, output_cotangent[:, 0], o_w, o_r, own_ew, own_er, triple, pt,
                                               att, mixed, n2, normed, xp, sv, eb)
    if not near:
        scatter = lambda v, axis: lax.psum_scatter(v.astype(F32), AXES, scatter_dimension=axis, tiled=True)
        gt, ge, gr = scatter(gt.reshape(D, -1), 0), scatter(ge.reshape(D, -1), 0), scatter(gr.reshape(FF, D), 0)
        gs, gb, t4 = scatter(gs, 1), scatter(gb, 1), lax.psum(t4, AXES)
    n, rr = expand_bias.shape[0], reduce_weight.shape[0]
    image = jax.ShapeDtypeStruct((2, TOK, D), BF16)
    shapes = [(rows, 3 * D), (rows, D), (rows, FF), (rr, D), (HEADS, EXT * EXT)] + [(rows,)] * 8 + [(n,)]
    out, dx, tr, mg, ex, re, table, *vec = pl.pallas_call(
        finish_kernel, out_shape=[image, image] + [jax.ShapeDtypeStruct(s, F32) for s in shapes],
        in_specs=[VM] * 9, out_specs=[VM] * (2 + len(shapes)), name="finish",
        compiler_params=pltpu.CompilerParams(vmem_limit_bytes=VMEM_LIMIT),
    )(jnp.asarray(TARGET), out, dx, gt, ge, gr, gs, gb, t4)
    return (out[:, None], dx[:, None], tr, mg, ex, re, *vec[:7], vec[8], vec[7], table.T)


def solution(mesh):
    image = P(None, AXES, None, None)
    rows = P(AXES, None)
    vec = P(AXES)
    return jax.shard_map(
        functools.partial(shards, mesh_dims(mesh)), mesh=mesh,
        in_specs=(image, P(None, AXES), image) + (rows,) * 4 + (vec,) * 9 + (P(),),
        out_specs=(image, image) + (rows,) * 4 + (vec,) * 9 + (P(),),
        check_vma=False)
```

```python
import math
import functools

import numpy as np
import jax
import jax.numpy as jnp
from jax import lax
from jax.experimental import pallas as pl
from jax.experimental.pallas import tpu as pltpu
from jax.sharding import PartitionSpec as P

D = 768
FF = 3072
HEADS = 24
HEAD_DIM = 32
WIN = 12
SIDE = 24
SHIFT = 6
TOK = SIDE * SIDE
ROWS = 2 * TOK
WT = WIN * WIN
EXT = 2 * WIN - 1
GROUPS = 3
GH = HEADS // GROUPS
GW = GH * HEAD_DIM
QL = GH * WT
SCALE = HEAD_DIM ** -0.5
MASKED = -1e30
EPS = 1e-5
F32 = jnp.float32
BF16 = jnp.bfloat16
VMEM_LIMIT = 63 << 20
AXES = ("dp", "fsdp")
MESH = pl.DeviceIdType.MESH
ANY = pl.BlockSpec(memory_space=pl.ANY)
VM = pl.BlockSpec(memory_space=pltpu.VMEM)
SM = pl.BlockSpec(memory_space=pltpu.SMEM)
every = slice(None)

NN = (((1,), (0,)), ((), ()))
NT = (((1,), (1,)), ((), ()))
TN = (((0,), (0,)), ((), ()))


def dot(a, b, dims=NN):
    return lax.dot_general(a, b, dims, preferred_element_type=F32)


def layout_constants():
    j = np.arange(WT)
    reg = lambda c: (c >= SIDE - WIN).astype(np.int32) + (c >= SIDE - SHIFT).astype(np.int32)
    raster, label = np.zeros((4, WT), np.int32), np.zeros((4, WT), np.int32)
    for w in range(4):
        rr = (w // 2) * WIN + j // WIN
        rc = (w % 2) * WIN + j % WIN
        raster[w] = ((rr + SHIFT) % SIDE) * SIDE + (rc + SHIFT) % SIDE
        label[w] = reg(rr) * 3 + reg(rc)
    target = np.full((4, WT), -1, np.int32)
    for p in range(4):
        r = j // WIN + (WIN - 1 if p // 2 == 0 else -1)
        s = j % WIN + (WIN - 1 if p % 2 == 0 else -1)
        target[p] = np.where((r >= 0) & (s >= 0), r * EXT + s, -1)
    spread = lambda v: np.broadcast_to(v.reshape(1, TOK), (8, TOK)).astype(np.int32)
    return np.broadcast_to(np.tile(label, (1, GH))[:, None, :], (4, 8, QL)).astype(np.int32), spread(target), spread(raster)


LABEL_Q, TARGET, RASTER_Q = layout_constants()


def fill_places(raster, label=None):
    j = lax.broadcasted_iota(jnp.int32, (WT, 128), 0)
    a = (j * 171) >> 11
    c = j - a * WIN
    reg = lambda v: (v >= SIDE - WIN).astype(jnp.int32) + (v >= SIDE - SHIFT).astype(jnp.int32)
    turn = lambda v: jnp.where(v >= SIDE - SHIFT, v + SHIFT - SIDE, v + SHIFT)
    for w in range(4):
        rr, rc = a + (w // 2) * WIN, c + (w % 2) * WIN
        raster[w] = turn(rr) * SIDE + turn(rc)
        if label is not None:
            label[w] = reg(rr) * 3 + reg(rc)


def lane_iota(shape):
    return lax.broadcasted_iota(jnp.int32, shape, len(shape) - 1)


def aligned(v, n):
    return v if isinstance(v, int) else pl.multiple_of(v, n)


def lanes(start, width):
    return pl.ds(aligned(start, 128), width)


def window(i):
    return pl.ds(aligned(i * WT, WT), WT)


def to_window(raster, w):
    return (raster[w][:, 0:1] == lane_iota((WT, TOK))).astype(BF16)


def to_raster(raster_q, m):
    t = lax.broadcasted_iota(jnp.int32, (WT, TOK), 0) + m * WT
    return (raster_q[0:1, :] == t).astype(BF16)


def stats(x):
    mean = jnp.mean(x, axis=-1, keepdims=True)
    center = x - mean
    var = jnp.mean(center * center, axis=-1, keepdims=True)
    inv = lax.rsqrt(var + EPS)
    return center * inv, inv


def head_stack(dst, x):
    lane = lane_iota(x.shape) // HEAD_DIM
    zero = jnp.zeros_like(x)
    for h in range(GH):
        dst[h * WT:(h + 1) * WT, :] = jnp.where(lane == h, x, zero)


def head_pick(o):
    lane = lane_iota((WT, GW)) // HEAD_DIM
    out = jnp.where(lane == 0, o[0:WT], 0.0)
    for h in range(1, GH):
        out = jnp.where(lane == h, o[h * WT:(h + 1) * WT], out)
    return out


def onehot(target_ref):
    t = lax.broadcasted_iota(jnp.int32, (EXT * EXT, 4 * WT), 0)
    return (t == target_ref[0:1, :]).astype(F32)


def table_rows(table_ref, target_ref, t4):
    t4[...] = lax.dot_general(table_ref[...], onehot(target_ref), NN,
                              precision=lax.Precision.HIGHEST, preferred_element_type=F32) * (1.0 / SCALE)


def spread_bias(g, t4, bias, rowbuf):
    a_of = (lane_iota((1, QL)) % WT) // WIN
    c_of = lane_iota((16, QL)) % WIN
    rows = []
    for p in range(4):
        acc = jnp.zeros((1, QL), F32)
        for h in range(GH):
            piece = t4[pl.ds(g * GH + h, 1), p * WT:(p + 1) * WT]
            piece = jnp.concatenate([piece, jnp.zeros((1, QL - WT), F32)], axis=1)
            acc = acc + (pltpu.roll(piece, h * WT, axis=1) if h else piece)
        rows.append(acc)
    for s in range(2):
        for b in range(WIN):
            pos = pltpu.roll(rows[s], WIN * b, axis=1) if b else rows[s]
            neg = pltpu.roll(rows[2 + s], (WIN * b - WT) % QL, axis=1)
            rowbuf[s, b:b + 1, :] = jnp.where(a_of >= b, pos, neg)
    for d in range(WIN):
        pos = pltpu.roll(rowbuf[0], d, axis=1) if d else rowbuf[0]
        neg = pltpu.roll(rowbuf[1], (d - WIN) % QL, axis=1)
        both = jnp.where(c_of >= d, pos, neg)
        for n in range(9):
            bias[g * 9 + n, pl.ds(d, WIN, stride=WIN), :] = both[0:WIN, n * 128:(n + 1) * 128]


def gather_bias(g, bgrad, accbuf, t4):
    a_of = (lane_iota((1, QL)) % WT) // WIN
    c_of = lane_iota((WIN, QL)) % WIN
    pos = jnp.zeros((WIN, QL), F32)
    neg = jnp.zeros((WIN, QL), F32)
    for d in range(WIN):
        r = jnp.concatenate([bgrad[n, pl.ds(d, WIN, stride=WIN), :] for n in range(9)], axis=1)
        p = jnp.where(c_of >= d, r, 0.0)
        pos = pos + (pltpu.roll(p, QL - d, axis=1) if d else p)
        if d:
            neg = neg + pltpu.roll(jnp.where(c_of < d, r, 0.0), WIN - d, axis=1)
    accbuf[0, 0:WIN, :] = pos
    accbuf[1, 0:WIN, :] = neg
    for s in range(2):
        pp = jnp.zeros((1, QL), F32)
        nn = jnp.zeros((1, QL), F32)
        for b in range(WIN):
            r = accbuf[s, b:b + 1, :]
            p = jnp.where(a_of >= b, r, 0.0)
            pp = pp + (pltpu.roll(p, QL - WIN * b, axis=1) if b else p)
            if b:
                nn = nn + pltpu.roll(jnp.where(a_of < b, r, 0.0), WT - WIN * b, axis=1)
        for part, row in ((s, pp), (2 + s, nn)):
            for h in range(GH):
                moved = pltpu.roll(row, QL - h * WT, axis=1) if h else row
                t4[pl.ds(g * GH + h, 1), part * WT:(part + 1) * WT] = moved[:, 0:WT]


ERF_SLOPE = 0.35
ERF_FIT = (0.19434814435164116, 0.235843067071591, -0.008625688056468914, 0.6849613674275746, -0.6811631064960405, 0.7727015621272543, -0.19806535099226122)


def gelu_pair(v):
    e = jnp.exp(v * v * -0.5)
    t = 1.0 / (1.0 + jnp.abs(v) * (ERF_SLOPE * math.sqrt(0.5)))
    poly = jnp.full_like(t, 0.5 * ERF_FIT[-1])
    for c in ERF_FIT[-2::-1]:
        poly = poly * t + 0.5 * c
    tail = poly * t * e
    cdf = jnp.where(v >= 0, 1.0 - tail, tail)
    return v * cdf, cdf + v * e * (1.0 / math.sqrt(2.0 * math.pi))


def norm_back(hat, inv, gain, grad):
    scaled = grad * gain
    return inv * (scaled - jnp.mean(scaled, axis=-1, keepdims=True)
                  - hat * jnp.mean(scaled * hat, axis=-1, keepdims=True))


class Place:
    def __init__(self, dims):
        self.nz, self.ny, self.nx = dims
        f = lax.axis_index("fsdp")
        self.z = lax.axis_index("dp")
        self.c = lax.rem(f, 2)
        self.x = lax.rem(f // 2, self.nx)
        self.y = f // (2 * self.nx)

    def size(self, axis):
        return {"z": self.nz, "y": self.ny, "x": self.nx, "c": 2}[axis]

    def at(self, axis):
        return {"z": self.z, "y": self.y, "x": self.x, "c": self.c}[axis]

    def step(self, axis, k):
        return lax.rem(self.at(axis) + k, self.size(axis))

    def back(self, axis, k):
        return self.step(axis, self.size(axis) - k)

    def device(self, axis, k):
        p = {a: (self.step(a, k) if a == axis else self.at(a)) for a in "zyxc"}
        return (p["z"], (p["y"] * self.nx + p["x"]) * 2 + p["c"])

    def greet(self):
        barrier = pltpu.get_barrier_semaphore()
        total = 0
        for axis in "czyx":
            for k in range(1, self.size(axis)):
                pl.semaphore_signal(barrier, inc=1, device_id=self.device(axis, k), device_id_type=MESH)
                total += 1
        pl.semaphore_wait(barrier, total)


def mesh_dims(mesh):
    chips = mesh.shape["fsdp"] // 2
    ny = max(n for n in range(1, chips + 1) if n * n <= chips and chips % n == 0)
    return mesh.shape["dp"], ny, chips // ny


class Swap:
    def __init__(self, place, axis, sems, src, dst, came, has=None):
        self.has = has
        self.place, self.axis, self.sems = place, axis, sems
        self.src, self.dst, self.came = src, dst, came

    def make(self, k, src, dst):
        return pltpu.make_async_remote_copy(
            src_ref=src(k), dst_ref=dst(k), send_sem=self.sems[0](k), recv_sem=self.sems[1](k),
            device_id=self.place.device(self.axis, k), device_id_type=MESH)

    def peers(self):
        return range(1, self.place.size(self.axis))

    def each(self, sender, act):
        for k in self.peers():
            if self.has is None:
                act(k)
            else:
                pl.when(self.has(sender(k)))(lambda k=k: act(k))

    def start(self):
        self.each(lambda k: self.place.at(self.axis), lambda k: self.make(k, self.src, self.dst).start())

    def arrive(self):
        self.each(lambda k: self.place.back(self.axis, k), lambda k: self.make(k, self.came, self.came).wait_recv())

    def done(self):
        self.each(lambda k: self.place.at(self.axis), lambda k: self.make(k, self.src, self.dst).wait_send())


def when(cond, body):
    if isinstance(cond, (bool, np.bool_)):
        if cond:
            body()
    else:
        pl.when(cond)(body)


def both(*conds):
    out = True
    for c in conds:
        if isinstance(c, (bool, np.bool_)):
            if not c:
                return False
        else:
            out = c if out is True else jnp.logical_and(out, c)
    return out


def twos(n, body):
    lax.fori_loop(0, n // 2, lambda i, _: (body(2 * i, 0), body(2 * i + 1, 0))[0], 0)


def call(kernel, outs, scratch, ins, name):
    return pl.pallas_call(
        kernel, out_shape=[jax.ShapeDtypeStruct(s, d) for s, d in outs], in_specs=[VM] * len(ins),
        out_specs=[VM] * len(outs), scratch_shapes=scratch, name=name,
        compiler_params=pltpu.CompilerParams(vmem_limit_bytes=VMEM_LIMIT))(*ins)


HALF = 4 * D
TM_HALF = 2 * D
FF_HALF = FF // 2
FF_PART = FF // 4


class Gather:
    def __init__(self, place, w, half, base, n_w, r, part, send, recv):
        self.place = place
        self.w, self.half, self.base, self.n_w, self.r, self.part = w, half, base, n_w, r, part
        self.send, self.recv = send, recv
        self.n = n_w + 3

    def block(self, wide, p, c, ab=None):
        if wide:
            at, n = c * self.half + self.base + p * 256, 256
            return (every, lanes(at, n) if ab is None else lanes(at + ab * 128, 128))
        n = self.r.shape[3] // 2
        return (every if ab is None else pl.ds(ab * n, n), lanes(c * (D // 2) + p * 128, 128))

    def swaps(self, wide, p, s):
        return [self.swap(wide, p, s, ab) for ab in ((None,) if s in (0, 3) else (0, 1))]

    def swap(self, wide, p, s, ab):
        pc = self.place
        ref = self.w if wide else self.r
        q = p if wide else self.n_w + p
        n = {0: 0, 1: 1, 2: 3, 3: 5}[s] + (ab or 0)
        sems = (lambda k: self.send.at[q, n, k - 1], lambda k: self.recv.at[q, n, k - 1])
        blk = self.block(wide, p, pc.c, ab)
        zs = every if wide else pl.ds(self.part * (pc.nz // 2), pc.nz // 2)
        at = lambda zz, yy, xx, b=blk: ref.at[(zz, yy, xx) + b]
        z, y, x = pc.z, pc.y, pc.x
        if s == 0:
            has = None if wide else (lambda zz: (zz >= pc.nz // 2) == (self.part == 1))
            own = lambda k: at(z, y, x)
            return Swap(pc, "z", sems, own, own, lambda k: at(pc.back("z", k), y, x), has)
        if s == 3:
            mine = lambda k: at(zs, every, every)
            return Swap(pc, "c", sems, mine, mine, lambda k: at(zs, every, every, self.block(wide, p, 1 - pc.c)))
        first = "xy"[ab]
        if s == 1:
            own = lambda k: at(zs, y, x)
            if first == "x":
                return Swap(pc, "x", sems, own, own, lambda k: at(zs, y, pc.back("x", k)))
            return Swap(pc, "y", sems, own, own, lambda k: at(zs, pc.back("y", k), x))
        if first == "x":
            own = lambda k: at(zs, y, every)
            return Swap(pc, "y", sems, own, own, lambda k: at(zs, pc.back("y", k), every))
        own = lambda k: at(zs, every, x)
        return Swap(pc, "x", sems, own, own, lambda k: at(zs, every, pc.back("x", k)))

    def on_piece(self, p, body):
        when(both(p >= 0, p < self.n_w), lambda: body(True, p))
        when(both(p >= self.n_w, p < self.n), lambda: body(False, p - self.n_w))

    def tick(self, u, landed=None):
        def last(wide, p):
            for swap in self.swaps(wide, p, 3):
                swap.arrive()
            if landed is not None:
                landed(wide, p)

        def step(s):
            def body(wide, p):
                if s:
                    for swap in self.swaps(wide, p, s - 1):
                        swap.arrive()
                for swap in self.swaps(wide, p, s):
                    swap.start()
            return body

        self.on_piece(u - 8, last)
        for s in (3, 2, 1, 0):
            self.on_piece(u - 2 * s, step(s))

    def finish(self):
        for q in range(self.n):
            for s in range(4):
                for swap in self.swaps(q < self.n_w, q if q < self.n_w else q - self.n_w, s):
                    swap.done()


def small_swap(pc, sb, send, recv, s):
    sems = (lambda k: send.at[s, k - 1], lambda k: recv.at[s, k - 1])
    at = lambda zz, yy, xx, c=pc.c: sb.at[zz, yy, xx, c]
    z, y, x = pc.z, pc.y, pc.x
    own = [lambda k: at(z, y, x), lambda k: at(every, y, x), lambda k: at(every, y, every),
           lambda k: at(every, every, every)][s]
    came = [lambda k: at(pc.back("z", k), y, x), lambda k: at(every, y, pc.back("x", k)),
            lambda k: at(every, pc.back("y", k), every), lambda k: at(every, every, every, 1 - pc.c)][s]
    return Swap(pc, "zxyc"[s], sems, own, own, came)


def place_small(sb, sv, eb, n_small, n_wide):
    nz, ny, nx = sb.shape[:3]
    for out, row0, width, total in ((sv, 0, n_small, D), (eb, 8, n_wide, FF)):
        tiles = [jnp.zeros((8, 128), F32) for _ in range(total // 128)]
        lane = lane_iota((8, 128))
        n = 0
        for q in range(nz * ny * nx):
            for c in range(2):
                blk = sb[q // (ny * nx), (q // nx) % ny, q % nx, c, row0:row0 + 8, :]
                tile, off = divmod(n * width, 128)
                moved = pltpu.roll(blk, off, axis=1) if off else blk
                end = off + width
                tiles[tile] = jnp.where((lane >= off) & (lane < min(end, 128)), moved, tiles[tile])
                if end > 128:
                    tiles[tile + 1] = jnp.where(lane < end - 128, moved, tiles[tile + 1])
                n += 1
        out[...] = jnp.concatenate(tiles, axis=1)


def group_cols(g):
    return (((0, g * 384, 256),), ((0, g * 384 + 256, 128), (1, g * 384, 128)), ((1, g * 384 + 128, 256),))


def merge_cols(n):
    return tuple((b // 3, 1152 + lax.rem(b, 3) * 128, 128) for b in (2 * n, 2 * n + 1))


def columns(ref, parts, half):
    take = [ref[:, lanes(h * half + lo, n)] for h, lo, n in parts]
    return take[0] if len(take) == 1 else jnp.concatenate(take, axis=1)


class Flat:
    def __init__(self, ref):
        self.ref = ref

    def __getitem__(self, idx):
        v = self.ref[:, :, :, :, idx[1]]
        return v.reshape(-1, v.shape[-1])


def own_halves(h):
    for g in range(GROUPS):
        yield 0, g * GW + h * 2 * D, g * 384 + h * 128, 256
        yield 0, D + g * GW + h * 128, g * 384 + 256 * (1 - h), 128
    yield 1, h * (D // 2), 1152, D // 2
    for s in range(2):
        yield 2, s * FF_HALF + h * FF_PART, TM_HALF + s * FF_PART, FF_PART
    yield 3, h * (D // 2), 0, D // 2


def forward_kernel(near, dims, counts, x, labq, target, table, *rest):
    n_in = 13 if near else 4
    given = rest[:n_in]
    (o_w, o_r, o_triple, o_pt, o_att, o_mixed, o_n2, o_normed, o_xp, sv, eb, o_ew, o_er,
     w, r, sb, stage_w, stage_r, xp, normed, triple, attended, mixed, n2, pt, t4, bias, rowbuf, qs, st, lk, raster, labk,
     send, recv, ssend, srecv, lsem, psem) = rest[n_in:]

    def keep(n, src, dst):
        return pltpu.make_async_copy(src, dst, lsem.at[n])

    if near:
        pc = Place(dims)
        gather = Gather(pc, w, HALF, 0, 9, r, 0, send, recv)

    def part_of(wide, p):
        zs = every if wide else pl.ds(0, dims[0] // 2)
        for c in range(2):
            n = 2 * (p if wide else 9 + p) + c
            blk = (zs, every, every) + gather.block(wide, p, c)
            yield (keep(n, w.at[blk], o_w.at[blk]) if wide else keep(n, r.at[blk], o_r.at[blk]))

    def landed(wide, p):
        for copy in part_of(wide, p):
            copy.start()

    def small_tick(u):
        if u:
            small_swap(pc, sb, ssend, srecv, u // 2 - 1).arrive()
        if u < 8:
            small_swap(pc, sb, ssend, srecv, u // 2).start()

    if near:
        pc.greet()
        own, vectors = given[:4], given[4:]
        first = []
        for i, ((n, src, dst, width), (_, _, back, _)) in enumerate(zip(own_halves(1 - pc.c), own_halves(pc.c))):
            ref, stage = own[n], (stage_r if n == 3 else stage_w)
            rows = lambda c, m=ref.shape[0]: pl.ds(aligned(c * m, 8), m)
            sems = (lambda k, i=i: ssend.at[4 + i, 0], lambda k, i=i: srecv.at[4 + i, 0])
            first.append(Swap(pc, "c", sems, lambda k, v=ref.at[:, lanes(src, width)]: v,
                              lambda k, v=stage.at[rows(pc.c), lanes(dst, width)]: v,
                              lambda k, v=stage.at[rows(1 - pc.c), lanes(back, width)]: v))
        for s in first:
            s.start()
        sb[pc.z, pc.y, pc.x, pc.c] = jnp.zeros((16, 128), F32)
        for k, v in enumerate(vectors):
            sb[pc.z, pc.y, pc.x, pc.c, k, 0:v.shape[0]] = v[...].astype(BF16).astype(F32)
        for n, src, dst, width in own_halves(pc.c):
            ref, stage = own[n], (stage_r if n == 3 else stage_w)
            stage[pl.ds(aligned(pc.c * ref.shape[0], 8), ref.shape[0]), lanes(dst, width)] = ref[:, lanes(src, width)]
        for s in first[:7]:
            s.arrive()
        w[pc.z, pc.y, pc.x, :, lanes(pc.c * HALF, TM_HALF)] = stage_w[:, 0:TM_HALF].astype(BF16)
        gather.tick(0, landed)
        small_tick(0)
        gather.tick(1, landed)
        for s in first[7:9]:
            s.arrive()
        w[pc.z, pc.y, pc.x, :, lanes(pc.c * HALF + TM_HALF, FF_HALF)] = stage_w[:, TM_HALF:].astype(BF16)
        first[-1].arrive()
        r[pc.z, pc.y, pc.x, :, lanes(pc.c * (D // 2), D // 2)] = stage_r[...].astype(BF16)
        o_ew[...] = stage_w[:, TM_HALF + FF_PART:HALF].astype(BF16)
        o_er[...] = stage_r[...].astype(BF16)
    else:
        wown, rown, sv_in, eb_in = given
        loads = [keep(0, wown, w), keep(1, rown, r)]
        for c in loads:
            c.start()
        for c in loads:
            c.wait()
        sv[...] = sv_in[...]
        eb[...] = eb_in[...]

    def permute(i, _):
        xp[window(i), :] = dot(to_window(raster, i % 4), x[i // 4]).astype(BF16)
        return 0

    fill_places(raster, labk)
    table_rows(table, target, t4)

    def prologue(u, _):
        if near:
            gather.tick(u, landed)
            for k in range(1, 5):
                pl.when(u == 2 * k)(lambda k=k: small_tick(2 * k))

        @pl.when(u < 5)
        def _():
            spread_bias(u - 2, t4, bias, rowbuf)

        @pl.when(jnp.logical_and(u >= 5, u < 9))
        def _():
            permute(2 * (u - 5), 0)
            permute(2 * (u - 5) + 1, 0)

        return 0

    lax.fori_loop(2, 10, prologue, 0)
    if near:
        place_small(sb, sv, eb, given[0].shape[0], given[3].shape[0])

    def ln1(i, _):
        hat, _i = stats(xp[window(i), :].astype(F32))
        normed[window(i), :] = (hat * sv[0:1, :] + sv[1:2, :]).astype(BF16)
        return 0

    twos(8, ln1)
    keep(24, xp, o_xp).start()
    keep(25, normed, o_normed).start()
    wf = Flat(w)

    def products(i, g, u):
        rows, v = window(i), i % 4
        lk[u] = jnp.where(raster[v] < counts[i // 4], labk[v], -1)
        head_stack(qs.at[u], triple[rows, lanes(g * D, GW)])
        st[u] = dot(triple[rows, lanes(g * D + GW, GW)], qs[u], NT)

    def softmax(i, g, u):
        for n in range(9):
            c = lanes(n * 128, 128)
            s = st[u, :, c] + bias[g * 9 + n]
            s = jnp.where(lk[u] == labq[i % 4, 0:1, c], s, MASKED)
            m = jnp.max(s, axis=0, keepdims=True)
            e = jnp.exp((s - m) * SCALE)
            tot = jnp.sum(e, axis=0, keepdims=True)
            pt[u, :, c] = (e * (1.0 / tot)).astype(BF16)

    def attend(i, g, u):
        rows = window(i)
        pltpu.make_async_copy(pt.at[u], o_pt.at[g * 8 + i], psem.at[u]).start()
        out = head_pick(dot(pt[u], triple[rows, lanes(g * D + 2 * GW, GW)], TN))
        valid = raster[i % 4] < counts[i // 4]
        vq = jnp.concatenate([valid, valid], axis=1)
        attended[rows, lanes(g * GW, GW)] = jnp.where(vq, out, 0.0).astype(BF16)

    def quarter(q, _):
        g = q // 4

        @pl.when(q % 4 == 0)
        def _():
            for k, parts in enumerate(group_cols(g)):
                v = dot(normed[...], columns(wf, parts, HALF))
                if k != 1:
                    v = v + sv[2 + k // 2:3 + k // 2, lanes(g * GW, GW)]
                triple[:, lanes(g * D + k * GW, GW)] = v.astype(BF16)

        @pl.when(q >= 1)
        def _():
            for u in range(2):
                pltpu.make_async_copy(pt.at[u], o_pt.at[0], psem.at[u]).wait()

        i = 2 * lax.rem(q, 4)
        products(i, g, 0)
        products(i + 1, g, 1)
        softmax(i, g, 0)
        attend(i, g, 0)
        softmax(i + 1, g, 1)
        attend(i + 1, g, 1)
        if near:
            gather.tick(10 + q, landed)
        return 0

    lax.fori_loop(0, 4 * GROUPS, quarter, 0)
    keep(26, triple, o_triple).start()
    keep(27, attended, o_att).start()
    def merge(n, _):
        cols = lanes(n * 256, 256)
        v = dot(attended[...], columns(wf, merge_cols(n), HALF))
        mixed[:, cols] = xp[:, cols].astype(F32) + v + sv[4:5, cols]
        return 0

    lax.fori_loop(0, 3, merge, 0)
    keep(28, mixed, o_mixed).start()

    def ln2(i, _):
        hat, _i = stats(mixed[window(i), :])
        n2[window(i), :] = (hat * sv[5:6, :] + sv[6:7, :]).astype(BF16)
        return 0

    twos(8, ln2)
    keep(29, n2, o_n2).start()
    if near:
        gather.finish()
        for s in first:
            s.done()
        for s in range(4):
            small_swap(pc, sb, ssend, srecv, s).done()
        for q in range(12):
            for copy in part_of(q < 9, q if q < 9 else q - 9):
                copy.wait()
    for n, src, dst in ((24, xp, o_xp), (25, normed, o_normed), (26, triple, o_triple), (27, attended, o_att),
                        (28, mixed, o_mixed), (29, n2, o_n2)):
        keep(n, src, dst).wait()
    for slot in range(2):
        pltpu.make_async_copy(pt.at[slot], o_pt.at[0], psem.at[slot]).wait()


def forward(near, dims, counts, x, table, *given):
    nz, ny, nx = dims if near else (1, 1, 1)
    rw, rr = (given[0].shape[0] * 2, given[3].shape[0] * 2) if near else (D, FF)
    peers = max(nz, ny, nx, 2) - 1
    full_w, full_r = (nz, ny, nx, rw, 2 * HALF), (nz, ny, nx, rr, D)
    tiny = (8, 128)
    outs = [(full_w if near else tiny, BF16), (full_r if near else tiny, BF16), ((ROWS, 3 * D), BF16),
            ((8 * GROUPS, WT, QL), BF16), ((ROWS, D), BF16), ((ROWS, D), F32), ((ROWS, D), BF16), ((ROWS, D), BF16),
            ((ROWS, D), BF16), ((8, D), F32), ((8, FF), F32), ((rw, FF_PART) if near else tiny, BF16),
            ((rr, D // 2) if near else tiny, BF16)]
    if not near:
        given = (given[0].reshape(full_w), given[1].reshape(full_r)) + given[2:]
    vm = pltpu.VMEM
    dma = pltpu.SemaphoreType.DMA
    scratch = [vm(full_w, BF16), vm(full_r, BF16), vm((nz, ny, nx, 2, 16, 128), F32), vm((rw if near else 8, HALF), F32),
               vm((rr if near else 8, D // 2), F32), vm((ROWS, D), BF16), vm((ROWS, D), BF16), vm((ROWS, 3 * D), BF16),
               vm((ROWS, D), BF16), vm((ROWS, D), F32), vm((ROWS, D), BF16), vm((2, WT, QL), BF16),
               vm((HEADS, 4 * WT), F32), vm((GROUPS * 9, WT, 128), F32), vm((2, 16, QL), F32), vm((2, QL, GW), BF16),
               vm((2, WT, QL), F32), vm((2, WT, 128), jnp.int32), vm((4, WT, 128), jnp.int32), vm((4, WT, 128), jnp.int32),
               dma((12, 6, peers)), dma((12, 6, peers)), dma((14, peers)), dma((14, peers)), dma((30,)), dma((2,))]
    params = dict(collective_id=0, has_side_effects=True) if near else {}
    return pl.pallas_call(
        functools.partial(forward_kernel, near, dims),
        out_shape=[jax.ShapeDtypeStruct(s, d) for s, d in outs],
        in_specs=[SM] + [VM] * 4 + ([VM] * 13 if near else [ANY, ANY, VM, VM]),
        out_specs=[ANY] * 9 + [VM] * 4,
        scratch_shapes=scratch, name="forward",
        compiler_params=pltpu.CompilerParams(vmem_limit_bytes=VMEM_LIMIT, **params),
    )(counts, x, jnp.asarray(LABEL_Q), jnp.asarray(TARGET), table.T,
      *given)


class Scatter:
    def __init__(self, place, bufs, send, recv):
        self.place = place
        self.bufs, self.send, self.recv = bufs, send, recv

    def src(self, kind, g, i, ab, c):
        if kind == "r":
            n = g.shape[3] // 2
            return g.at[every, every, every, pl.ds(ab * n, n), lanes(c * (D // 2) + i * 128, 128)]
        return g.at[every, every, every, every, lanes(c * FF_HALF + i * 256 + ab * 128, 128)]

    def swap(self, kind, g, out, i, ab, s):
        pc = self.place
        r0, r1, r2, r3, fin = self.bufs[kind]
        q = {"e": 0, "t": 6, "r": 12}[kind] + i
        sems = (lambda k: self.send.at[q, ab, s, k - 1], lambda k: self.recv.at[q, ab, s, k - 1])
        first, second = ("y", "x") if ab == 0 else ("x", "y")
        if s == 0:
            to = lambda k: r0.at[i, ab]
            return Swap(pc, "c", sems, lambda k: self.src(kind, g, i, ab, 1 - pc.c), to, to)
        if s == 1:
            to = lambda k: r1.at[i, ab, k - 1]
            at = lambda k: (every, pc.step("y", k), every) if first == "y" else (every, every, pc.step("x", k))
            return Swap(pc, first, sems, lambda k: r0.at[(i, ab) + at(k)], to, to)
        if s == 2:
            to = lambda k: r2.at[i, ab, k - 1]
            return Swap(pc, second, sems, lambda k: r1.at[i, ab, 0, every, pc.step(second, k)], to, to)
        if s == 3:
            to = lambda k: r3.at[i, ab, k - 1]
            return Swap(pc, "z", sems, lambda k: r2.at[i, ab, 0, pc.step("z", k)], to, to)
        n = out.shape[0]
        if kind == "r":
            cols = lambda c: lanes(c * (D // 2) + i * 128, 128)
            return Swap(pc, "c", sems, lambda k: fin.at[i, 1 - pc.c], lambda k: out.at[:, cols(pc.c)],
                        lambda k: out.at[:, cols(1 - pc.c)])
        cols = lambda c: lanes(c * FF_HALF + i * 256 + ab * 128, 128)
        return Swap(pc, "c", sems, lambda k: fin.at[i, ab, pl.ds(aligned((1 - pc.c) * n, 8), n), :],
                    lambda k: out.at[:, cols(pc.c)], lambda k: out.at[:, cols(1 - pc.c)])

    def advance(self, kind, g, out, i, s):
        pc = self.place
        r0, r1, r2, r3, fin = self.bufs[kind]
        if s == 5:
            for ab in range(1 if kind == "r" else 2):
                self.swap(kind, g, out, i, ab, 4).arrive()
            return
        for ab in range(2):
            first, second = ("y", "x") if ab == 0 else ("x", "y")
            if s:
                self.swap(kind, g, out, i, ab, s - 1).arrive()
            if s == 1:
                n = r0.shape[-2]

                def add(z, _):
                    if kind == "r":
                        own = g[z, :, :, ab * n:(ab + 1) * n, lanes(pc.c * (D // 2) + i * 128, 128)]
                    else:
                        own = g[z, :, :, :, lanes(pc.c * FF_HALF + i * 256 + ab * 128, 128)]
                    r0[i, ab, z] = (r0[i, ab, z].astype(F32) + own.astype(F32)).astype(BF16)
                    return 0

                lax.fori_loop(0, pc.nz, add, 0)
            if s == 2:
                at = (every, pc.y, every) if first == "y" else (every, every, pc.x)
                v = r0[(i, ab) + at].astype(F32)
                for k in range(pc.size(first) - 1):
                    v = v + r1[i, ab, k].astype(F32)
                r1[i, ab, 0] = v.astype(BF16)
            if s == 3:
                v = r1[i, ab, 0, :, pc.at(second)].astype(F32)
                for k in range(pc.size(second) - 1):
                    v = v + r2[i, ab, k].astype(F32)
                r2[i, ab, 0] = v.astype(BF16)
            if s == 4:
                v = r2[i, ab, 0, pc.z].astype(F32)
                for k in range(pc.nz - 1):
                    v = v + r3[i, ab, k].astype(F32)
                fin[i, ab] = v
                if kind != "r":
                    n = out.shape[0]
                    out[:, lanes(pc.c * FF_HALF + i * 256 + ab * 128, 128)] = fin[i, ab, pl.ds(aligned(pc.c * n, 8), n), :]
            if s < 4 or kind != "r":
                self.swap(kind, g, out, i, ab, s).start()
        if s == 4 and kind == "r":
            out[:, lanes(pc.c * (D // 2) + i * 128, 128)] = fin[i, pc.c]
            self.swap(kind, g, out, i, 0, 4).start()

    def done(self, kind, g, out, pieces, steps):
        for i in range(pieces):
            for s in steps:
                for ab in range(1 if (kind == "r" and s == 4) else 2):
                    self.swap(kind, g, out, i, ab, s).done()


class SmallSum:
    def __init__(self, place, slots, send, recv):
        self.place, self.slots, self.send, self.recv = place, slots, send, recv

    def base(self, i):
        return sum(self.place.size(a) for a in "cyxz"[:i])

    def swap(self, i):
        pc, a = self.place, "cyxz"[i]
        sems = (lambda k: self.send.at[i, k - 1], lambda k: self.recv.at[i, k - 1])
        me = lambda k: self.slots.at[self.base(i) + pc.at(a)]
        return Swap(pc, a, sems, me, me, lambda k: self.slots.at[self.base(i) + pc.back(a, k)])

    def start(self):
        self.swap(0).start()

    def advance(self, i):
        self.swap(i).arrive()
        s = self.slots[self.base(i)]
        for k in range(1, self.place.size("cyxz"[i])):
            s = s + self.slots[self.base(i) + k]
        if i == 3:
            return s
        self.slots[self.base(i + 1) + self.place.at("cyxz"[i + 1])] = s
        self.swap(i + 1).start()

    def done(self):
        for i in range(4):
            self.swap(i).done()


def events(t):
    out = [("e", i, s) for i in range(6) for s in range(6) if 2 * i + 1 + 2 * s == t and t >= 12]
    for i, at in enumerate(((12, 14, 16, 18, 20, 22), (13, 15, 17, 19, 21, 23), (14, 15, 18, 20, 22, 24))):
        out += [("r", i, s) for s in range(6) if at[s] == t]
    for pieces, at in (((5,), (16, 18, 20, 22, 24, 26)), ((3, 4), (19, 20, 22, 23, 25, 26)), ((2,), (21, 22, 24, 25, 27, 28)),
                       ((0, 1), (23, 24, 26, 27, 29, 30))):
        out += [("t", i, s) for i in pieces for s in range(6) if at[s] == t]
    return sorted(out, key=lambda e: -e[2])


def backward_kernel(near, dims, counts, rasq, do, w, r, own_ew, own_er, triple_h, pt_h, att_h, mixed_h, n2_h, normed_h,
                    xp_h, sv, eb, o_out, o_dx, o_act, o_t, o_e, o_r, o_small, o_deb, o_t4,
                    raster, ew, rw, dop, dn2, mixed, part, e0, e1, e2, e3, ef, t0, t1, t2, t3, tf, b0, b1, b2, b3, bf, slots_a, slots_g, late, slots_l, smalls,
                    gsend, grecv, send, recv, ssend, srecv, lsem):
    def load(n, src, dst):
        return pltpu.make_async_copy(src, dst, lsem.at[n])

    if near:
        pc = Place(dims)
        rs = Scatter(pc, {"e": (e0, e1, e2, e3, ef), "t": (t0, t1, t2, t3, tf), "r": (b0, b1, b2, b3, bf)}, send, recv)
        sum_a = SmallSum(pc, slots_a, ssend.at[0], srecv.at[0])
        sum_l = SmallSum(pc, slots_l, ssend.at[1], srecv.at[1])
        sum_g = SmallSum(pc, slots_g, ssend.at[2], srecv.at[2])
        pc.greet()
    else:
        pc = None
    small = smalls
    fill_places(raster)
    small[...] = jnp.zeros(small.shape, F32)

    def feed_forward(n2, n2t, act, hs, ds, hl, de, dr):
        half_z = dims[0] // 2
        loads = [load(0, n2_h, n2), load(3, mixed_h, mixed)]
        if near:
            for c in range(2):
                a, b = lanes(c * HALF + TM_HALF, FF_PART), lanes(c * FF_HALF, FF_PART)
                loads.append(load(4 + c, w.at[:, :, :, :, a], ew.at[:, :, :, :, b]))
            loads.append(load(2, r.at[0:half_z], rw.at[0:half_z]))
        else:
            for c in range(2):
                a, b = lanes(c * HALF + TM_HALF, FF_HALF), lanes(c * FF_HALF, FF_HALF)
                loads.append(load(4 + c, w.at[:, :, :, :, a], ew.at[:, :, :, :, b]))
            loads.append(load(2, r, rw))
        for c in loads:
            c.start()
        if near:
            gather = Gather(pc, ew, FF_HALF, FF_PART, 3, rw, 1, gsend, grecv)
            ew[pc.z, pc.y, pc.x, :, lanes(pc.c * FF_HALF + FF_PART, FF_PART)] = own_ew[...]

            @pl.when(pc.z >= half_z)
            def _():
                rw[pc.z, pc.y, pc.x, :, lanes(pc.c * (D // 2), D // 2)] = own_er[...]

            gather.tick(0)
            gather.tick(1)

        def permute(i, _):
            dop[window(i), :] = dot(to_window(raster, i % 4), do[i // 4]).astype(BF16)
            return 0

        twos(8, permute)
        if near:
            gather.tick(2)
            gather.tick(3)
        for c in loads:
            c.wait()
        n2t[...] = n2[...].T
        dn2[...] = jnp.zeros(dn2.shape, F32)
        small[7:8, :] = jnp.sum(dop[...].astype(F32), axis=0, keepdims=True)
        nz, ny, nx, rr = rw.shape[:4]
        per = FF // 256

        def rows_of(n0):
            return flat_r[pl.ds(aligned(n0, 256), 256), :]

        flat_r = rw.reshape(FF, D)
        fe, fde = Flat(ew), de

        def chunk(j, _):
            s, k = j // 6, j % 6
            c, off = k % 2, k // 2
            col = lanes(c * FF_HALF + s * FF_PART + off * 256, 256)
            n0 = s * FF_HALF + c * FF_PART + off * 256
            nat = lanes(n0, 256)
            weights = fe[:, col]
            rows = rows_of(n0)
            bias = eb[0:1, nat]
            total = jnp.zeros((8, 256), F32)

            def products(m):
                rows_m = pl.ds(m * 288, 288)
                hs[rows_m, :] = dot(n2[rows_m, :], weights)
                ds[rows_m, :] = dot(dop[rows_m, :], rows, NT)

            def gate(m, total):
                for q in range(288 // 32):
                    rr_ = pl.ds(m * 288 + q * 32, 32)
                    a, slope = gelu_pair(hs[rr_, :] + bias)
                    act[rr_, nat] = a.astype(BF16)
                    hg = ds[rr_, :] * slope
                    for p in range(4):
                        total = total + hg[p * 8:(p + 1) * 8]
                    hl[rr_, :] = hg.astype(BF16)
                return total

            products(0)
            for m in range(4):
                if m + 1 < 4:
                    products(m + 1)
                total = gate(m, total)
            small[pl.ds(8 + s * 2 + c, 1), lanes(off * 256, 256)] = jnp.sum(total, axis=0, keepdims=True)
            de[:, :, :, :, col] = dot(n2t[...], hl[...]).astype(BF16).reshape(de.shape[:4] + (256,))
            for n in range(3):
                cc = lanes(n * 256, 256)
                dn2[:, cc] += dot(hl[...], weights[n * 256:(n + 1) * 256], NT)
            if near:
                gather.tick(4 + 2 * j)
                gather.tick(5 + 2 * j)
                for step in range(5, -1, -1):
                    i = j // 2 - step
                    pl.when(jnp.logical_and(lax.rem(j, 2) == 1, i >= 0))(
                        lambda i=i, step=step: rs.advance("e", de, o_e, i, step))
            return 0

        lax.fori_loop(0, per, chunk, 0)

        def er_tick(t):
            for kind, i, s in events(t):
                rs.advance(kind, de if kind == "e" else dr, o_e if kind == "e" else o_r, i, s)

        spill = load(6, act, o_act)
        spill.start()
        flat_dr = dr.reshape(FF, D)

        def reduce_part(n, _):
            def quarter(m, _):
                two = jnp.concatenate([dop[:, lanes(n * 128, 128)], dop[:, lanes(D // 2 + n * 128, 128)]], axis=1)
                v = dot(act[:, lanes(m * D, D)], two, TN).astype(BF16)
                rows = pl.ds(aligned(m * D, D), D)
                flat_dr[rows, lanes(n * 128, 128)] = v[:, :128]
                flat_dr[rows, lanes(D // 2 + n * 128, 128)] = v[:, 128:]
                return 0

            lax.fori_loop(0, 4, quarter, 0)
            if near:
                for t in range(3):
                    pl.when(n == t)(lambda t=t: er_tick(12 + t))
            return 0

        lax.fori_loop(0, 3, reduce_part, 0)

        def ln2b(i, _):
            rows = window(i)
            hat, inv = stats(mixed[rows, :])
            g = dn2[rows, :]
            small[5:6, :] += jnp.sum(g * hat, axis=0, keepdims=True)
            small[6:7, :] += jnp.sum(g, axis=0, keepdims=True)
            m = dop[rows, :].astype(F32) + norm_back(hat, inv, sv[5:6, :], g)
            small[4:5, :] += jnp.sum(m, axis=0, keepdims=True)
            mixed[rows, :] = m
            part[rows, :] = m.astype(BF16)
            return 0

        twos(8, ln2b)
        if near:
            er_tick(15)
            gather.finish()
            rs.done("e", de, o_e, 6, range(1))
            rs.done("r", dr, o_r, 3, range(1))
        else:
            for c in (load(4, de, o_e), load(5, dr, o_r)):
                c.start()
                c.wait()
        spill.wait()

    nz, ny, nx, rw_rows = w.shape[:4]
    rr_rows = r.shape[3]
    vm = pltpu.VMEM
    pl.run_scoped(feed_forward, vm((ROWS, D), BF16),
                  vm((D, ROWS), BF16), vm((ROWS, FF), BF16), vm((ROWS, 256), F32), vm((ROWS, 256), F32), vm((ROWS, 256), BF16),
                  vm((nz, ny, nx, rw_rows, FF), BF16), vm((nz, ny, nx, rr_rows, D), BF16))
    tw = ew
    flat_tw = tw.reshape(D, FF)
    flat_r = rw.reshape(FF, D)

    def after_feed_forward(dt, triple, ml, xp, t4g, sum_keep):
        def ert_tick(t):
            if near:
                for kind, i, s in events(t):
                    rs.advance(kind, {"e": None, "r": None, "t": dt}[kind], {"e": o_e, "r": o_r, "t": o_t}[kind], i, s)

        def put(parts, v):
            at = 0
            for h, lo, n in parts:
                dt[:, :, :, :, lanes(h * TM_HALF + lo, n)] = v[:, at:at + n].reshape(dt.shape[:4] + (n,))
                at += n

        def attention(datt, xt, xn, qs, dos, st, raw, pt, bgrad, accbuf, psem):
            loads = [load(0, att_h, xn), load(1, triple_h, triple), load(2, xp_h, xp)]
            loads += [load(4 + c, w.at[:, :, :, :, lanes(c * HALF, TM_HALF)], tw.at[:, :, :, :, lanes(c * TM_HALF, TM_HALF)])
                      for c in range(2)]
            for c in loads:
                c.start()

            def fetch(step):
                return pltpu.make_async_copy(pt_h.at[(2 - step // 8) * 8 + step % 8], pt.at[step % 4], psem.at[step % 4])

            fetch(0).start()
            fetch(1).start()
            for c in loads:
                c.wait()
            xt[...] = xn[...].T
            again = load(0, normed_h, xn)
            again.start()

            def merge_grad(n, _):
                put(merge_cols(n), dot(xt[...], part[:, lanes(n * 256, 256)]).astype(BF16))
                return 0

            lax.fori_loop(0, 3, merge_grad, 0)
            ert_tick(16)

            def merge_back(n, _):
                rows = pl.ds(aligned(n * 256, 256), 256)
                m = jnp.concatenate([flat_tw[rows, 1152:TM_HALF], flat_tw[rows, TM_HALF + 1152:]], axis=1)
                datt[:, lanes(n * 256, 256)] = dot(part[...], m, NT).astype(BF16)
                return 0

            lax.fori_loop(0, 3, merge_back, 0)
            again.wait()
            xt[...] = xn[...].T
            ert_tick(17)
            if near:
                slots_a[pc.c, 0:4, :] = small[4:8, :]
                slots_a[pc.c, 4:8, :] = small[8:12, :]
                sum_a.start()

            def place_of(step):
                i = step % 8
                return window(i), raster[i % 4] < counts[i // 4]

            def products(step, g, u):
                rows, valid = place_of(step)
                vq = jnp.concatenate([valid, valid], axis=1)
                da = datt[rows, lanes(g * GW, GW)]
                da = jnp.where(vq, da.astype(F32), 0.0).astype(BF16)
                head_stack(qs.at[u], triple[rows, lanes(g * D, GW)])
                head_stack(dos.at[u], da)
                st[u] = dot(triple[rows, lanes(g * D + 2 * GW, GW)], dos[u], NT)

            def softmax_back(slot, u):
                for n in range(9):
                    c = lanes(n * 128, 128)
                    p = pt[slot, :, c].astype(F32)
                    d = st[u, :, c]
                    inner = jnp.sum(p * d, axis=0, keepdims=True)
                    s = p * (d - inner)
                    bgrad[n] += s
                    raw[u, :, c] = (s * SCALE).astype(BF16)

            def grads(step, g, slot, u):
                rows, _ = place_of(step)
                col = lambda k: lanes(g * D + k * GW, GW)
                key = triple[rows, col(1)]
                triple[rows, col(2)] = dot(pt[slot], dos[u]).astype(BF16)
                triple[rows, col(1)] = dot(raw[u], qs[u]).astype(BF16)
                triple[rows, col(0)] = head_pick(dot(raw[u], key, TN)).astype(BF16)

            def pair(p, g):
                step, slot = 2 * p, 2 * lax.rem(p, 2)

                @pl.when(p < 11)
                def _():
                    fetch(step + 2).start()
                    fetch(step + 3).start()

                products(step, g, 0)
                products(step + 1, g, 1)
                fetch(step).wait()
                fetch(step + 1).wait()
                softmax_back(slot, 0)
                grads(step, g, slot, 0)
                softmax_back(slot + 1, 1)
                grads(step + 1, g, slot + 1, 1)

            def half_group(q, _):
                g = 2 - q // 2

                @pl.when(q % 2 == 0)
                def _():
                    bgrad[...] = jnp.zeros(bgrad.shape, F32)

                lax.fori_loop(0, 2, lambda j, _: (pair(q * 2 + j, g), 0)[1], 0)

                @pl.when(q % 2 == 1)
                def _():
                    gather_bias(g, bgrad, accbuf, t4g)
                    for k, parts in enumerate(group_cols(g)):
                        v = triple[:, lanes(g * D + k * GW, GW)]
                        if k != 1:
                            small[2 + k // 2:3 + k // 2, lanes(g * GW, GW)] = jnp.sum(v.astype(F32), axis=0, keepdims=True)
                        put(parts, dot(xt[...], v).astype(BF16))

                if near:
                    for t in range(18, 24):
                        if events(t):
                            pl.when(q == t - 18)(lambda t=t: ert_tick(t))
                    for m, at in enumerate((0, 2, 4)):
                        pl.when(q == at)(lambda m=m: sum_a.advance(m) and None)

                return 0

            lax.fori_loop(0, 2 * GROUPS, half_group, 0)
            if near:
                own = slots_g.at[pc.c]
                own[...] = jnp.zeros(own.shape, F32)
                own[:, 0:4 * WT] = t4g[...]
                sum_g.start()
        def rest(act):
            again = load(0, o_act, act)
            again.start()

            def normed_grad(n, _):
                rows = pl.ds(aligned(n * 256, 256), 256)
                weights = jnp.concatenate([flat_tw[rows, h * TM_HALF + lo:h * TM_HALF + lo + m]
                                           for g in range(GROUPS) for p in group_cols(g) for h, lo, m in p], axis=1)
                dn2[:, lanes(n * 256, 256)] = dot(triple[...], weights, NT)
                if near:
                    for t in range(2):
                        @pl.when(n == t)
                        def _(t=t):
                            ert_tick(24 + t)
                            if t == 1:
                                sum_g.advance(0)
                return 0

            lax.fori_loop(0, 3, normed_grad, 0)

            def ln1b(i, _):
                rows = window(i)
                hat, inv = stats(xp[rows, :].astype(F32))
                g = dn2[rows, :]
                late[0:1, :] += jnp.sum(g * hat, axis=0, keepdims=True)
                late[1:2, :] += jnp.sum(g, axis=0, keepdims=True)
                ml[rows, :] = (mixed[rows, :] + norm_back(hat, inv, sv[0:1, :], g)).astype(BF16)
                return 0

            late[...] = jnp.zeros(late.shape, F32)
            twos(8, ln1b)
            if near:
                slots_l[pc.c, 0:2, :] = late[0:2, :]
                slots_l[pc.c, 2:4, :] = small[2:4, :]
                sum_l.start()
                ert_tick(26)
                sum_g.advance(1)
                sum_keep[...] = sum_a.advance(3)
            mixed_again = load(3, mixed_h, mixed)
            mixed_again.start()

            def back_to_raster(src, dst):
                def block(k, _):
                    b, m = k // 4, k % 4
                    dst[window(k), :] = dot(to_raster(rasq, m), src[pl.ds(aligned(b * TOK, TOK), TOK), :]).astype(BF16)
                    return 0

                twos(8, block)

            back_to_raster(ml, part)
            saves = [load(4 + b, part.at[b * TOK:(b + 1) * TOK, :], o_dx.at[b]) for b in range(2)]
            for c in saves:
                c.start()
            if near:
                ert_tick(27)
                sum_g.advance(2)
                sum_l.advance(0)
            again.wait()
            mixed_again.wait()

            def output(n, _):
                c = lanes(n * 256, 256)
                ml[:, c] = (mixed[:, c] + dot(act[...], flat_r[:, c]) + sv[7:8, c]).astype(BF16)
                if near:
                    for t in range(2):
                        @pl.when(n == t)
                        def _(t=t):
                            ert_tick(28 + t)
                            sum_l.advance(1 + t)
                return 0

            lax.fori_loop(0, 3, output, 0)
            back_to_raster(ml, dop)
            more = [load(b, dop.at[b * TOK:(b + 1) * TOK, :], o_out.at[b]) for b in range(2)]
            for c in more:
                c.start()
            if near:
                ert_tick(30)
                total_g = sum_g.advance(3)
                total_l = sum_l.advance(3)
                dev = pc.z * (2 * pc.ny * pc.nx) + (pc.y * pc.nx + pc.x) * 2 + pc.c
                n = o_small.shape[1]
                shift = lax.rem(D - dev * n, D)
                rows = jnp.concatenate([total_l, sum_keep[0:4, :]], axis=0)
                o_small[...] = pltpu.roll(rows, shift, axis=1)[:, 0:n]
                wide_n = o_deb.shape[1]
                per = D // wide_n
                row = sum_keep[pl.ds(4 + dev // per, 1), :]
                o_deb[...] = pltpu.roll(row, lax.rem(D - lax.rem(dev, per) * wide_n, D), axis=1)[:, 0:wide_n]
                o_t4[...] = total_g[:, 0:4 * WT]
                rs.done("e", None, o_e, 6, range(1, 5))
                rs.done("r", None, o_r, 3, range(1, 5))
                rs.done("t", dt, o_t, 6, range(5))
                sum_a.done()
                sum_l.done()
                sum_g.done()
            else:
                o_small[0:2, :] = late[0:2]
                o_small[2:8, :] = small[2:8, :]
                for k in range(4):
                    o_deb[0:1, k * D:(k + 1) * D] = small[8 + k:9 + k, :]
                o_t4[...] = t4g[...]
                save = load(3, dt, o_t)
                save.start()
                save.wait()
            for c in saves + more:
                c.wait()

        pl.run_scoped(attention, vm((ROWS, D), BF16), vm((D, ROWS), BF16), vm((ROWS, D), BF16), vm((2, QL, GW), BF16),
                      vm((2, QL, GW), BF16), vm((2, WT, QL), F32), vm((2, WT, QL), BF16), vm((4, WT, QL), BF16),
                      vm((9, WT, 128), F32), vm((2, 16, QL), F32), pltpu.SemaphoreType.DMA((4,)))
        pl.run_scoped(rest, vm((ROWS, FF), BF16))

    pl.run_scoped(after_feed_forward, vm((nz, ny, nx, rw_rows, 2 * TM_HALF), BF16), vm((ROWS, 3 * D), BF16),
                  vm((ROWS, D), BF16), vm((ROWS, D), BF16), vm((HEADS, 4 * WT), F32), vm((8, D), F32))


def backward(near, dims, counts, do, w, r, own_ew, own_er, triple, pt, att, mixed, n2, normed, xp, sv, eb):
    nz, ny, nx = dims if near else (1, 1, 1)
    if not near:
        w, r = w.reshape(1, 1, 1, D, -1), r.reshape(1, 1, 1, FF, D)
    rw, rr = w.shape[3], r.shape[3]
    peers = max(nz, ny, nx, 2) - 1
    vm = pltpu.VMEM
    dma = pltpu.SemaphoreType.DMA
    bufs = []
    for count, n in ((6, rw), (6, rw), (3, rr // 2)) if near else ((1, 16),) * 3:
        bufs += [vm((count, 2, nz, ny, nx, n, 128), BF16), vm((count, 2, max(ny - 1, 1), nz, nx, n, 128), BF16),
                 vm((count, 2, max(nx - 1, 1), nz, n, 128), BF16), vm((count, 2, max(nz - 1, 1), n, 128), BF16),
                 vm((count, 2, n, 128), F32)]
    n_slots = 2 + nz + ny + nx
    if near:
        outs = [((rw // 2, 2 * TM_HALF), F32), ((rw // 2, FF), F32), ((rr // 2, D), F32), ((8, rw // 2), F32), ((1, rr // 2), F32)]
    else:
        outs = [((1, 1, 1, D, 2 * TM_HALF), BF16), ((1, 1, 1, D, FF), BF16), ((1, 1, 1, FF, D), BF16), ((8, D), F32), ((1, FF), F32)]
    outs = [((2, TOK, D), BF16), ((2, TOK, D), BF16), ((ROWS, FF), BF16)] + outs + [((HEADS, 4 * WT), F32)]
    params = dict(collective_id=1, has_side_effects=True) if near else {}
    return pl.pallas_call(
        functools.partial(backward_kernel, near, dims),
        out_shape=[jax.ShapeDtypeStruct(s, d) for s, d in outs],
        in_specs=[SM, VM, VM, ANY, ANY, VM, VM] + [ANY] * 7 + [VM] * 2,
        out_specs=[ANY] * 3 + ([VM] * 3 if near else [ANY] * 3) + [VM] * 3,
        scratch_shapes=[vm((4, WT, 128), jnp.int32), vm((nz, ny, nx, rw, FF), BF16), vm((nz, ny, nx, rr, D), BF16), vm((ROWS, D), BF16), vm((ROWS, D), F32),
                        vm((ROWS, D), F32), vm((ROWS, D), BF16)] + bufs
        + [vm((n_slots, 8, D), F32), vm((n_slots, HEADS, 640), F32), vm((8, D), F32), vm((n_slots, 4, D), F32),
           vm((16, D), F32),
           dma((6, 6, peers)), dma((6, 6, peers)), dma((15, 2, 5, peers)), dma((15, 2, 5, peers)), dma((3, 4, peers)),
           dma((3, 4, peers)), dma((7,))],
        name="backward",
        compiler_params=pltpu.CompilerParams(vmem_limit_bytes=VMEM_LIMIT, **params),
    )(counts, jnp.asarray(RASTER_Q), do, w, r, own_ew, own_er, triple, pt, att, mixed, n2, normed, xp, sv,
      eb)


def finish_kernel(target, out_h, dx_h, t, e, r, small, deb, t4, out, dx, triple, merge, expand, reduce, table, *rest):
    vectors, sem = rest[:-1], rest[-1]
    copies = [pltpu.make_async_copy(out_h, out, sem.at[0]), pltpu.make_async_copy(dx_h, dx, sem.at[1])]
    for c in copies:
        c.start()
    for g in range(GROUPS):
        for k, parts in enumerate(group_cols(g)):
            at = k * D + g * GW
            for h, lo, n in parts:
                triple[:, at:at + n] = t[:, h * TM_HALF + lo:h * TM_HALF + lo + n]
                at += n
    for c in range(2):
        merge[:, c * D // 2:(c + 1) * D // 2] = t[:, c * TM_HALF + 1152:(c + 1) * TM_HALF]
        for s in range(2):
            expand[:, s * FF_HALF + c * FF_PART:s * FF_HALF + (c + 1) * FF_PART] = (
                e[:, c * FF_HALF + s * FF_PART:c * FF_HALF + (s + 1) * FF_PART])
    reduce[...] = r[...]
    for k, v in enumerate(vectors[:8]):
        v[...] = small[k, :]
    vectors[8][...] = deb[0, :]
    table[...] = lax.dot_general(t4[...], onehot(target), NT, precision=lax.Precision.HIGHEST,
                                 preferred_element_type=F32)
    for c in copies:
        c.wait()


def weights_in_pieces(triple_weight, merge_weight, expand_weight):
    halves = []
    for c in range(2):
        for g in range(GROUPS):
            q, k, v = (triple_weight[:, i * D + g * GW:i * D + (g + 1) * GW] for i in range(3))
            halves += [q, k[:, :128]] if c == 0 else [k[:, 128:], v]
        halves.append(merge_weight[:, c * D // 2:(c + 1) * D // 2])
        halves += [expand_weight[:, s * FF_HALF + c * FF_PART:s * FF_HALF + (c + 1) * FF_PART] for s in range(2)]
    return jnp.concatenate(halves, axis=1)


def shards(dims, block_input, valid_counts, output_cotangent, triple_weight, merge_weight, expand_weight, reduce_weight,
           first_gain, first_shift, query_bias, value_bias, merge_bias, second_gain, second_shift, expand_bias,
           reduce_bias, position_table):
    counts = valid_counts[:, 0]
    rows = triple_weight.shape[0]
    near = rows % 8 == 0 and dims[0] % 4 == 0 and dims[1] == dims[2]
    if near:
        given = (triple_weight, merge_weight, expand_weight, reduce_weight, first_gain, first_shift, query_bias, value_bias,
                 merge_bias, second_gain, second_shift, reduce_bias, expand_bias)
    else:
        small = jnp.stack([first_gain, first_shift, query_bias, value_bias, merge_bias, second_gain, second_shift,
                           reduce_bias])
        gather = lambda v, axis: lax.all_gather(v.astype(BF16), AXES, axis=axis, tiled=True)
        given = (gather(weights_in_pieces(triple_weight, merge_weight, expand_weight), 0), gather(reduce_weight, 0),
                 gather(small, 1).astype(F32), jnp.broadcast_to(gather(expand_bias, 0).astype(F32)[None], (8, FF)))
    o_w, o_r, triple, pt, att, mixed, n2, normed, xp, sv, eb, own_ew, own_er = forward(
        near, dims, counts, block_input[:, 0], position_table, *given)
    if not near:
        o_w, o_r = given[:2]
    out, dx, _, gt, ge, gr, gs, gb, t4 = backward(near, dims, counts, output_cotangent[:, 0], o_w, o_r, own_ew, own_er, triple, pt,
                                               att, mixed, n2, normed, xp, sv, eb)
    if not near:
        scatter = lambda v, axis: lax.psum_scatter(v.astype(F32), AXES, scatter_dimension=axis, tiled=True)
        gt, ge, gr = scatter(gt.reshape(D, -1), 0), scatter(ge.reshape(D, -1), 0), scatter(gr.reshape(FF, D), 0)
        gs, gb, t4 = scatter(gs, 1), scatter(gb, 1), lax.psum(t4, AXES)
    n, rr = expand_bias.shape[0], reduce_weight.shape[0]
    image = jax.ShapeDtypeStruct((2, TOK, D), BF16)
    shapes = [(rows, 3 * D), (rows, D), (rows, FF), (rr, D), (HEADS, EXT * EXT)] + [(rows,)] * 8 + [(n,)]
    out, dx, tr, mg, ex, re, table, *vec = pl.pallas_call(
        finish_kernel, out_shape=[image, image] + [jax.ShapeDtypeStruct(s, F32) for s in shapes],
        in_specs=[VM, ANY, ANY] + [VM] * 6, out_specs=[VM] * (2 + len(shapes)),
        scratch_shapes=[pltpu.SemaphoreType.DMA((2,))], name="finish",
        compiler_params=pltpu.CompilerParams(vmem_limit_bytes=VMEM_LIMIT),
    )(jnp.asarray(TARGET), out, dx, gt, ge, gr, gs, gb, t4)
    return (out[:, None], dx[:, None], tr, mg, ex, re, *vec[:7], vec[8], vec[7], table.T)


def solution(mesh):
    image = P(None, AXES, None, None)
    rows = P(AXES, None)
    vec = P(AXES)
    return jax.shard_map(
        functools.partial(shards, mesh_dims(mesh)), mesh=mesh,
        in_specs=(image, P(None, AXES), image) + (rows,) * 4 + (vec,) * 9 + (P(),),
        out_specs=(image, image) + (rows,) * 4 + (vec,) * 9 + (P(),),
        check_vma=False)
```
